32 devices in a mesh: cells: 8 (over z, y), depth: 4 (over x, core).
Axes of the slice: x: 2, y: 2, z: 4, core: 2. Of those that a mesh axis runs over, the one named last changes fastest.
Arguments:
- x_in: float32 [2, 4096, 256], P(None, ('cells', 'depth')), may hold values from -6 to 6
- vec_in: float32 [2, 3, 4096, 256], P(None, None, ('cells', 'depth')), may hold values from -6 to 6
- cot_x: float32 [2, 4096, 256], P(None, ('cells', 'depth')), may hold values from -6 to 6
- cot_vec: float32 [2, 3, 4096, 256], P(None, None, ('cells', 'depth')), may hold values from -6 to 6
- mats: float32 [753664], P('cells')
- vecs: float32 [3584], P('cells')
- mats_first: float32 [753664], P('cells')
- mats_second: float32 [753664], P('cells')
- vecs_first: float32 [3584], P('cells')
- vecs_second: float32 [3584], P('cells')
- atom_count: int32 [2, 32], P(None, ('cells', 'depth')), may hold values from 64 to 128, as said below
- neighbours: int32 [2, 64, 4096], P(None, None, ('cells', 'depth')), may hold values from 0 to 1663, as said below
- edge_mask: int32 [2, 64, 4096], P(None, None, ('cells', 'depth')), may hold values from 0 to 1, as said below
- edge_vec: float32 [2, 3, 64, 4096], P(None, None, None, ('cells', 'depth')), may hold values from -2.8 to 2.8, as said below
- send_list: int32 [2, 192, 256], P(None, ('cells', 'depth')), may hold values from 0 to 127, as said below
Outputs:
- out_x: float32 [2, 4096, 256], P(None, ('cells', 'depth'))
- out_vec: float32 [2, 3, 4096, 256], P(None, None, ('cells', 'depth'))
- grad_x: float32 [2, 4096, 256], P(None, ('cells', 'depth'))
- grad_vec: float32 [2, 3, 4096, 256], P(None, None, ('cells', 'depth'))
- grad_mats: float32 [753664], P('cells')
- grad_vecs: float32 [3584], P('cells')
- new_mats: float32 [753664], P('cells')
- new_vecs: float32 [3584], P('cells')
- new_mats_first: float32 [753664], P('cells')
- new_mats_second: float32 [753664], P('cells')
- new_vecs_first: float32 [3584], P('cells')
- new_vecs_second: float32 [3584], P('cells')
The draws below stay inside these ranges and needn't reach their ends.
Inputs may be any that keep to these rules, and one draw needn't show every extreme that they name: `atom_count`: in every micro-batch some domain holds exactly 128 real atoms. `edge_mask`: live edges of an atom are its first slots: 4 to 64 for each real atom, none for padding atoms; some atom has 64 in every micro-batch. `neighbours`: A slot below the domain's atom count is an own atom; slot 128 + f * 256 + h is the h-th atom received across face f; never a padding atom. `send_list`: every entry is below its domain's atom count; entries may repeat. `edge_vec`: each component's magnitude is 0.3 or more.
All inputs are finite; a program needn't handle non-finite values.
Results may differ from the reference program's by a relative error of at most 0.012.
The reference program's roundings to bfloat16 on the way count: a program that leaves them out, or rounds other values in their place, can miss the bound.
Values may be sent and summed in bfloat16 or wider, within the bound.
A program may use at most 512 MiB of HBM per device.

```python
import math
from functools import partial
import jax
import jax.numpy as jnp
from jax import lax

F = 256
HEADS = 8
NR = 32
K = 64
A_DEV = 128
HALO = 256
MB = 2
FOLD = 4
STEP = 3
DOMAINS = 32
ATOMS = 4096
SLOTS = 1664
PM = 753664
PV = 3584
N_CELLS = 8
N_DEPTH = 4


mats_grad = [0.5, 0.5, 0.5, 2.0, 1.5, 2.0, 2.0]


vecs_grad = [1.0, 1.0, 0.5, 0.5, 0.5, 1.5, 2.0, 2.0]


def count_table(key):
    dropped = jax.random.randint(jax.random.fold_in(key, 11), (MB, DOMAINS), 0, A_DEV // 2 + 1)
    chosen = jax.random.randint(jax.random.fold_in(key, 12), (MB,), 0, DOMAINS)
    is_full = jnp.arange(DOMAINS)[None, :] == chosen[:, None]
    return jnp.where(is_full, A_DEV, A_DEV - dropped).astype(jnp.int32)


def draw_atom_count(key, part):
    return count_table(key)


def edge_lengths(key):
    counts = count_table(key)
    per_atom = jax.random.randint(jax.random.fold_in(key, 21), (MB, DOMAINS, A_DEV), 4, K + 1)
    chosen = jax.random.randint(jax.random.fold_in(key, 22), (MB,), 0, DOMAINS)
    is_top = (jnp.arange(DOMAINS)[None, :, None] == chosen[:, None, None]) & (jnp.arange(A_DEV)[None, None, :] == 0)
    per_atom = jnp.where(is_top, K, per_atom)
    is_real = jnp.arange(A_DEV)[None, None, :] < counts[:, :, None]
    return jnp.where(is_real, per_atom, 0)


def draw_edge_mask(key, part):
    lengths = edge_lengths(key)
    slot_ids = jnp.arange(K)[None, :, None, None]
    return (slot_ids < lengths[:, None]).astype(jnp.int32).reshape(MB, K, ATOMS)


def draw_neighbours(key, part):
    counts = count_table(key)[:, None, :, None]
    raw_slots = jax.random.randint(jax.random.fold_in(key, 31), (MB, K, DOMAINS, A_DEV), 0, counts + 6 * HALO)
    slot_ids = jnp.where(raw_slots < counts, raw_slots, raw_slots - counts + A_DEV)
    is_last = (jnp.arange(K)[None, :, None, None] == 0) & (jnp.arange(DOMAINS)[None, None, :, None] == 0) & (jnp.arange(A_DEV)[None, None, None, :] == 0)
    slot_ids = jnp.where(is_last, A_DEV + 6 * HALO - 1, slot_ids)
    return slot_ids.astype(jnp.int32).reshape(MB, K, ATOMS)


def draw_send_list(key, part):
    counts = count_table(key)[:, :, None, None]
    send_rows = jax.random.randint(jax.random.fold_in(key, 41), (MB, DOMAINS, 6, HALO), 0, counts)
    is_first = (jnp.arange(6)[None, None, :, None] == 0) & (jnp.arange(HALO)[None, None, None, :] == 0)
    send_rows = jnp.where((counts == A_DEV) & is_first, A_DEV - 1, send_rows)
    return send_rows.astype(jnp.int32).reshape(MB, DOMAINS * 6, HALO)


def draw_edge_vec(key, part):
    shape_all = (MB, 3, K, ATOMS)
    magnitude = jax.random.uniform(jax.random.fold_in(key, 51), shape_all, jnp.float32, 0.5, 2.5)
    signs = (jax.random.randint(jax.random.fold_in(key, 52), shape_all, 0, 2) * 2 - 1).astype(jnp.float32)
    return magnitude * signs


def segment_scale(sizes_list, factors):
    return jnp.concatenate([jnp.full((size_one,), factor, jnp.float32) for size_one, factor in zip(sizes_list, factors)])


def mats_sizes():
    return [F * F, F * F, 3 * F * F, 3 * F * F, 3 * F * F, NR * F, 3 * NR * F]


def vecs_sizes():
    return [F, F, F, F, 3 * F, 3 * F, F, 3 * F]


def grad_root():
    return math.sqrt(MB * ATOMS * 0.75)


def draw_mats(key, part):
    scales = segment_scale(mats_sizes(), [F ** (-0.5)] * 4 + [(4 * F) ** (-0.5)] + [(NR / 8.0) ** (-0.5)] * 2)
    noise = jnp.clip(jax.random.normal(jax.random.fold_in(key, 61), (PM,), jnp.float32), -4.0, 4.0)
    return noise * scales


def draw_vecs(key, part):
    scales = segment_scale(vecs_sizes(), [0.1, 0.1, 0.1, 0.1, 0.1, 0.1, 0.3, 0.3])
    offsets = segment_scale(vecs_sizes(), [1.0, 0.0, 0.0, 0.0, 0.0, 0.0, 0.0, 0.0])
    noise = jnp.clip(jax.random.normal(jax.random.fold_in(key, 62), (PV,), jnp.float32), -4.0, 4.0)
    return offsets + noise * scales


def draw_mats_first(key, part):
    estimate = segment_scale(mats_sizes(), mats_grad) * grad_root()
    noise = jnp.clip(jax.random.normal(jax.random.fold_in(key, 63), (PM,), jnp.float32), -3.0, 3.0)
    return estimate * noise


def draw_mats_second(key, part):
    estimate = segment_scale(mats_sizes(), mats_grad) * grad_root()
    factor_draw = jax.random.uniform(jax.random.fold_in(key, 64), (PM,), jnp.float32, 1.0, 4.0)
    return estimate * estimate * factor_draw


def draw_vecs_first(key, part):
    estimate = segment_scale(vecs_sizes(), vecs_grad) * grad_root()
    noise = jnp.clip(jax.random.normal(jax.random.fold_in(key, 65), (PV,), jnp.float32), -3.0, 3.0)
    return estimate * noise


def draw_vecs_second(key, part):
    estimate = segment_scale(vecs_sizes(), vecs_grad) * grad_root()
    factor_draw = jax.random.uniform(jax.random.fold_in(key, 66), (PV,), jnp.float32, 1.0, 4.0)
    return estimate * estimate * factor_draw


def shard_levels(stream_key, extent, split, smallest, top_value):
    def one(axis_at, parts):
        steps = jax.random.uniform(jax.random.fold_in(jax.random.fold_in(stream_key, 6), axis_at), (parts,), jnp.float32, smallest / len(split), top_value / len(split))
        return jnp.repeat(jnp.exp(steps), extent[axis_at] // parts).reshape((-1,) + (1,) * (len(extent) - axis_at - 1))

    loudness = one(*split[0])
    for cut in split[1:]:
        loudness = loudness * one(*cut)
    return loudness


def centred(own_key, extent, deviation, reach, split=(), held_as=jnp.bfloat16):
    result = jax.random.normal(own_key, extent, jnp.float32) * deviation
    if len(split) > 0:
        result = shard_levels(own_key, extent, split, -0.22, 0.18) * result
    return jnp.clip(result, min=-reach, max=reach).astype(held_as)


def setup_inputs(seed: int = 0) -> dict:
    arg_keys = jax.random.split(jax.random.key(seed), 16)
    x_in = centred(arg_keys[0], (MB, ATOMS, F), 1.0, 6.0, ((1, 32),), jnp.float32)
    vec_in = centred(arg_keys[1], (MB, 3, ATOMS, F), 1.0, 6.0, ((2, 32),), jnp.float32)
    cot_x = centred(arg_keys[2], (MB, ATOMS, F), 1.0, 6.0, ((1, 32),), jnp.float32)
    cot_vec = centred(arg_keys[3], (MB, 3, ATOMS, F), 1.0, 6.0, ((2, 32),), jnp.float32)
    mats = draw_mats(jax.random.fold_in(arg_keys[15], 71), 0)
    vecs = draw_vecs(jax.random.fold_in(arg_keys[15], 71), 0)
    mats_first = draw_mats_first(jax.random.fold_in(arg_keys[15], 71), 0)
    mats_second = draw_mats_second(jax.random.fold_in(arg_keys[15], 71), 0)
    vecs_first = draw_vecs_first(jax.random.fold_in(arg_keys[15], 71), 0)
    vecs_second = draw_vecs_second(jax.random.fold_in(arg_keys[15], 71), 0)
    atom_count = draw_atom_count(jax.random.fold_in(arg_keys[15], 71), 0)
    neighbours = draw_neighbours(jax.random.fold_in(arg_keys[15], 71), 0)
    edge_mask = draw_edge_mask(jax.random.fold_in(arg_keys[15], 71), 0)
    edge_vec = draw_edge_vec(jax.random.fold_in(arg_keys[15], 71), 0)
    send_list = draw_send_list(jax.random.fold_in(arg_keys[15], 71), 0)
    return dict(x_in=x_in, vec_in=vec_in, cot_x=cot_x, cot_vec=cot_vec, mats=mats, vecs=vecs, mats_first=mats_first, mats_second=mats_second, vecs_first=vecs_first, vecs_second=vecs_second, atom_count=atom_count, neighbours=neighbours, edge_mask=edge_mask, edge_vec=edge_vec, send_list=send_list)


@jax.custom_vjp
def low(v):
    return lax.optimization_barrier(v.astype(jnp.bfloat16)).astype(jnp.float32)

@jax.custom_vjp
def low_back(v):
    return v

def low_keep(v):
    return (low(v), None)

def low_pass(kept, grad):
    return (grad,)

def back_keep(v):
    return (v, None)

def back_low(kept, grad):
    return (low(grad),)
low.defvjp(low_keep, low_pass)
low_back.defvjp(back_keep, back_low)
norm_eps = 1e-05
cut_radius = 5.0
beta_one = 0.5
beta_two = 0.5
learn_rate = 0.05
decay_rate = 0.01
adam_eps = 1e-08

def unpack_mats(flat_array, feat_width, basis_count):
    shapes = ((feat_width, feat_width), (feat_width, feat_width), (feat_width, 3 * feat_width), (feat_width, 3 * feat_width), (feat_width, 3 * feat_width), (basis_count, feat_width), (basis_count, 3 * feat_width))
    pieces = []
    offset = 0
    for shape_one in shapes:
        length = shape_one[0] * shape_one[1]
        pieces.append(flat_array[offset:offset + length].reshape(shape_one))
        offset = offset + length
    return pieces

def unpack_vecs(flat_array, feat_width):
    lengths = (feat_width, feat_width, feat_width, feat_width, 3 * feat_width, 3 * feat_width, feat_width, 3 * feat_width)
    pieces = []
    offset = 0
    for length in lengths:
        pieces.append(flat_array[offset:offset + length])
        offset = offset + length
    return pieces

def layer_norm(x_rows, gain, shift):
    mean_val = lax.optimization_barrier(jnp.mean(x_rows, axis=-1, keepdims=True))
    centered = x_rows - mean_val
    variance = lax.optimization_barrier(jnp.mean(centered * centered, axis=-1, keepdims=True))
    return centered * lax.rsqrt(variance + norm_eps) * gain + shift

def radial_terms(edge_geom, edge_live):
    radius = jnp.sqrt(lax.optimization_barrier(jnp.sum(edge_geom * edge_geom, axis=0)))
    unit_dir = edge_geom / radius
    live_float = edge_live.astype(jnp.float32)
    cosine_cut = 0.5 * (jnp.cos(math.pi * radius / cut_radius) + 1.0) * live_float
    start_value = math.exp(-cut_radius)
    centers = jnp.linspace(start_value, 1.0, NR).astype(jnp.float32)
    width_coef = (2.0 / NR * (1.0 - start_value)) ** (-2)
    decayed = jnp.exp(-(5.0 / cut_radius) * radius)
    basis = cosine_cut[..., None] * jnp.exp(-width_coef * (decayed[..., None] - centers) ** 2)
    return (unit_dir, cosine_cut, basis)

def message_sum(query_rows, key_edge, value_edge, vec_edge, filt_key, filt_value, cosine_cut, unit_dir, live_float):
    feat_width = query_rows.shape[-1]
    edge_shape = key_edge.shape[:2]
    head_shape = edge_shape + (HEADS, feat_width // HEADS)
    product_qk = query_rows[None] * key_edge * jax.nn.silu(filt_key)
    scores = lax.optimization_barrier(jnp.sum(product_qk.reshape(head_shape), axis=-1))
    attention = jax.nn.silu(scores) * cosine_cut[..., None]
    gated = value_edge * jax.nn.silu(filt_value)
    x_part = gated[..., :feat_width]
    vec_gate = gated[..., feat_width:2 * feat_width]
    dir_gate = gated[..., 2 * feat_width:]
    x_msg = (x_part.reshape(head_shape) * attention[..., None]).reshape(edge_shape + (feat_width,))
    x_agg = lax.optimization_barrier(jnp.sum(x_msg, axis=0))
    vec_msg = (vec_edge * vec_gate[None] + dir_gate[None] * unit_dir[..., None]) * live_float[None, :, :, None]
    vec_agg = lax.optimization_barrier(jnp.sum(vec_msg, axis=1))
    return (x_agg, vec_agg)

def branch_out(out_all, vec_proj, vec_agg, atom_live):
    feat_width = vec_agg.shape[-1]
    out_one = out_all[:, :feat_width]
    out_two = out_all[:, feat_width:2 * feat_width]
    out_three = out_all[:, 2 * feat_width:]
    proj_one = vec_proj[..., :feat_width]
    proj_two = vec_proj[..., feat_width:2 * feat_width]
    proj_three = vec_proj[..., 2 * feat_width:]
    vec_dot = lax.optimization_barrier(jnp.sum(proj_one * proj_two, axis=0))
    delta_x = (vec_dot * out_two + out_three) * atom_live[:, None]
    delta_vec = (proj_three * out_one[None] + vec_agg) * atom_live[None, :, None]
    return (delta_x, delta_vec)

def domain_layer(own_norm, table_x, own_vec, table_vec, nbr_rows, edge_live, edge_geom, atom_live, weights):
    w_query, w_key, w_value, w_vector, w_out, w_fkey, w_fvalue, b_query, b_key, b_value, b_out, b_fkey, b_fvalue = weights
    highest = lax.Precision.HIGHEST
    query = low_back(low(jnp.dot(own_norm, w_query, precision=highest) + b_query))
    keys = low_back(low(jnp.dot(table_x, w_key, precision=highest) + b_key))
    values = low_back(low(jnp.dot(table_x, w_value, precision=highest) + b_value))
    vec_proj = low_back(jnp.einsum('cai,io->cao', own_vec, w_vector, precision=highest))
    unit_dir, cosine_cut, basis = radial_terms(edge_geom, edge_live)
    basis_low = low(basis)
    filt_key = low_back(jnp.einsum('kar,rf->kaf', basis_low, w_fkey, precision=highest) + b_fkey)
    filt_value = low_back(jnp.einsum('kar,rf->kaf', basis_low, w_fvalue, precision=highest) + b_fvalue)
    key_edge = keys[nbr_rows]
    value_edge = values[nbr_rows]
    vec_edge = table_vec[:, nbr_rows]
    x_agg, vec_agg = message_sum(query, key_edge, value_edge, vec_edge, filt_key, filt_value, cosine_cut, unit_dir, edge_live.astype(jnp.float32))
    out_all = low_back(jnp.dot(low(x_agg), w_out, precision=highest) + b_out)
    return branch_out(out_all, vec_proj, vec_agg, atom_live)

def micro_forward(x_rows, vec_rows, mats, vecs, counts, nbr_all, edge_live, edge_geom, send_all):
    mats_low = low(mats)
    vecs_low = low(vecs)
    feat_width = x_rows.shape[-1]
    w_query, w_key, w_value, w_vector, w_out, w_fkey, w_fvalue = unpack_mats(mats_low, feat_width, NR)
    ln_gain, ln_shift, b_query, b_key, b_value, b_out, b_fkey, b_fvalue = unpack_vecs(vecs_low, feat_width)
    normed = low(layer_norm(x_rows, ln_gain, ln_shift))
    vec_low = low(vec_rows)
    grid_x = normed.reshape(N_CELLS, N_DEPTH, A_DEV, feat_width)
    grid_vec = vec_low.reshape(3, N_CELLS, N_DEPTH, A_DEV, feat_width)
    grid_send = send_all.reshape(N_CELLS, N_DEPTH, 6, HALO)
    halo_x = []
    halo_vec = []
    moves = ((0, 1), (0, -1), (0, FOLD), (0, -FOLD), (1, 1), (1, -1))
    for face_idx, (axis_id, offset) in enumerate(moves):
        source_x = jnp.roll(grid_x, offset, axis=axis_id)
        source_vec = jnp.roll(grid_vec, offset, axis=axis_id + 1)
        source_rows = jnp.roll(grid_send, offset, axis=axis_id)[:, :, face_idx]
        halo_x.append(low_back(jnp.take_along_axis(source_x, source_rows[..., None], axis=2)))
        halo_vec.append(low_back(jnp.take_along_axis(source_vec, source_rows[None, ..., None], axis=3)))
    table_x = jnp.concatenate([grid_x] + halo_x, axis=2).reshape(DOMAINS, SLOTS, feat_width)
    table_vec = jnp.moveaxis(jnp.concatenate([grid_vec] + halo_vec, axis=3).reshape(3, DOMAINS, SLOTS, feat_width), 1, 0)
    own_norm = normed.reshape(DOMAINS, A_DEV, feat_width)
    own_vec = jnp.moveaxis(vec_low.reshape(3, DOMAINS, A_DEV, feat_width), 1, 0)
    atom_live = (jnp.arange(A_DEV)[None, :] < counts[:, None]).astype(jnp.float32)
    nbr_dom = jnp.moveaxis(nbr_all.reshape(K, DOMAINS, A_DEV), 1, 0)
    live_dom = jnp.moveaxis(edge_live.reshape(K, DOMAINS, A_DEV), 1, 0)
    geom_dom = jnp.moveaxis(edge_geom.reshape(3, K, DOMAINS, A_DEV), 2, 0)
    weights = (w_query, w_key, w_value, w_vector, w_out, w_fkey, w_fvalue, b_query, b_key, b_value, b_out, b_fkey, b_fvalue)

    def one_domain(items):
        return domain_layer(*items, weights)
    delta_x, delta_vec = lax.map(jax.checkpoint(one_domain), (own_norm, table_x, own_vec, table_vec, nbr_dom, live_dom, geom_dom, atom_live))
    out_x = x_rows + delta_x.reshape(ATOMS, feat_width)
    out_vec = vec_rows + jnp.moveaxis(delta_vec, 0, 1).reshape(3, ATOMS, feat_width)
    return (out_x, out_vec)

def adam_update(weight, grad, first, second):
    first_new = beta_one * first + (1.0 - beta_one) * grad
    second_new = beta_two * second + (1.0 - beta_two) * grad * grad
    first_hat = first_new / (1.0 - beta_one ** STEP)
    second_hat = second_new / (1.0 - beta_two ** STEP)
    weight_new = weight - learn_rate * (first_hat / (jnp.sqrt(second_hat) + adam_eps) + decay_rate * weight)
    return (weight_new, first_new, second_new)

def reference(x_in, vec_in, cot_x, cot_vec, mats, vecs, mats_first, mats_second, vecs_first, vecs_second, atom_count, neighbours, edge_mask, edge_vec, send_list):
    grad_mats = jnp.zeros(mats.shape, jnp.float32)
    grad_vecs = jnp.zeros(vecs.shape, jnp.float32)
    outs_x = []
    outs_vec = []
    grads_x = []
    grads_vec = []
    for micro_idx in range(MB):
        step_fn = partial(micro_forward, counts=atom_count[micro_idx], nbr_all=neighbours[micro_idx], edge_live=edge_mask[micro_idx], edge_geom=edge_vec[micro_idx], send_all=send_list[micro_idx])
        (out_x, out_vec), pull_back = jax.vjp(step_fn, x_in[micro_idx], vec_in[micro_idx], mats, vecs)
        g_x, g_vec, g_mats, g_vecs = pull_back((cot_x[micro_idx], cot_vec[micro_idx]))
        outs_x.append(out_x)
        outs_vec.append(out_vec)
        grads_x.append(g_x)
        grads_vec.append(g_vec)
        grad_mats = grad_mats + g_mats
        grad_vecs = grad_vecs + g_vecs
    new_mats, mats_one, mats_two = adam_update(mats, grad_mats, mats_first, mats_second)
    new_vecs, vecs_one, vecs_two = adam_update(vecs, grad_vecs, vecs_first, vecs_second)
    return (jnp.stack(outs_x), jnp.stack(outs_vec), jnp.stack(grads_x), jnp.stack(grads_vec), grad_mats, grad_vecs, new_mats, new_vecs, mats_one, mats_two, vecs_one, vecs_two)
```

```python
from functools import partial
import math

import jax
import jax.numpy as jnp
from jax import lax
from jax.experimental import pallas as pl
from jax.experimental.pallas import tpu as pltpu
from jax.sharding import PartitionSpec as P

HEADS = 8
NR = 32
FOLD = 4
STEP = 3

LANES = 128
ROWS = 256
UNIT = 256
BLOCK_SLOTS = 4
TILE = 128

norm_eps = 1e-05
cut_radius = 5.0
beta_one = 0.5
beta_two = 0.5
learn_rate = 0.05
decay_rate = 0.01
adam_eps = 1e-08

f32 = jnp.float32
bf16 = jnp.bfloat16
i32 = jnp.int32

VMEM_LIMIT = 60 * 1024 * 1024


def dot_nn(left, right):
    return lax.dot_general(left, right, (((1,), (0,)), ((), ())), preferred_element_type=f32)


def dot_nt(left, right):
    return lax.dot_general(left, right, (((1,), (1,)), ((), ())), preferred_element_type=f32)


def dot_tn(left, right):
    return lax.dot_general(left, right, (((0,), (0,)), ((), ())), preferred_element_type=f32)


def lane_mean(block):
    return jnp.sum(block, axis=-1, keepdims=True) * (1.0 / block.shape[-1])


def normalise(block):
    centered = block - lane_mean(block)
    spread = lax.rsqrt(lane_mean(centered * centered) + norm_eps)
    return centered * spread, spread


def norm_kernel(x_ref, vec_ref, *own_refs):
    for micro, own_ref in enumerate(own_refs):
        own_ref[0] = normalise(x_ref[micro])[0].astype(bf16)
        own_ref[1:] = vec_ref[micro].astype(bf16)


def prep_kernel(
    block_of,
    buckets,
    nbr_ref,
    mask_ref,
    geom_ref,
    list_ref,
    table_ref,
    units_ref,
    feat,
    place,
    count_vec,
    count_sc,
    packed,
    sem,
):
    micro = pl.program_id(0)
    slots, atoms = nbr_ref.shape[1], nbr_ref.shape[2]
    blocks = slots // BLOCK_SLOTS
    wide = BLOCK_SLOTS * atoms

    @pl.when(micro == 0)
    def _():
        feat[...] = jnp.zeros_like(feat)

    source = nbr_ref[0]
    live = mask_ref[0] > 0
    halo_at = source - atoms
    list_row = halo_at >> 7
    list_lane = halo_at & (LANES - 1)
    atom_in = source
    block_id = jnp.zeros_like(source)
    for row in range(list_ref.shape[1]):
        table = jnp.broadcast_to(list_ref[0, row : row + 1, :], (slots, atoms))
        picked = jnp.take_along_axis(table, list_lane, axis=1)
        here = list_row == row
        atom_in = jnp.where(here, picked, atom_in)
        block_id = jnp.where(here, block_of[row], block_id)
    entry = block_id * atoms + atom_in
    bucket = entry >> 8
    low = ((entry & (ROWS - 1)) + 1).astype(f32)
    atom_id = (lax.broadcasted_iota(i32, (slots, atoms), 1) + 1).astype(f32)
    live_float = live.astype(f32)

    comps = [geom_ref[0, axis] for axis in range(3)]
    radius = jnp.sqrt(comps[0] * comps[0] + comps[1] * comps[1] + comps[2] * comps[2])
    units = [comp / radius for comp in comps]
    cut = 0.5 * (jnp.cos(math.pi * radius / cut_radius) + 1.0) * live_float
    cut_high = cut.astype(bf16).astype(f32)
    cut_low = cut - cut_high
    decayed = jnp.exp(-(5.0 / cut_radius) * radius)
    start_value = math.exp(-cut_radius)
    ramp = lax.broadcasted_iota(i32, (NR, 1), 0).astype(f32) / float(NR - 1)
    centers = start_value * (1.0 - ramp) + ramp
    width_coef = (2.0 / NR * (1.0 - start_value)) ** (-2)
    extras = [live_float, low, atom_id, cut_high, cut_low] + units
    zeros = jnp.zeros((16 - len(extras), atoms), f32)
    for slot in range(slots):
        gap = decayed[slot : slot + 1, :] - centers
        basis = cut[slot : slot + 1, :] * jnp.exp(-width_coef * gap * gap)
        feat[slot, 0:NR, :] = basis.astype(bf16)
        rows = [extra[slot : slot + 1, :] for extra in extras] + [zeros]
        feat[slot, NR : NR + 16, :] = jnp.concatenate(rows, axis=0).astype(bf16)

    members = [jnp.where(live & (bucket == b), 1.0, 0.0) for b in range(buckets)]
    lane_from = lax.broadcasted_iota(i32, (atoms, 2 * atoms), 0)
    lane_to = lax.broadcasted_iota(i32, (atoms, 2 * atoms), 1)
    before = jnp.where((lane_from < lane_to) | (lane_to >= atoms), 1.0, 0.0).astype(bf16)
    slot_to = lax.broadcasted_iota(i32, (slots, slots), 0)
    slot_from = lax.broadcasted_iota(i32, (slots, slots), 1)
    same = (slot_to // BLOCK_SLOTS) == (slot_from // BLOCK_SLOTS)
    earlier = jnp.where(same & (slot_from < slot_to), 1.0, 0.0).astype(bf16)
    block_row = lax.broadcasted_iota(i32, (blocks, slots), 0)
    block_slot = lax.broadcasted_iota(i32, (blocks, slots), 1)
    gather_block = jnp.where(block_slot // BLOCK_SLOTS == block_row, 1.0, 0.0).astype(bf16)
    lane = lax.broadcasted_iota(i32, (blocks, LANES), 1)
    rank = jnp.zeros((slots, atoms), f32)
    counts = jnp.zeros((blocks, LANES), f32)
    for b in range(buckets):
        sums = dot_nn(members[b].astype(bf16), before)
        row_total = sums[:, atoms:].astype(bf16)
        offset = sums[:, :atoms] + dot_nn(earlier, row_total)
        rank = jnp.where(members[b] > 0.0, offset, rank)
        counts = jnp.where(lane == b, dot_nn(gather_block, row_total), counts)
    place[...] = jnp.where(live, bucket * 1024 + rank.astype(i32), -1)
    count_vec[...] = counts.astype(i32)
    copy = pltpu.make_async_copy(count_vec, count_sc, sem)
    copy.start()
    copy.wait()

    def block_body(b, block, at):
        number = count_sc[block, b]
        first = block * BLOCK_SLOTS
        places = jnp.concatenate(
            [place[pl.ds(first + t, 1), :] for t in range(BLOCK_SLOTS)], axis=1
        )

        def tile_body(tile, carry):
            feats = jnp.concatenate([feat[first + t] for t in range(BLOCK_SLOTS)], axis=1)
            wanted = lax.broadcasted_iota(i32, (TILE, wide), 0) + (b * 1024 + tile * TILE)
            pick = jnp.where(places == wanted, 1.0, 0.0).astype(bf16)
            packed[pl.ds(pl.multiple_of(at + tile * TILE, 8), TILE), :] = dot_nt(pick, feats)
            return carry

        lax.fori_loop(0, (number + (TILE - 1)) >> 7, tile_body, 0)
        return at + (((number + 7) >> 3) << 3)

    base = jnp.int32(0)
    for b in range(buckets):
        end = lax.fori_loop(0, blocks, partial(block_body, b), base)
        packed[pl.ds(pl.multiple_of(end, 8), UNIT), :] = jnp.zeros((UNIT, LANES), f32)
        held = (end - base + (UNIT - 1)) >> 8
        units_ref[micro, b] = held
        base = base + held * UNIT

    def cast_body(unit, carry):
        at = pl.ds(pl.multiple_of(unit * UNIT, UNIT), UNIT)
        table_ref[0, at, :] = packed[at, :].astype(bf16)
        return carry

    lax.fori_loop(0, base >> 8, cast_body, 0)


Q_AT, K_AT, V_AT, VEC_AT, O_AT, DK_AT, DV_AT = 0, 512, 1024, 2560, 4096, 5632, 5696
W_Q, W_K, W_V, W_VEC, W_O = 0, 1, 2, 5, 8


def edge_kernel(
    micro,
    domains,
    buckets,
    atoms,
    feat_width,
    has_prior,
    *refs,
):
    refs = list(refs)
    units_ref, count_ref, table_ref, x_ref, vec_ref, cotx_ref, cotv_ref, own_ref = refs[:8]
    halo_refs = refs[8 : 8 + domains - 1]
    at = 8 + domains - 1
    w_ref, v_ref = refs[at : at + 2]
    at += 2
    if has_prior:
        prior_m_ref, prior_v_ref = refs[at : at + 2]
        at += 2
    outx_ref, outv_ref, gown_ref = refs[at : at + 3]
    at += 3
    back_refs = refs[at : at + domains - 1]
    at += domains - 1
    gm_ref, gv_ref = refs[at : at + 2]
    at += 2
    (
        wide_w,
        wb,
        wd,
        norm_table,
        tab,
        acc,
        atom_tab,
        dir_tab,
        proj,
        go,
        agg,
        gwd,
        heads,
        hit,
        gath,
        per_atom,
        filt,
        cutb,
        pair,
        pair_sum,
        dedge,
        dfilt,
        msg,
    ) = refs[at:]

    def vector(index):
        both = [v_ref[2 * index + half : 2 * index + half + 1, :].astype(f32) for half in range(2)]
        return jnp.concatenate(both, axis=1)

    wide_w[...] = w_ref[...].astype(f32)

    def weight_block(first, stride, column, rows):
        halves = [
            wide_w[pl.ds(first + 2 * column + half, rows, stride=stride), :] for half in range(2)
        ]
        return jnp.concatenate(halves, axis=1)

    for slot, first, stride, count in (
        (W_Q, Q_AT, 2, 1),
        (W_K, K_AT, 2, 1),
        (W_V, V_AT, 6, 3),
        (W_VEC, VEC_AT, 6, 3),
        (W_O, O_AT, 6, 3),
    ):
        for column in range(count):
            wb[slot + column] = weight_block(first, stride, column, ROWS).astype(bf16)
    bias_row = lax.broadcasted_iota(i32, (LANES - NR, 1), 0) == 0
    for column in range(4):
        if column == 0:
            block = weight_block(DK_AT, 2, 0, NR)
        else:
            block = weight_block(DV_AT, 6, column - 1, NR)
        bias = jnp.where(bias_row, vector(10 + column), 0.0)
        cols = slice(column * ROWS, (column + 1) * ROWS)
        wd[:, cols] = (jnp.concatenate([block, bias], axis=0) * 0.5).astype(bf16)

    head_from = lax.broadcasted_iota(i32, (ROWS, ROWS), 0) // (feat_width // HEADS)
    head_to = lax.broadcasted_iota(i32, (ROWS, ROWS), 1) // (feat_width // HEADS)
    heads[...] = jnp.where(head_from == head_to, 0.5, 0.0).astype(bf16)

    gain = vector(0)
    shift = vector(1)
    own_hat, unused = normalise(x_ref[0])
    for domain in range(2 * buckets):
        rows = slice(domain * atoms, (domain + 1) * atoms)
        here = slice((domain % 2) * atoms, (domain % 2 + 1) * atoms)
        if domain == 0:
            norm_table[rows, :] = (own_hat * gain + shift).astype(bf16)
        elif domain < domains:
            hat = halo_refs[domain - 1][0].astype(f32)
            norm_table[rows, :] = (hat * gain + shift).astype(bf16)
        else:
            norm_table[rows, :] = jnp.zeros((atoms, feat_width), bf16)
        for axis in range(3):
            cols = slice((4 + axis) * ROWS, (5 + axis) * ROWS)
            if domain < domains:
                block = own_ref[1 + axis] if domain == 0 else halo_refs[domain - 1][1 + axis]
            else:
                block = jnp.zeros((atoms, feat_width), bf16)
            tab[domain // 2, here, cols] = block
    for b in range(buckets):
        rows = slice(b * ROWS, (b + 1) * ROWS)
        for column in range(4):
            cols = slice(column * ROWS, (column + 1) * ROWS)
            made = dot_nn(norm_table[rows, :], wb[W_K + column]) + vector(3 + column)
            tab[b, :, cols] = made.astype(bf16)

    live = (lax.broadcasted_iota(i32, (atoms, 1), 0) < count_ref[micro, 0]).astype(f32)
    query = dot_nn(norm_table[0:atoms, :], wb[W_Q]) + vector(2)
    atom_tab[:, 0:ROWS] = query.astype(bf16)
    vec_low = own_ref[1:].reshape(3 * atoms, feat_width)
    for part in range(3):
        proj[part] = dot_nn(vec_low, wb[W_VEC + part])
    parts = [slice(axis * atoms, (axis + 1) * atoms) for axis in range(3)]
    cot_x = cotx_ref[0] * live
    vec_dot = jnp.zeros((atoms, feat_width), f32)
    go_one = jnp.zeros((atoms, feat_width), f32)
    for axis in range(3):
        cot_v = cotv_ref[0, axis] * live
        vec_dot += proj[0, parts[axis], :] * proj[1, parts[axis], :]
        go_one += proj[2, parts[axis], :] * cot_v
        low = cot_v.astype(bf16)
        dir_tab[parts[axis], :] = low
        atom_tab[:, (2 + axis) * ROWS : (3 + axis) * ROWS] = low
    go[0] = go_one.astype(bf16)
    go[1] = (vec_dot * cot_x).astype(bf16)
    go[2] = cot_x.astype(bf16)
    g_agg = dot_nt(go[0], wb[W_O])
    for part in range(1, 3):
        g_agg += dot_nt(go[part], wb[W_O + part])
    atom_tab[:, ROWS : 2 * ROWS] = g_agg.astype(bf16)

    agg[...] = jnp.zeros_like(agg)
    gwd[...] = jnp.zeros_like(gwd)
    for b in range(buckets):
        acc[b] = jnp.zeros((ROWS, 7 * ROWS), f32)

    lane_row = lax.broadcasted_iota(i32, (UNIT, ROWS), 1).astype(f32) + 1.0
    lane_atom = lax.broadcasted_iota(i32, (UNIT, LANES), 1).astype(f32) + 1.0
    sub_row = lax.broadcasted_iota(i32, (ROWS, UNIT), 0).astype(f32) + 1.0
    sub_atom = lax.broadcasted_iota(i32, (atoms, UNIT), 0).astype(f32) + 1.0

    def unit_body(b, first, unit, carry):
        rows = pl.ds(pl.multiple_of((first + unit) * UNIT, UNIT), UNIT)
        low = table_ref[0, rows, :]
        full = low.astype(f32)
        turned = full.T

        def column(index):
            return full[:, NR + index : NR + index + 1]

        def across(index):
            return turned[NR + index : NR + index + 1, :]

        hit[...] = jnp.where(column(1) == lane_row, 1.0, 0.0).astype(bf16)
        cutb[...] = jnp.broadcast_to(column(3) + column(4), (UNIT, LANES))
        atom_hit = column(2) == lane_atom
        atom_one = jnp.where(atom_hit, 1.0, 0.0).astype(bf16)
        for block in range(7):
            cols = slice(block * ROWS, (block + 1) * ROWS)
            gath[:, cols] = dot_nn(hit[...], tab[b, :, cols])
        for block in range(5):
            cols = slice(block * ROWS, (block + 1) * ROWS)
            per_atom[:, cols] = dot_nn(atom_one, atom_tab[:, cols])
        along = jnp.concatenate(
            [jnp.where(atom_hit, column(5 + axis), 0.0).astype(bf16) for axis in range(3)],
            axis=1,
        )
        per_atom[:, 5 * ROWS :] = dot_nn(along, dir_tab[...])
        for block in range(4):
            cols = slice(block * ROWS, (block + 1) * ROWS)
            filt[:, cols] = dot_nn(low, wd[:, cols])

        def part(ref, block, here, half):
            start = block * ROWS + half * LANES
            return ref[here, start : start + LANES]

        def gate(here, block, half):
            value = part(filt, block, here, half)
            lift = 1.0 + jnp.tanh(value)
            return lift, value * lift

        def first_stage(step, carry):
            here = pl.ds(pl.multiple_of(step * 16, 16), 16)
            there = pl.ds(pl.multiple_of(UNIT + step * 16, 16), 16)
            for half in range(2):
                cols = slice(half * LANES, (half + 1) * LANES)
                silu_k = gate(here, 0, half)[1]
                silu_x = gate(here, 1, half)[1]
                score = part(per_atom, 0, here, half) * part(gath, 0, here, half) * silu_k
                back = part(per_atom, 1, here, half) * part(gath, 1, here, half) * silu_x
                pair[here, cols] = score.astype(bf16)
                pair[there, cols] = back.astype(bf16)
            return carry

        lax.fori_loop(0, UNIT // 16, first_stage, 0, unroll=2)
        pair_sum[...] = dot_nn(pair[...], heads[...])

        def second_stage(step, carry):
            here = pl.ds(pl.multiple_of(step * 16, 16), 16)
            there = pl.ds(pl.multiple_of(UNIT + step * 16, 16), 16)
            cut = cutb[here, :]
            for half in range(2):
                cols = slice(half * LANES, (half + 1) * LANES)

                def put(ref, block, value):
                    start = block * ROWS + half * LANES
                    ref[here, start : start + LANES] = value.astype(bf16)

                half_score = pair_sum[here, cols]
                lift = 1.0 + jnp.tanh(half_score)
                silu_s = half_score * lift
                attention = silu_s * cut
                dscore = pair_sum[there, cols] * cut * (lift + silu_s * (2.0 - lift))

                query_e = part(per_atom, 0, here, half)
                key_e = part(gath, 0, here, half)
                lift, silu = gate(here, 0, half)
                scaled = dscore * query_e
                put(dedge, 0, scaled * silu)
                put(dfilt, 0, scaled * key_e * (lift + silu * (2.0 - lift)))
                put(msg, 4, dscore * key_e * silu)

                value_e = part(gath, 1, here, half)
                lift, silu = gate(here, 1, half)
                down = part(per_atom, 1, here, half) * attention
                put(dedge, 1, down * silu)
                put(dfilt, 1, down * value_e * (lift + silu * (2.0 - lift)))
                put(msg, 0, value_e * silu * attention)

                value_e = part(gath, 2, here, half)
                lift, silu = gate(here, 2, half)
                gated = value_e * silu
                down = jnp.zeros_like(gated)
                for axis in range(3):
                    vec_e = part(gath, 4 + axis, here, half)
                    cot_e = part(per_atom, 2 + axis, here, half)
                    down += cot_e * vec_e
                    put(msg, 1 + axis, vec_e * gated)
                    put(dedge, 4 + axis, cot_e * gated)
                put(dedge, 2, down * silu)
                put(dfilt, 2, down * value_e * (lift + silu * (2.0 - lift)))

                value_e = part(gath, 3, here, half)
                lift, silu = gate(here, 3, half)
                down = part(per_atom, 5, here, half)
                put(dedge, 3, down * silu)
                put(dfilt, 3, down * value_e * (lift + silu * (2.0 - lift)))
                put(msg, 5, value_e * silu)
            return carry

        lax.fori_loop(0, UNIT // 16, second_stage, 0, unroll=2)

        hit_t = jnp.where(across(1) == sub_row, 1.0, 0.0).astype(bf16)
        for block in range(7):
            cols = slice(block * ROWS, (block + 1) * ROWS)
            acc[b, :, cols] += dot_nn(hit_t, dedge[:, cols])
        atom_hit_t = across(2) == sub_atom
        atom_one_t = jnp.where(atom_hit_t, 1.0, 0.0).astype(bf16)
        for block in (0, 4):
            cols = slice(block * ROWS, (block + 1) * ROWS)
            agg[:, cols] += dot_nn(atom_one_t, msg[:, cols])
        for axis in range(3):
            cols = slice((1 + axis) * ROWS, (2 + axis) * ROWS)
            along_t = jnp.where(atom_hit_t, across(5 + axis), 0.0).astype(bf16)
            agg[:, cols] += dot_nn(atom_one_t, msg[:, cols]) + dot_nn(
                along_t, msg[:, 5 * ROWS :]
            )
        feats_t = turned.astype(bf16)
        for block in range(4):
            cols = slice(block * ROWS, (block + 1) * ROWS)
            gwd[:, cols] += dot_nn(feats_t, dfilt[:, cols])
        return carry

    first = jnp.int32(0)
    for b in range(buckets):
        number = units_ref[micro, b]
        lax.fori_loop(0, number, partial(unit_body, b, first), 0)
        first = first + number

    agg_low = agg[:, 0:ROWS].astype(bf16)
    outs = [dot_nn(agg_low, wb[W_O + part]) + vector(7 + part) for part in range(3)]
    outx_ref[...] = x_ref[0] + (vec_dot * outs[1] + outs[2]) * live
    g_dot = cot_x * outs[1]
    for axis in range(3):
        rows = parts[axis]
        vec_agg = agg[:, (1 + axis) * ROWS : (2 + axis) * ROWS]
        outv_ref[axis] = vec_ref[0, axis] + (proj[2, rows, :] * outs[0] + vec_agg) * live
        proj[2, rows, :] = cotv_ref[0, axis] * live * outs[0]
        held = proj[0, rows, :]
        proj[0, rows, :] = g_dot * proj[1, rows, :]
        proj[1, rows, :] = g_dot * held

    def put_grad(first, stride, column, rows, value):
        for half in range(2):
            at = pl.ds(first + 2 * column + half, rows, stride=stride)
            gm_ref[at, :] = value[:, half * LANES : (half + 1) * LANES]

    def put_vector(index, value):
        for half in range(2):
            row = 2 * index + half
            gv_ref[row : row + 1, :] = value[:, half * LANES : (half + 1) * LANES]

    def column_sum(value):
        return jnp.sum(value.astype(f32), axis=0, keepdims=True)

    put_vector(0, jnp.zeros((1, ROWS), f32))
    put_vector(1, jnp.zeros((1, ROWS), f32))
    g_vec = jnp.zeros((3 * atoms, feat_width), f32)
    for part in range(3):
        put_grad(O_AT, 6, part, ROWS, dot_tn(agg_low, go[part]))
        put_vector(7 + part, column_sum(go[part]))
        gp = proj[part].astype(bf16)
        put_grad(VEC_AT, 6, part, ROWS, dot_tn(vec_low, gp))
        g_vec += dot_nt(gp, wb[W_VEC + part])

    g_query = agg[:, 4 * ROWS : 5 * ROWS].astype(bf16)
    put_grad(Q_AT, 2, 0, ROWS, dot_tn(norm_table[0:atoms, :], g_query))
    put_vector(2, column_sum(g_query))
    g_norm = dot_nt(g_query, wb[W_Q])

    sums = [jnp.zeros((ROWS, ROWS), f32) for column in range(4)]
    biases = [jnp.zeros((1, ROWS), f32) for column in range(4)]
    for b in range(buckets):
        rows = slice(b * ROWS, (b + 1) * ROWS)
        g_table = jnp.zeros((ROWS, ROWS), f32)
        for column in range(4):
            low = acc[b, :, column * ROWS : (column + 1) * ROWS].astype(bf16)
            sums[column] += dot_tn(norm_table[rows, :], low)
            biases[column] += column_sum(low)
            g_table += dot_nt(low, wb[W_K + column])
        for half in range(2):
            domain = 2 * b + half
            if domain >= domains:
                continue
            here = slice(half * atoms, (half + 1) * atoms)
            if domain == 0:
                gown_ref[0] = g_table[here, :] + g_norm
            else:
                back_refs[domain - 1][0] = g_table[here, :].astype(bf16)
            for axis in range(3):
                block = acc[b, here, (4 + axis) * ROWS : (5 + axis) * ROWS]
                if domain == 0:
                    gown_ref[1 + axis] = block + g_vec[parts[axis], :]
                else:
                    back_refs[domain - 1][1 + axis] = block.astype(bf16)
    for column in range(4):
        if column == 0:
            put_grad(K_AT, 2, 0, ROWS, sums[column])
        else:
            put_grad(V_AT, 6, column - 1, ROWS, sums[column])
        put_vector(3 + column, biases[column])
        cols = slice(column * ROWS, (column + 1) * ROWS)
        block = gwd[0:NR, cols] * 0.5
        if column == 0:
            put_grad(DK_AT, 2, 0, NR, block)
        else:
            put_grad(DV_AT, 6, column - 1, NR, block)
        put_vector(10 + column, gwd[NR : NR + 1, cols] * 0.5)
    if has_prior:
        gm_ref[...] += prior_m_ref[...]
        gv_ref[...] += prior_v_ref[...]


def close_kernel(domains, x_ref, cotx_ref, cotv_ref, gown_ref, *refs):
    back_refs = refs[: domains - 1]
    v_ref, gx_ref, gvec_ref, gln_ref = refs[domains - 1 :]
    total = [gown_ref[part] for part in range(4)]
    for back_ref in back_refs:
        for part in range(4):
            total[part] = total[part] + back_ref[part].astype(f32)
    gain = jnp.concatenate([v_ref[half : half + 1, :].astype(f32) for half in range(2)], axis=1)
    hat, spread = normalise(x_ref[0])
    for at, value in ((0, total[0] * hat), (2, total[0])):
        summed = jnp.sum(value, axis=0, keepdims=True)
        for half in range(2):
            gln_ref[at + half : at + half + 1, :] = summed[:, half * LANES : (half + 1) * LANES]
    g_hat = total[0] * gain
    g_x = spread * (g_hat - lane_mean(g_hat) - hat * lane_mean(g_hat * hat))
    gx_ref[...] = cotx_ref[0] + g_x
    for axis in range(3):
        gvec_ref[axis] = cotv_ref[0, axis] + total[1 + axis]


def adam_update(weight, grad, first, second):
    first_new = beta_one * first + (1.0 - beta_one) * grad
    second_new = beta_two * second + (1.0 - beta_two) * grad * grad
    first_hat = first_new / (1.0 - beta_one**STEP)
    second_hat = second_new / (1.0 - beta_two**STEP)
    weight_new = weight - learn_rate * (
        first_hat / (jnp.sqrt(second_hat) + adam_eps) + decay_rate * weight
    )
    return (weight_new, first_new, second_new)


def from_behind(shard, axis, by):
    length = lax.axis_size(axis)
    return lax.ppermute(shard, axis, [(i, (i + by) % length) for i in range(length)])


def micro_block(shape, micro):
    rest = tuple(shape[1:])
    zeros = (0,) * len(rest)
    return pl.BlockSpec((1,) + rest, lambda i: (micro,) + zeros)


def shards(
    x_in,
    vec_in,
    cot_x,
    cot_vec,
    mats,
    vecs,
    mats_first,
    mats_second,
    vecs_first,
    vecs_second,
    atom_count,
    neighbours,
    edge_mask,
    edge_vec,
    send_list,
):
    micros, atoms, width = x_in.shape
    slots = neighbours.shape[1]
    halo = send_list.shape[-1]
    per_face = halo // LANES
    cells, depth = lax.axis_size("cells"), lax.axis_size("depth")
    faces = [("cells", 1), ("cells", -1), ("cells", FOLD), ("cells", -FOLD), ("depth", 1), ("depth", -1)]
    sizes = {"cells": cells, "depth": depth}
    sources = []
    face_source = []
    for axis, by in faces:
        key = (axis, by % sizes[axis])
        if key not in sources:
            sources.append(key)
        face_source.append(sources.index(key))
    domains = 1 + len(sources)
    buckets = (domains * atoms + ROWS - 1) // ROWS
    block_of = [1 + face_source[row // per_face] for row in range(6 * per_face)]

    whole = pl.BlockSpec(memory_space=pltpu.VMEM)
    scalars = pl.BlockSpec(memory_space=pltpu.SMEM)

    lists = [None] * 6
    for index, (axis, by) in enumerate(sources):
        mine = [face for face in range(6) if face_source[face] == index]
        sent = jnp.stack([send_list[:, face] for face in mine], axis=1)
        got = from_behind(sent, axis, by)
        for order, face in enumerate(mine):
            lists[face] = got[:, order]
    list_rows = jnp.stack(lists, axis=1).reshape(micros, 6 * per_face, LANES)

    own = pl.pallas_call(
        norm_kernel,
        out_shape=tuple(
            jax.ShapeDtypeStruct((4, atoms, width), bf16) for micro in range(micros)
        ),
        in_specs=[whole] * 2,
        out_specs=[whole] * micros,
        name="norm",
    )(x_in, vec_in)

    halos = [[from_behind(own[micro], axis, by) for axis, by in sources] for micro in range(micros)]

    mats_rows = mats.reshape(-1, LANES)
    w_all = lax.all_gather(mats_rows.astype(bf16), "cells", axis=0, tiled=True)
    v_all = lax.all_gather(vecs.astype(bf16), "cells", axis=0, tiled=True).reshape(-1, LANES)
    w_rows, v_rows = w_all.shape[0], v_all.shape[0]

    limit = slots * atoms + buckets * (slots // BLOCK_SLOTS) * 8 + buckets * UNIT
    capacity = (limit + UNIT - 1) // UNIT * UNIT

    def by_micro(shape):
        zeros = (0,) * (len(shape) - 1)
        return pl.BlockSpec((1,) + tuple(shape[1:]), lambda i: (i,) + zeros)

    edge_table, units = pl.pallas_call(
        partial(prep_kernel, block_of, buckets),
        out_shape=(
            jax.ShapeDtypeStruct((micros, capacity, LANES), bf16),
            jax.ShapeDtypeStruct((micros, buckets), i32),
        ),
        grid=(micros,),
        in_specs=[
            by_micro(neighbours.shape),
            by_micro(edge_mask.shape),
            by_micro(edge_vec.shape),
            by_micro(list_rows.shape),
        ],
        out_specs=[by_micro((micros, capacity, LANES)), scalars],
        scratch_shapes=[
            pltpu.VMEM((slots, LANES, LANES), bf16),
            pltpu.VMEM((slots, atoms), i32),
            pltpu.VMEM((slots // BLOCK_SLOTS, LANES), i32),
            pltpu.SMEM((slots // BLOCK_SLOTS, LANES), i32),
            pltpu.VMEM((capacity + UNIT, LANES), f32),
            pltpu.SemaphoreType.DMA(()),
        ],
        compiler_params=pltpu.CompilerParams(vmem_limit_bytes=VMEM_LIMIT),
        name="prep",
    )(neighbours, edge_mask, edge_vec, list_rows)

    grads = []
    outs = []
    for micro in range(micros):
        prior = list(grads)
        operands = [
            units,
            atom_count,
            edge_table,
            x_in,
            vec_in,
            cot_x,
            cot_vec,
            own[micro],
            *halos[micro],
            w_all,
            v_all,
            *prior,
        ]
        specs = (
            [scalars, scalars]
            + [
                micro_block(array.shape, micro)
                for array in (edge_table, x_in, vec_in, cot_x, cot_vec)
            ]
            + [whole] * (1 + len(sources) + 2 + len(prior))
        )
        shapes = (
            [
                jax.ShapeDtypeStruct((atoms, width), f32),
                jax.ShapeDtypeStruct((3, atoms, width), f32),
                jax.ShapeDtypeStruct((4, atoms, width), f32),
            ]
            + [jax.ShapeDtypeStruct((4, atoms, width), bf16)] * len(sources)
            + [
                jax.ShapeDtypeStruct((w_rows, LANES), f32),
                jax.ShapeDtypeStruct((v_rows, LANES), f32),
            ]
        )
        results = pl.pallas_call(
            partial(edge_kernel, micro, domains, buckets, atoms, width, bool(prior)),
            out_shape=tuple(shapes),
            grid=(1,),
            in_specs=specs,
            out_specs=[whole] * len(shapes),
            scratch_shapes=[
                pltpu.VMEM((w_rows, LANES), f32),
                pltpu.VMEM((11, ROWS, ROWS), bf16),
                pltpu.VMEM((LANES, 4 * ROWS), bf16),
                pltpu.VMEM((buckets * ROWS, ROWS), bf16),
                pltpu.VMEM((buckets, ROWS, 7 * ROWS), bf16),
                pltpu.VMEM((buckets, ROWS, 7 * ROWS), f32),
                pltpu.VMEM((atoms, 5 * ROWS), bf16),
                pltpu.VMEM((3 * atoms, ROWS), bf16),
                pltpu.VMEM((3, 3 * atoms, ROWS), f32),
                pltpu.VMEM((3, atoms, ROWS), bf16),
                pltpu.VMEM((atoms, 5 * ROWS), f32),
                pltpu.VMEM((LANES, 4 * ROWS), f32),
                pltpu.VMEM((ROWS, ROWS), bf16),
                pltpu.VMEM((UNIT, ROWS), bf16),
                pltpu.VMEM((UNIT, 7 * ROWS), f32),
                pltpu.VMEM((UNIT, 6 * ROWS), f32),
                pltpu.VMEM((UNIT, 4 * ROWS), f32),
                pltpu.VMEM((UNIT, LANES), f32),
                pltpu.VMEM((2 * UNIT, ROWS), bf16),
                pltpu.VMEM((2 * UNIT, ROWS), f32),
                pltpu.VMEM((UNIT, 7 * ROWS), bf16),
                pltpu.VMEM((UNIT, 4 * ROWS), bf16),
                pltpu.VMEM((UNIT, 6 * ROWS), bf16),
            ],
            compiler_params=pltpu.CompilerParams(vmem_limit_bytes=VMEM_LIMIT),
            name="edges",
        )(*operands)
        outs.append(results)
        grads = list(results[-2:])

    closed = []
    for micro in range(micros):
        back = outs[micro][3 : 3 + len(sources)]
        returned = [
            from_behind(block, axis, -by) for block, (axis, by) in zip(back, sources)
        ]
        closed.append(
            pl.pallas_call(
                partial(close_kernel, domains),
                out_shape=(
                    jax.ShapeDtypeStruct((atoms, width), f32),
                    jax.ShapeDtypeStruct((3, atoms, width), f32),
                    jax.ShapeDtypeStruct((4, LANES), f32),
                ),
                grid=(1,),
                in_specs=[
                    micro_block(array.shape, micro) for array in (x_in, cot_x, cot_vec)
                ]
                + [whole] * (2 + len(sources)),
                out_specs=[whole] * 3,
                name="close",
            )(x_in, cot_x, cot_vec, outs[micro][2], *returned, v_all)
        )

    grad_m, grad_v = grads
    grad_norm = closed[0][2]
    for micro in range(1, micros):
        grad_norm = grad_norm + closed[micro][2]
    sum_mats = lax.psum_scatter(grad_m, "cells", scatter_dimension=0, tiled=True)
    sum_mats = lax.psum(sum_mats, "depth").reshape(-1)
    grad_v = jnp.concatenate([grad_norm, grad_v[4:]], axis=0)
    sum_vecs = lax.psum(grad_v, ("cells", "depth")).reshape(-1)
    sum_vecs = lax.dynamic_slice_in_dim(
        sum_vecs, lax.axis_index("cells") * vecs.shape[0], vecs.shape[0]
    )
    new_mats, mats_one, mats_two = adam_update(mats, sum_mats, mats_first, mats_second)
    new_vecs, vecs_one, vecs_two = adam_update(vecs, sum_vecs, vecs_first, vecs_second)
    return (
        jnp.stack([result[0] for result in outs]),
        jnp.stack([result[1] for result in outs]),
        jnp.stack([result[0] for result in closed]),
        jnp.stack([result[1] for result in closed]),
        sum_mats,
        sum_vecs,
        new_mats,
        new_vecs,
        mats_one,
        mats_two,
        vecs_one,
        vecs_two,
    )


def solution(mesh):
    by_atom = ("cells", "depth")
    shard = P("cells")
    in_specs = (
        P(None, by_atom, None),
        P(None, None, by_atom, None),
        P(None, by_atom, None),
        P(None, None, by_atom, None),
        shard,
        shard,
        shard,
        shard,
        shard,
        shard,
        P(None, by_atom),
        P(None, None, by_atom),
        P(None, None, by_atom),
        P(None, None, None, by_atom),
        P(None, by_atom, None),
    )
    out_specs = (
        P(None, by_atom, None),
        P(None, None, by_atom, None),
        P(None, by_atom, None),
        P(None, None, by_atom, None),
    ) + (shard,) * 8
    return jax.shard_map(shards, mesh=mesh, in_specs=in_specs, out_specs=out_specs, check_vma=False)
```

```python
from functools import partial
import math

import jax
import jax.numpy as jnp
from jax import lax
from jax.experimental import pallas as pl
from jax.experimental.pallas import tpu as pltpu
from jax.sharding import PartitionSpec as P

HEADS = 8
NR = 32
FOLD = 4
STEP = 3

LANES = 128
ROWS = 256
UNIT = 256
BLOCK_SLOTS = 4
TILE = 128

norm_eps = 1e-05
cut_radius = 5.0
beta_one = 0.5
beta_two = 0.5
learn_rate = 0.05
decay_rate = 0.01
adam_eps = 1e-08

f32 = jnp.float32
bf16 = jnp.bfloat16
i32 = jnp.int32

VMEM_LIMIT = 60 * 1024 * 1024


def dot_nn(left, right):
    return lax.dot_general(left, right, (((1,), (0,)), ((), ())), preferred_element_type=f32)


def dot_nt(left, right):
    return lax.dot_general(left, right, (((1,), (1,)), ((), ())), preferred_element_type=f32)


def dot_tn(left, right):
    return lax.dot_general(left, right, (((0,), (0,)), ((), ())), preferred_element_type=f32)


def lane_mean(block):
    return jnp.sum(block, axis=-1, keepdims=True) * (1.0 / block.shape[-1])


def normalise(block):
    centered = block - lane_mean(block)
    spread = lax.rsqrt(lane_mean(centered * centered) + norm_eps)
    return centered * spread, spread


def norm_kernel(x_ref, vec_ref, mats_ref, *refs):
    *own_refs, low_ref = refs
    quarter = low_ref.shape[1]
    for part in range(low_ref.shape[0]):
        low_ref[part] = mats_ref[part * quarter : (part + 1) * quarter, :].astype(bf16)
    for micro, own_ref in enumerate(own_refs):
        own_ref[0] = normalise(x_ref[micro])[0].astype(bf16)
        own_ref[1:] = vec_ref[micro].astype(bf16)


def prep_kernel(
    block_of,
    buckets,
    nbr_ref,
    mask_ref,
    geom_ref,
    list_ref,
    table_ref,
    units_ref,
    feat,
    place,
    count_vec,
    count_sc,
    packed,
    sem,
):
    micro = pl.program_id(0)
    slots, atoms = nbr_ref.shape[1], nbr_ref.shape[2]
    blocks = slots // BLOCK_SLOTS
    wide = BLOCK_SLOTS * atoms

    @pl.when(micro == 0)
    def _():
        feat[...] = jnp.zeros_like(feat)

    source = nbr_ref[0]
    live = mask_ref[0] > 0
    halo_at = source - atoms
    list_row = halo_at >> 7
    list_lane = halo_at & (LANES - 1)
    atom_in = source
    block_id = jnp.zeros_like(source)
    for row in range(list_ref.shape[1]):
        table = jnp.broadcast_to(list_ref[0, row : row + 1, :], (slots, atoms))
        picked = jnp.take_along_axis(table, list_lane, axis=1)
        here = list_row == row
        atom_in = jnp.where(here, picked, atom_in)
        block_id = jnp.where(here, block_of[row], block_id)
    entry = block_id * atoms + atom_in
    bucket = entry >> 8
    low = ((entry & (ROWS - 1)) + 1).astype(f32)
    atom_id = (lax.broadcasted_iota(i32, (slots, atoms), 1) + 1).astype(f32)
    live_float = live.astype(f32)

    comps = [geom_ref[0, axis] for axis in range(3)]
    radius = jnp.sqrt(comps[0] * comps[0] + comps[1] * comps[1] + comps[2] * comps[2])
    units = [comp / radius for comp in comps]
    cut = 0.5 * (jnp.cos(math.pi * radius / cut_radius) + 1.0) * live_float
    cut_high = cut.astype(bf16).astype(f32)
    cut_low = cut - cut_high
    decayed = jnp.exp(-(5.0 / cut_radius) * radius)
    start_value = math.exp(-cut_radius)
    ramp = lax.broadcasted_iota(i32, (NR, 1), 0).astype(f32) / float(NR - 1)
    centers = start_value * (1.0 - ramp) + ramp
    width_coef = (2.0 / NR * (1.0 - start_value)) ** (-2)
    extras = [live_float, low, atom_id, cut_high, cut_low] + units
    zeros = jnp.zeros((16 - len(extras), atoms), f32)
    for slot in range(slots):
        gap = decayed[slot : slot + 1, :] - centers
        basis = cut[slot : slot + 1, :] * jnp.exp(-width_coef * gap * gap)
        feat[slot, 0:NR, :] = basis.astype(bf16)
        rows = [extra[slot : slot + 1, :] for extra in extras] + [zeros]
        feat[slot, NR : NR + 16, :] = jnp.concatenate(rows, axis=0).astype(bf16)

    members = [jnp.where(live & (bucket == b), 1.0, 0.0) for b in range(buckets)]
    lane_from = lax.broadcasted_iota(i32, (atoms, 2 * atoms), 0)
    lane_to = lax.broadcasted_iota(i32, (atoms, 2 * atoms), 1)
    before = jnp.where((lane_from < lane_to) | (lane_to >= atoms), 1.0, 0.0).astype(bf16)
    slot_to = lax.broadcasted_iota(i32, (slots, slots), 0)
    slot_from = lax.broadcasted_iota(i32, (slots, slots), 1)
    same = (slot_to // BLOCK_SLOTS) == (slot_from // BLOCK_SLOTS)
    earlier = jnp.where(same & (slot_from < slot_to), 1.0, 0.0).astype(bf16)
    block_row = lax.broadcasted_iota(i32, (blocks, slots), 0)
    block_slot = lax.broadcasted_iota(i32, (blocks, slots), 1)
    gather_block = jnp.where(block_slot // BLOCK_SLOTS == block_row, 1.0, 0.0).astype(bf16)
    lane = lax.broadcasted_iota(i32, (blocks, LANES), 1)
    rank = jnp.zeros((slots, atoms), f32)
    counts = jnp.zeros((blocks, LANES), f32)
    for b in range(buckets):
        sums = dot_nn(members[b].astype(bf16), before)
        row_total = sums[:, atoms:].astype(bf16)
        offset = sums[:, :atoms] + dot_nn(earlier, row_total)
        rank = jnp.where(members[b] > 0.0, offset, rank)
        counts = jnp.where(lane == b, dot_nn(gather_block, row_total), counts)
    place[...] = jnp.where(live, bucket * 1024 + rank.astype(i32), -1)
    count_vec[...] = counts.astype(i32)
    copy = pltpu.make_async_copy(count_vec, count_sc, sem)
    copy.start()
    copy.wait()

    def block_body(b, block, at):
        number = count_sc[block, b]
        first = block * BLOCK_SLOTS
        places = jnp.concatenate(
            [place[pl.ds(first + t, 1), :] for t in range(BLOCK_SLOTS)], axis=1
        )

        def tile_body(tile, carry):
            feats = jnp.concatenate([feat[first + t] for t in range(BLOCK_SLOTS)], axis=1)
            wanted = lax.broadcasted_iota(i32, (TILE, wide), 0) + (b * 1024 + tile * TILE)
            pick = jnp.where(places == wanted, 1.0, 0.0).astype(bf16)
            packed[pl.ds(pl.multiple_of(at + tile * TILE, 8), TILE), :] = dot_nt(pick, feats)
            return carry

        lax.fori_loop(0, (number + (TILE - 1)) >> 7, tile_body, 0)
        return at + (((number + 7) >> 3) << 3)

    base = jnp.int32(0)
    for b in range(buckets):
        end = lax.fori_loop(0, blocks, partial(block_body, b), base)
        packed[pl.ds(pl.multiple_of(end, 8), UNIT), :] = jnp.zeros((UNIT, LANES), f32)
        held = (end - base + (UNIT - 1)) >> 8
        units_ref[micro, b] = held
        base = base + held * UNIT

    def cast_body(unit, carry):
        at = pl.ds(pl.multiple_of(unit * UNIT, UNIT), UNIT)
        table_ref[0, at, :] = packed[at, :].astype(bf16)
        return carry

    lax.fori_loop(0, base >> 8, cast_body, 0)


Q_AT, K_AT, V_AT, VEC_AT, O_AT, DK_AT, DV_AT = 0, 512, 1024, 2560, 4096, 5632, 5696
W_Q, W_K, W_V, W_VEC, W_O = 0, 1, 2, 5, 8


def edge_kernel(
    micro,
    domains,
    buckets,
    atoms,
    feat_width,
    has_prior,
    *refs,
):
    refs = list(refs)
    units_ref, count_ref, table_ref, x_ref, vec_ref, cotx_ref, cotv_ref, own_ref = refs[:8]
    halo_refs = refs[8 : 8 + domains - 1]
    at = 8 + domains - 1
    w_ref, v_ref = refs[at : at + 2]
    at += 2
    if has_prior:
        prior_m_ref, prior_v_ref = refs[at : at + 2]
        at += 2
    outx_ref, outv_ref, gown_ref = refs[at : at + 3]
    at += 3
    back_refs = refs[at : at + domains - 1]
    at += domains - 1
    gm_ref, gv_ref = refs[at : at + 2]
    at += 2
    (
        wide_w,
        wb,
        wd,
        norm_table,
        tab,
        acc,
        atom_tab,
        dir_tab,
        proj,
        go,
        agg,
        gwd,
        heads,
        hit,
        gath,
        per_atom,
        filt,
        cutb,
        pair,
        pair_sum,
        dedge,
        dfilt,
        msg,
    ) = refs[at:]

    def vector(index):
        both = [v_ref[2 * index + half : 2 * index + half + 1, :].astype(f32) for half in range(2)]
        return jnp.concatenate(both, axis=1)

    cells, parts_w, quarter = w_ref.shape[0], w_ref.shape[1], w_ref.shape[2]
    for cell in range(cells):
        for part in range(parts_w):
            start = (cell * parts_w + part) * quarter
            wide_w[start : start + quarter, :] = w_ref[cell, part].astype(f32)

    def weight_block(first, stride, column, rows):
        halves = [
            wide_w[pl.ds(first + 2 * column + half, rows, stride=stride), :] for half in range(2)
        ]
        return jnp.concatenate(halves, axis=1)

    for slot, first, stride, count in (
        (W_Q, Q_AT, 2, 1),
        (W_K, K_AT, 2, 1),
        (W_V, V_AT, 6, 3),
        (W_VEC, VEC_AT, 6, 3),
        (W_O, O_AT, 6, 3),
    ):
        for column in range(count):
            wb[slot + column] = weight_block(first, stride, column, ROWS).astype(bf16)
    bias_row = lax.broadcasted_iota(i32, (LANES - NR, 1), 0) == 0
    for column in range(4):
        if column == 0:
            block = weight_block(DK_AT, 2, 0, NR)
        else:
            block = weight_block(DV_AT, 6, column - 1, NR)
        bias = jnp.where(bias_row, vector(10 + column), 0.0)
        cols = slice(column * ROWS, (column + 1) * ROWS)
        wd[:, cols] = (jnp.concatenate([block, bias], axis=0) * 0.5).astype(bf16)

    head_from = lax.broadcasted_iota(i32, (ROWS, ROWS), 0) // (feat_width // HEADS)
    head_to = lax.broadcasted_iota(i32, (ROWS, ROWS), 1) // (feat_width // HEADS)
    heads[...] = jnp.where(head_from == head_to, 0.5, 0.0).astype(bf16)

    gain = vector(0)
    shift = vector(1)
    own_hat, unused = normalise(x_ref[0])
    for domain in range(2 * buckets):
        rows = slice(domain * atoms, (domain + 1) * atoms)
        here = slice((domain % 2) * atoms, (domain % 2 + 1) * atoms)
        if domain == 0:
            norm_table[rows, :] = (own_hat * gain + shift).astype(bf16)
        elif domain < domains:
            hat = halo_refs[domain - 1][0].astype(f32)
            norm_table[rows, :] = (hat * gain + shift).astype(bf16)
        else:
            norm_table[rows, :] = jnp.zeros((atoms, feat_width), bf16)
        for axis in range(3):
            cols = slice((4 + axis) * ROWS, (5 + axis) * ROWS)
            if domain < domains:
                block = own_ref[1 + axis] if domain == 0 else halo_refs[domain - 1][1 + axis]
            else:
                block = jnp.zeros((atoms, feat_width), bf16)
            tab[domain // 2, here, cols] = block
    for b in range(buckets):
        rows = slice(b * ROWS, (b + 1) * ROWS)
        for column in range(4):
            cols = slice(column * ROWS, (column + 1) * ROWS)
            made = dot_nn(norm_table[rows, :], wb[W_K + column]) + vector(3 + column)
            tab[b, :, cols] = made.astype(bf16)

    live = (lax.broadcasted_iota(i32, (atoms, 1), 0) < count_ref[micro, 0]).astype(f32)
    query = dot_nn(norm_table[0:atoms, :], wb[W_Q]) + vector(2)
    atom_tab[:, 0:ROWS] = query.astype(bf16)
    vec_low = own_ref[1:].reshape(3 * atoms, feat_width)
    for part in range(3):
        proj[part] = dot_nn(vec_low, wb[W_VEC + part])
    parts = [slice(axis * atoms, (axis + 1) * atoms) for axis in range(3)]
    cot_x = cotx_ref[0] * live
    vec_dot = jnp.zeros((atoms, feat_width), f32)
    go_one = jnp.zeros((atoms, feat_width), f32)
    for axis in range(3):
        cot_v = cotv_ref[0, axis] * live
        vec_dot += proj[0, parts[axis], :] * proj[1, parts[axis], :]
        go_one += proj[2, parts[axis], :] * cot_v
        low = cot_v.astype(bf16)
        dir_tab[parts[axis], :] = low
        atom_tab[:, (2 + axis) * ROWS : (3 + axis) * ROWS] = low
    go[0] = go_one.astype(bf16)
    go[1] = (vec_dot * cot_x).astype(bf16)
    go[2] = cot_x.astype(bf16)
    g_agg = dot_nt(go[0], wb[W_O])
    for part in range(1, 3):
        g_agg += dot_nt(go[part], wb[W_O + part])
    atom_tab[:, ROWS : 2 * ROWS] = g_agg.astype(bf16)

    agg[...] = jnp.zeros_like(agg)
    gwd[...] = jnp.zeros_like(gwd)
    for b in range(buckets):
        acc[b] = jnp.zeros((ROWS, 7 * ROWS), f32)

    lane_row = lax.broadcasted_iota(i32, (UNIT, ROWS), 1).astype(f32) + 1.0
    lane_atom = lax.broadcasted_iota(i32, (UNIT, LANES), 1).astype(f32) + 1.0
    sub_row = lax.broadcasted_iota(i32, (ROWS, UNIT), 0).astype(f32) + 1.0
    sub_atom = lax.broadcasted_iota(i32, (atoms, UNIT), 0).astype(f32) + 1.0

    def unit_body(b, first, unit, carry):
        rows = pl.ds(pl.multiple_of((first + unit) * UNIT, UNIT), UNIT)
        low = table_ref[0, rows, :]
        full = low.astype(f32)
        turned = full.T

        def column(index):
            return full[:, NR + index : NR + index + 1]

        def across(index):
            return turned[NR + index : NR + index + 1, :]

        hit[...] = jnp.where(column(1) == lane_row, 1.0, 0.0).astype(bf16)
        cutb[...] = jnp.broadcast_to(column(3) + column(4), (UNIT, LANES))
        atom_hit = column(2) == lane_atom
        atom_one = jnp.where(atom_hit, 1.0, 0.0).astype(bf16)
        for block in range(7):
            cols = slice(block * ROWS, (block + 1) * ROWS)
            gath[:, cols] = dot_nn(hit[...], tab[b, :, cols])
        for block in range(5):
            cols = slice(block * ROWS, (block + 1) * ROWS)
            per_atom[:, cols] = dot_nn(atom_one, atom_tab[:, cols])
        along = jnp.concatenate(
            [jnp.where(atom_hit, column(5 + axis), 0.0).astype(bf16) for axis in range(3)],
            axis=1,
        )
        per_atom[:, 5 * ROWS :] = dot_nn(along, dir_tab[...])
        for block in range(4):
            cols = slice(block * ROWS, (block + 1) * ROWS)
            filt[:, cols] = dot_nn(low, wd[:, cols])

        def part(ref, block, here, half):
            start = block * ROWS + half * LANES
            return ref[here, start : start + LANES]

        def gate(here, block, half):
            value = part(filt, block, here, half)
            lift = 1.0 + jnp.tanh(value)
            return lift, value * lift

        def first_stage(step, carry):
            here = pl.ds(pl.multiple_of(step * 16, 16), 16)
            there = pl.ds(pl.multiple_of(UNIT + step * 16, 16), 16)
            for half in range(2):
                cols = slice(half * LANES, (half + 1) * LANES)
                silu_k = gate(here, 0, half)[1]
                silu_x = gate(here, 1, half)[1]
                score = part(per_atom, 0, here, half) * part(gath, 0, here, half) * silu_k
                back = part(per_atom, 1, here, half) * part(gath, 1, here, half) * silu_x
                pair[here, cols] = score.astype(bf16)
                pair[there, cols] = back.astype(bf16)
            return carry

        lax.fori_loop(0, UNIT // 16, first_stage, 0, unroll=2)
        pair_sum[...] = dot_nn(pair[...], heads[...])

        def second_stage(step, carry):
            here = pl.ds(pl.multiple_of(step * 16, 16), 16)
            there = pl.ds(pl.multiple_of(UNIT + step * 16, 16), 16)
            cut = cutb[here, :]
            for half in range(2):
                cols = slice(half * LANES, (half + 1) * LANES)

                def put(ref, block, value):
                    start = block * ROWS + half * LANES
                    ref[here, start : start + LANES] = value.astype(bf16)

                half_score = pair_sum[here, cols]
                lift = 1.0 + jnp.tanh(half_score)
                silu_s = half_score * lift
                attention = silu_s * cut
                dscore = pair_sum[there, cols] * cut * (lift + silu_s * (2.0 - lift))

                query_e = part(per_atom, 0, here, half)
                key_e = part(gath, 0, here, half)
                lift, silu = gate(here, 0, half)
                scaled = dscore * query_e
                put(dedge, 0, scaled * silu)
                put(dfilt, 0, scaled * key_e * (lift + silu * (2.0 - lift)))
                put(msg, 4, dscore * key_e * silu)

                value_e = part(gath, 1, here, half)
                lift, silu = gate(here, 1, half)
                down = part(per_atom, 1, here, half) * attention
                put(dedge, 1, down * silu)
                put(dfilt, 1, down * value_e * (lift + silu * (2.0 - lift)))
                put(msg, 0, value_e * silu * attention)

                value_e = part(gath, 2, here, half)
                lift, silu = gate(here, 2, half)
                gated = value_e * silu
                down = jnp.zeros_like(gated)
                for axis in range(3):
                    vec_e = part(gath, 4 + axis, here, half)
                    cot_e = part(per_atom, 2 + axis, here, half)
                    down += cot_e * vec_e
                    put(msg, 1 + axis, vec_e * gated)
                    put(dedge, 4 + axis, cot_e * gated)
                put(dedge, 2, down * silu)
                put(dfilt, 2, down * value_e * (lift + silu * (2.0 - lift)))

                value_e = part(gath, 3, here, half)
                lift, silu = gate(here, 3, half)
                down = part(per_atom, 5, here, half)
                put(dedge, 3, down * silu)
                put(dfilt, 3, down * value_e * (lift + silu * (2.0 - lift)))
                put(msg, 5, value_e * silu)
            return carry

        lax.fori_loop(0, UNIT // 16, second_stage, 0, unroll=2)

        hit_t = jnp.where(across(1) == sub_row, 1.0, 0.0).astype(bf16)
        for block in range(7):
            cols = slice(block * ROWS, (block + 1) * ROWS)
            acc[b, :, cols] += dot_nn(hit_t, dedge[:, cols])
        atom_hit_t = across(2) == sub_atom
        atom_one_t = jnp.where(atom_hit_t, 1.0, 0.0).astype(bf16)
        for block in (0, 4):
            cols = slice(block * ROWS, (block + 1) * ROWS)
            agg[:, cols] += dot_nn(atom_one_t, msg[:, cols])
        for axis in range(3):
            cols = slice((1 + axis) * ROWS, (2 + axis) * ROWS)
            along_t = jnp.where(atom_hit_t, across(5 + axis), 0.0).astype(bf16)
            agg[:, cols] += dot_nn(atom_one_t, msg[:, cols]) + dot_nn(
                along_t, msg[:, 5 * ROWS :]
            )
        feats_t = turned.astype(bf16)
        for block in range(4):
            cols = slice(block * ROWS, (block + 1) * ROWS)
            gwd[:, cols] += dot_nn(feats_t, dfilt[:, cols])
        return carry

    first = jnp.int32(0)
    for b in range(buckets):
        number = units_ref[micro, b]
        lax.fori_loop(0, number, partial(unit_body, b, first), 0)
        first = first + number

    agg_low = agg[:, 0:ROWS].astype(bf16)
    outs = [dot_nn(agg_low, wb[W_O + part]) + vector(7 + part) for part in range(3)]
    outx_ref[...] = x_ref[0] + (vec_dot * outs[1] + outs[2]) * live
    g_dot = cot_x * outs[1]
    for axis in range(3):
        rows = parts[axis]
        vec_agg = agg[:, (1 + axis) * ROWS : (2 + axis) * ROWS]
        outv_ref[axis] = vec_ref[0, axis] + (proj[2, rows, :] * outs[0] + vec_agg) * live
        proj[2, rows, :] = cotv_ref[0, axis] * live * outs[0]
        held = proj[0, rows, :]
        proj[0, rows, :] = g_dot * proj[1, rows, :]
        proj[1, rows, :] = g_dot * held

    gm_sum = wide_w if has_prior else gm_ref

    def put_grad(first, stride, column, rows, value):
        for half in range(2):
            at = pl.ds(first + 2 * column + half, rows, stride=stride)
            gm_sum[at, :] = value[:, half * LANES : (half + 1) * LANES]

    def put_vector(index, value):
        for half in range(2):
            row = 2 * index + half
            gv_ref[row : row + 1, :] = value[:, half * LANES : (half + 1) * LANES]

    def column_sum(value):
        return jnp.sum(value.astype(f32), axis=0, keepdims=True)

    put_vector(0, jnp.zeros((1, ROWS), f32))
    put_vector(1, jnp.zeros((1, ROWS), f32))
    g_vec = jnp.zeros((3 * atoms, feat_width), f32)
    for part in range(3):
        put_grad(O_AT, 6, part, ROWS, dot_tn(agg_low, go[part]))
        put_vector(7 + part, column_sum(go[part]))
        gp = proj[part].astype(bf16)
        put_grad(VEC_AT, 6, part, ROWS, dot_tn(vec_low, gp))
        g_vec += dot_nt(gp, wb[W_VEC + part])

    g_query = agg[:, 4 * ROWS : 5 * ROWS].astype(bf16)
    put_grad(Q_AT, 2, 0, ROWS, dot_tn(norm_table[0:atoms, :], g_query))
    put_vector(2, column_sum(g_query))
    g_norm = dot_nt(g_query, wb[W_Q])

    sums = [jnp.zeros((ROWS, ROWS), f32) for column in range(4)]
    biases = [jnp.zeros((1, ROWS), f32) for column in range(4)]
    for b in range(buckets):
        rows = slice(b * ROWS, (b + 1) * ROWS)
        g_table = jnp.zeros((ROWS, ROWS), f32)
        for column in range(4):
            low = acc[b, :, column * ROWS : (column + 1) * ROWS].astype(bf16)
            sums[column] += dot_tn(norm_table[rows, :], low)
            biases[column] += column_sum(low)
            g_table += dot_nt(low, wb[W_K + column])
        for half in range(2):
            domain = 2 * b + half
            if domain >= domains:
                continue
            here = slice(half * atoms, (half + 1) * atoms)
            if domain == 0:
                gown_ref[0] = g_table[here, :] + g_norm
            else:
                back_refs[domain - 1][0] = g_table[here, :].astype(bf16)
            for axis in range(3):
                block = acc[b, here, (4 + axis) * ROWS : (5 + axis) * ROWS]
                if domain == 0:
                    gown_ref[1 + axis] = block + g_vec[parts[axis], :]
                else:
                    back_refs[domain - 1][1 + axis] = block.astype(bf16)
    for column in range(4):
        if column == 0:
            put_grad(K_AT, 2, 0, ROWS, sums[column])
        else:
            put_grad(V_AT, 6, column - 1, ROWS, sums[column])
        put_vector(3 + column, biases[column])
        cols = slice(column * ROWS, (column + 1) * ROWS)
        block = gwd[0:NR, cols] * 0.5
        if column == 0:
            put_grad(DK_AT, 2, 0, NR, block)
        else:
            put_grad(DV_AT, 6, column - 1, NR, block)
        put_vector(10 + column, gwd[NR : NR + 1, cols] * 0.5)
    if has_prior:
        for cell in range(cells):
            for part in range(parts_w):
                start = (cell * parts_w + part) * quarter
                rows = slice(start, start + quarter)
                gm_ref[part, cell] = (gm_sum[rows, :] + prior_m_ref[rows, :]).astype(bf16)
        gv_ref[...] += prior_v_ref[...]


def core_mate(depth_at):
    return depth_at + 1 - 2 * (depth_at % 2)


def chip_mate(depth_at):
    return (depth_at + 2) % 4


def greet(cells, depth):
    barrier = pltpu.get_barrier_semaphore()
    cell_at, depth_at = lax.axis_index("cells"), lax.axis_index("depth")
    for by in range(1, cells):
        pl.semaphore_signal(barrier, inc=1, device_id={"cells": (cell_at + by) % cells})
    for by in range(1, depth):
        pl.semaphore_signal(barrier, inc=1, device_id={"depth": (depth_at + by) % depth})
    pl.semaphore_wait(barrier, cells + depth - 2)


def remote(source, target, send, receive, device):
    return pltpu.make_async_remote_copy(
        src_ref=source, dst_ref=target, send_sem=send, recv_sem=receive, device_id=device
    )


def fetch_kernel(cells, depth, micros, sources, faces, *refs):
    own_refs = refs[:micros]
    lists_ref, w_ref, v_ref = refs[micros : micros + 3]
    refs = refs[micros + 3 :]
    halo_refs = refs[: micros * len(sources)]
    got_lists, got_w, got_v = refs[micros * len(sources) : micros * len(sources) + 3]
    halo_send, halo_recv, list_send, list_recv, v_send, v_recv, w_send, w_recv = refs[
        micros * len(sources) + 3 :
    ]
    cell_at, depth_at = lax.axis_index("cells"), lax.axis_index("depth")
    sizes = {"cells": cells, "depth": depth}
    places = {"cells": cell_at, "depth": depth_at}
    got_w[cell_at] = w_ref[...]
    got_v[cell_at] = v_ref[...]
    greet(cells, depth)

    def ahead(axis, by):
        return {axis: (places[axis] + by) % sizes[axis]}

    started = []

    def start(*args):
        copy = remote(*args)
        copy.start()
        started.append(copy)
        return copy

    first = []
    for by in range(1, cells):
        there = ahead("cells", by)
        first.append(
            start(
                w_ref.at[depth_at],
                got_w.at[cell_at, depth_at],
                w_send.at[0, by],
                w_recv.at[0, by],
                there,
            )
        )
    lists = [
        start(
            lists_ref.at[face],
            got_lists.at[face],
            list_send.at[face],
            list_recv.at[face],
            ahead(axis, by),
        )
        for face, (axis, by) in enumerate(faces)
    ]
    vectors = [
        start(v_ref, got_v.at[cell_at], v_send.at[by], v_recv.at[by], ahead("cells", by))
        for by in range(1, cells)
    ]
    halos = []
    for micro in range(micros):
        for index, (axis, by) in enumerate(sources):
            halos.append(
                start(
                    own_refs[micro],
                    halo_refs[micro * len(sources) + index],
                    halo_send.at[micro, index],
                    halo_recv.at[micro, index],
                    ahead(axis, by),
                )
            )
    mate, other = core_mate(depth_at), chip_mate(depth_at)
    across = []
    last = []
    for by in range(1, cells):
        first[by - 1].wait_recv()
        piece = got_w.at[(cell_at + cells - by) % cells, depth_at]
        across.append(
            start(piece, piece, w_send.at[1, by], w_recv.at[1, by], {"depth": other})
        )
        last.append(start(piece, piece, w_send.at[2, by], w_recv.at[2, by], {"depth": mate}))
    for by in range(1, cells):
        across[by - 1].wait_recv()
        piece = got_w.at[(cell_at + cells - by) % cells, other]
        last.append(start(piece, piece, w_send.at[3, by], w_recv.at[3, by], {"depth": mate}))
    for copy in lists + vectors + last + halos:
        copy.wait_recv()
    for copy in started:
        copy.wait_send()


def close_kernel(cells, depth, micros, sources, *refs):
    x_ref, cotx_ref, cotv_ref, gain_ref, gvec_in, part_ref = refs[:6]
    refs = refs[6:]
    gown_refs = refs[:micros]
    back_refs = refs[micros : micros + micros * len(sources)]
    refs = refs[micros + micros * len(sources) :]
    gx_ref, gvec_ref, summ_ref, sumv_ref = refs[:4]
    came, one_in, two_out, two_in, three_out, three_in, held, quad, octo = refs[4:13]
    halo_send, halo_recv, m_send, m_recv, c_send, c_recv, d_send, d_recv, e_send, e_recv, f_send, f_recv = refs[13:]
    cell_at, depth_at = lax.axis_index("cells"), lax.axis_index("depth")
    sizes = {"cells": cells, "depth": depth}
    places = {"cells": cell_at, "depth": depth_at}
    greet(cells, depth)

    def ahead(axis, by):
        return {axis: (places[axis] + by) % sizes[axis]}

    started = []

    def start(*args):
        copy = remote(*args)
        copy.start()
        started.append(copy)
        return copy

    mate, other = core_mate(depth_at), chip_mate(depth_at)
    mate_other = chip_mate(mate)
    one_far = start(
        part_ref.at[mate_other], one_in.at[1], m_send.at[0], m_recv.at[0], {"depth": mate}
    )
    one_near = start(part_ref.at[mate], one_in.at[0], m_send.at[1], m_recv.at[1], {"depth": mate})
    halos = []
    for micro in range(micros):
        for index, (axis, by) in enumerate(sources):
            halos.append(
                start(
                    back_refs[micro * len(sources) + index],
                    came.at[micro, index],
                    halo_send.at[micro, index],
                    halo_recv.at[micro, index],
                    ahead(axis, -by),
                )
            )
    one_far.wait_recv()
    two_out[...] = (part_ref[other].astype(f32) + one_in[1].astype(f32)).astype(bf16)
    two = start(two_out, two_in, m_send.at[2], m_recv.at[2], {"depth": other})
    one_near.wait_recv()
    two.wait_recv()
    for cell in range(cells):
        total = (
            part_ref[depth_at, cell].astype(f32)
            + one_in[0, cell].astype(f32)
            + two_in[cell].astype(f32)
        )
        three_out[cell] = total.astype(bf16)
    three = []
    for by in range(1, cells):
        there = (cell_at + by) % cells
        three.append(
            start(
                three_out.at[there],
                three_in.at[by],
                c_send.at[by],
                c_recv.at[by],
                {"cells": there},
            )
        )

    for copy in halos:
        copy.wait_recv()
    gain = jnp.concatenate([gain_ref[half : half + 1, :].astype(f32) for half in range(2)], axis=1)
    norm_grads = [jnp.zeros((1, gain.shape[1]), f32) for part in range(2)]
    for micro in range(micros):
        total = [gown_refs[micro][part] for part in range(4)]
        for index in range(len(sources)):
            for part in range(4):
                total[part] = total[part] + came[micro, index, part].astype(f32)
        hat, spread = normalise(x_ref[micro])
        norm_grads[0] += jnp.sum(total[0] * hat, axis=0, keepdims=True)
        norm_grads[1] += jnp.sum(total[0], axis=0, keepdims=True)
        g_hat = total[0] * gain
        g_x = spread * (g_hat - lane_mean(g_hat) - hat * lane_mean(g_hat * hat))
        gx_ref[micro] = cotx_ref[micro] + g_x
        for axis in range(3):
            gvec_ref[micro, axis] = cotv_ref[micro, axis] + total[1 + axis]
    held[...] = gvec_in[...]
    for part in range(2):
        for half in range(2):
            row = 2 * part + half
            held[row : row + 1, :] = norm_grads[part][:, half * LANES : (half + 1) * LANES]
    quad[depth_at] = held[...]
    four = [
        start(held, quad.at[depth_at], d_send.at[by], d_recv.at[by], ahead("depth", by))
        for by in range(1, depth)
    ]

    for copy in three:
        copy.wait_recv()
    final = three_out[cell_at].astype(f32)
    for by in range(1, cells):
        final = final + three_in[by].astype(f32)
    summ_ref[depth_at] = final
    share = [
        start(
            summ_ref.at[depth_at],
            summ_ref.at[depth_at],
            e_send.at[by],
            e_recv.at[by],
            ahead("depth", by),
        )
        for by in range(1, depth)
    ]
    for copy in four:
        copy.wait_recv()
    total = quad[0]
    for at in range(1, depth):
        total = total + quad[at]
    octo[cell_at] = total
    eight = [
        start(
            octo.at[cell_at],
            octo.at[cell_at],
            f_send.at[by],
            f_recv.at[by],
            ahead("cells", by),
        )
        for by in range(1, cells)
    ]
    for copy in eight:
        copy.wait_recv()
    total = octo[0]
    for cell in range(1, cells):
        total = total + octo[cell]
    sumv_ref[...] = total
    for copy in share:
        copy.wait_recv()
    for copy in started:
        copy.wait_send()


def adam_update(weight, grad, first, second):
    first_new = beta_one * first + (1.0 - beta_one) * grad
    second_new = beta_two * second + (1.0 - beta_two) * grad * grad
    first_hat = first_new / (1.0 - beta_one**STEP)
    second_hat = second_new / (1.0 - beta_two**STEP)
    weight_new = weight - learn_rate * (
        first_hat / (jnp.sqrt(second_hat) + adam_eps) + decay_rate * weight
    )
    return (weight_new, first_new, second_new)


def micro_block(shape, micro):
    rest = tuple(shape[1:])
    zeros = (0,) * len(rest)
    return pl.BlockSpec((1,) + rest, lambda i: (micro,) + zeros)


def shards(
    x_in,
    vec_in,
    cot_x,
    cot_vec,
    mats,
    vecs,
    mats_first,
    mats_second,
    vecs_first,
    vecs_second,
    atom_count,
    neighbours,
    edge_mask,
    edge_vec,
    send_list,
):
    micros, atoms, width = x_in.shape
    slots = neighbours.shape[1]
    halo = send_list.shape[-1]
    per_face = halo // LANES
    cells, depth = lax.axis_size("cells"), lax.axis_size("depth")
    faces = [("cells", 1), ("cells", -1), ("cells", FOLD), ("cells", -FOLD), ("depth", 1), ("depth", -1)]
    sizes = {"cells": cells, "depth": depth}
    sources = []
    face_source = []
    for axis, by in faces:
        key = (axis, by % sizes[axis])
        if key not in sources:
            sources.append(key)
        face_source.append(sources.index(key))
    domains = 1 + len(sources)
    buckets = (domains * atoms + ROWS - 1) // ROWS
    block_of = [1 + face_source[row // per_face] for row in range(6 * per_face)]

    whole = pl.BlockSpec(memory_space=pltpu.VMEM)
    scalars = pl.BlockSpec(memory_space=pltpu.SMEM)

    any_space = pl.BlockSpec(memory_space=pl.ANY)
    count = len(sources)
    quarter = mats.shape[0] // LANES // depth
    v_rows = -(-vecs.shape[0] // LANES)
    v_low = jnp.pad(vecs.astype(bf16), (0, v_rows * LANES - vecs.shape[0])).reshape(v_rows, LANES)
    faces_first = jnp.moveaxis(
        send_list.reshape(micros, 6, per_face, LANES), 1, 0
    ).reshape(6, micros * per_face, LANES)

    *own, w_low = pl.pallas_call(
        norm_kernel,
        out_shape=tuple(
            jax.ShapeDtypeStruct((4, atoms, width), bf16) for micro in range(micros)
        )
        + (jax.ShapeDtypeStruct((depth, quarter, LANES), bf16),),
        in_specs=[whole] * 3,
        out_specs=[whole] * (micros + 1),
        name="norm",
    )(x_in, vec_in, mats.reshape(-1, LANES))

    dma = pltpu.SemaphoreType.DMA
    fetched = pl.pallas_call(
        partial(fetch_kernel, cells, depth, micros, sources, faces),
        out_shape=tuple(
            [jax.ShapeDtypeStruct((4, atoms, width), bf16)] * (micros * count)
            + [
                jax.ShapeDtypeStruct(faces_first.shape, i32),
                jax.ShapeDtypeStruct((cells, depth, quarter, LANES), bf16),
                jax.ShapeDtypeStruct((cells, v_rows, LANES), bf16),
            ]
        ),
        in_specs=[any_space] * micros + [whole] * 3,
        out_specs=[any_space] * (micros * count) + [whole] * 3,
        scratch_shapes=[
            dma((micros, count)),
            dma((micros, count)),
            dma((6,)),
            dma((6,)),
            dma((cells,)),
            dma((cells,)),
            dma((4, cells)),
            dma((4, cells)),
        ],
        compiler_params=pltpu.CompilerParams(
            collective_id=0, has_side_effects=True, vmem_limit_bytes=VMEM_LIMIT
        ),
        name="fetch",
    )(*own, faces_first, w_low, v_low)
    halos = [fetched[micro * count : (micro + 1) * count] for micro in range(micros)]
    got_lists, w_all, v_all = fetched[micros * count :]
    list_rows = jnp.moveaxis(
        got_lists.reshape(6, micros, per_face, LANES), 1, 0
    ).reshape(micros, 6 * per_face, LANES)
    v_all = v_all.reshape(cells, v_rows * LANES)[:, : vecs.shape[0]].reshape(-1, LANES)
    w_rows, v_rows = cells * depth * quarter, v_all.shape[0]

    limit = slots * atoms + buckets * (slots // BLOCK_SLOTS) * 8 + buckets * UNIT
    capacity = (limit + UNIT - 1) // UNIT * UNIT

    def by_micro(shape):
        zeros = (0,) * (len(shape) - 1)
        return pl.BlockSpec((1,) + tuple(shape[1:]), lambda i: (i,) + zeros)

    edge_table, units = pl.pallas_call(
        partial(prep_kernel, block_of, buckets),
        out_shape=(
            jax.ShapeDtypeStruct((micros, capacity, LANES), bf16),
            jax.ShapeDtypeStruct((micros, buckets), i32),
        ),
        grid=(micros,),
        in_specs=[
            by_micro(neighbours.shape),
            by_micro(edge_mask.shape),
            by_micro(edge_vec.shape),
            by_micro(list_rows.shape),
        ],
        out_specs=[by_micro((micros, capacity, LANES)), scalars],
        scratch_shapes=[
            pltpu.VMEM((slots, LANES, LANES), bf16),
            pltpu.VMEM((slots, atoms), i32),
            pltpu.VMEM((slots // BLOCK_SLOTS, LANES), i32),
            pltpu.SMEM((slots // BLOCK_SLOTS, LANES), i32),
            pltpu.VMEM((capacity + UNIT, LANES), f32),
            pltpu.SemaphoreType.DMA(()),
        ],
        compiler_params=pltpu.CompilerParams(vmem_limit_bytes=VMEM_LIMIT),
        name="prep",
    )(neighbours, edge_mask, edge_vec, list_rows)

    grads = []
    outs = []
    for micro in range(micros):
        prior = list(grads)
        operands = [
            units,
            atom_count,
            edge_table,
            x_in,
            vec_in,
            cot_x,
            cot_vec,
            own[micro],
            *halos[micro],
            w_all,
            v_all,
            *prior,
        ]
        specs = (
            [scalars, scalars]
            + [
                micro_block(array.shape, micro)
                for array in (edge_table, x_in, vec_in, cot_x, cot_vec)
            ]
            + [whole] * (1 + len(sources) + 2 + len(prior))
        )
        shapes = (
            [
                jax.ShapeDtypeStruct((atoms, width), f32),
                jax.ShapeDtypeStruct((3, atoms, width), f32),
                jax.ShapeDtypeStruct((4, atoms, width), f32),
            ]
            + [jax.ShapeDtypeStruct((4, atoms, width), bf16)] * len(sources)
            + [
                jax.ShapeDtypeStruct((depth, cells, quarter, LANES), bf16)
                if prior
                else jax.ShapeDtypeStruct((w_rows, LANES), f32),
                jax.ShapeDtypeStruct((v_rows, LANES), f32),
            ]
        )
        results = pl.pallas_call(
            partial(edge_kernel, micro, domains, buckets, atoms, width, bool(prior)),
            out_shape=tuple(shapes),
            grid=(1,),
            in_specs=specs,
            out_specs=[whole] * len(shapes),
            scratch_shapes=[
                pltpu.VMEM((w_rows, LANES), f32),
                pltpu.VMEM((11, ROWS, ROWS), bf16),
                pltpu.VMEM((LANES, 4 * ROWS), bf16),
                pltpu.VMEM((buckets * ROWS, ROWS), bf16),
                pltpu.VMEM((buckets, ROWS, 7 * ROWS), bf16),
                pltpu.VMEM((buckets, ROWS, 7 * ROWS), f32),
                pltpu.VMEM((atoms, 5 * ROWS), bf16),
                pltpu.VMEM((3 * atoms, ROWS), bf16),
                pltpu.VMEM((3, 3 * atoms, ROWS), f32),
                pltpu.VMEM((3, atoms, ROWS), bf16),
                pltpu.VMEM((atoms, 5 * ROWS), f32),
                pltpu.VMEM((LANES, 4 * ROWS), f32),
                pltpu.VMEM((ROWS, ROWS), bf16),
                pltpu.VMEM((UNIT, ROWS), bf16),
                pltpu.VMEM((UNIT, 7 * ROWS), f32),
                pltpu.VMEM((UNIT, 6 * ROWS), f32),
                pltpu.VMEM((UNIT, 4 * ROWS), f32),
                pltpu.VMEM((UNIT, LANES), f32),
                pltpu.VMEM((2 * UNIT, ROWS), bf16),
                pltpu.VMEM((2 * UNIT, ROWS), f32),
                pltpu.VMEM((UNIT, 7 * ROWS), bf16),
                pltpu.VMEM((UNIT, 4 * ROWS), bf16),
                pltpu.VMEM((UNIT, 6 * ROWS), bf16),
            ],
            compiler_params=pltpu.CompilerParams(vmem_limit_bytes=VMEM_LIMIT),
            name="edges",
        )(*operands)
        outs.append(results)
        grads = list(results[-2:])

    part_m, part_v = grads
    grad_x, grad_vec, sum_mats, sum_vecs = pl.pallas_call(
        partial(close_kernel, cells, depth, micros, sources),
        out_shape=(
            jax.ShapeDtypeStruct(x_in.shape, f32),
            jax.ShapeDtypeStruct(vec_in.shape, f32),
            jax.ShapeDtypeStruct((depth, quarter, LANES), f32),
            jax.ShapeDtypeStruct((v_rows, LANES), f32),
        ),
        in_specs=[whole] * (6 + micros) + [any_space] * (micros * count),
        out_specs=[whole] * 4,
        scratch_shapes=[
            pltpu.VMEM((micros, count, 4, atoms, width), bf16),
            pltpu.VMEM((2, cells, quarter, LANES), bf16),
            pltpu.VMEM((cells, quarter, LANES), bf16),
            pltpu.VMEM((cells, quarter, LANES), bf16),
            pltpu.VMEM((cells, quarter, LANES), bf16),
            pltpu.VMEM((cells, quarter, LANES), bf16),
            pltpu.VMEM((v_rows, LANES), f32),
            pltpu.VMEM((depth, v_rows, LANES), f32),
            pltpu.VMEM((cells, v_rows, LANES), f32),
            dma((micros, count)),
            dma((micros, count)),
            dma((3,)),
            dma((3,)),
            dma((cells,)),
            dma((cells,)),
            dma((depth,)),
            dma((depth,)),
            dma((depth,)),
            dma((depth,)),
            dma((cells,)),
            dma((cells,)),
        ],
        compiler_params=pltpu.CompilerParams(
            collective_id=1, has_side_effects=True, vmem_limit_bytes=VMEM_LIMIT
        ),
        name="close",
    )(
        x_in,
        cot_x,
        cot_vec,
        v_all,
        part_v,
        part_m,
        *[result[2] for result in outs],
        *[block for result in outs for block in result[3 : 3 + count]],
    )
    sum_mats = sum_mats.reshape(-1)
    sum_vecs = lax.dynamic_slice_in_dim(
        sum_vecs.reshape(-1), lax.axis_index("cells") * vecs.shape[0], vecs.shape[0]
    )
    new_mats, mats_one, mats_two = adam_update(mats, sum_mats, mats_first, mats_second)
    new_vecs, vecs_one, vecs_two = adam_update(vecs, sum_vecs, vecs_first, vecs_second)
    return (
        jnp.stack([result[0] for result in outs]),
        jnp.stack([result[1] for result in outs]),
        grad_x,
        grad_vec,
        sum_mats,
        sum_vecs,
        new_mats,
        new_vecs,
        mats_one,
        mats_two,
        vecs_one,
        vecs_two,
    )


def solution(mesh):
    by_atom = ("cells", "depth")
    shard = P("cells")
    in_specs = (
        P(None, by_atom, None),
        P(None, None, by_atom, None),
        P(None, by_atom, None),
        P(None, None, by_atom, None),
        shard,
        shard,
        shard,
        shard,
        shard,
        shard,
        P(None, by_atom),
        P(None, None, by_atom),
        P(None, None, by_atom),
        P(None, None, None, by_atom),
        P(None, by_atom, None),
    )
    out_specs = (
        P(None, by_atom, None),
        P(None, None, by_atom, None),
        P(None, by_atom, None),
        P(None, None, by_atom, None),
    ) + (shard,) * 8
    return jax.shard_map(shards, mesh=mesh, in_specs=in_specs, out_specs=out_specs, check_vma=False)
```

```python
from functools import partial
import math

import jax
import jax.numpy as jnp
from jax import lax
from jax.experimental import pallas as pl
from jax.experimental.pallas import tpu as pltpu
from jax.sharding import PartitionSpec as P

HEADS = 8
NR = 32
FOLD = 4
STEP = 3

LANES = 128
ROWS = 256
UNIT = 256
BLOCK_SLOTS = 4
TILE = 192

norm_eps = 1e-05
cut_radius = 5.0
beta_one = 0.5
beta_two = 0.5
learn_rate = 0.05
decay_rate = 0.01
adam_eps = 1e-08

f32 = jnp.float32
bf16 = jnp.bfloat16
i32 = jnp.int32

VMEM_LIMIT = 60 * 1024 * 1024


def dot_nn(left, right):
    return lax.dot_general(left, right, (((1,), (0,)), ((), ())), preferred_element_type=f32)


def dot_nt(left, right):
    return lax.dot_general(left, right, (((1,), (1,)), ((), ())), preferred_element_type=f32)


def dot_tn(left, right):
    return lax.dot_general(left, right, (((0,), (0,)), ((), ())), preferred_element_type=f32)


def lane_mean(block):
    return jnp.sum(block, axis=-1, keepdims=True) * (1.0 / block.shape[-1])


def normalise(block):
    centered = block - lane_mean(block)
    spread = lax.rsqrt(lane_mean(centered * centered) + norm_eps)
    return centered * spread, spread


def norm_kernel(x_ref, vec_ref, mats_ref, own_ref, low_ref):
    quarter = low_ref.shape[1]
    for part in range(low_ref.shape[0]):
        low_ref[part] = mats_ref[part * quarter : (part + 1) * quarter, :].astype(bf16)
    for micro in range(x_ref.shape[0]):
        own_ref[micro, 0] = normalise(x_ref[micro])[0].astype(bf16)
        own_ref[micro, 1:] = vec_ref[micro].astype(bf16)


Q_AT, K_AT, V_AT, VEC_AT, O_AT, DK_AT, DV_AT = 0, 512, 1024, 2560, 4096, 5632, 5696
W_Q, W_K, W_V, W_VEC, W_O = 0, 1, 2, 5, 8
FEATS = 48
CHUNK = 16
GATH, PER_ATOM, FILT, SUMS, KEPT, WORK = 0, 7, 12, 16, 18, 24


def edge_features(nbr, mask, geom, lists, block_of, buckets, feat, place, count_vec):
    slots, atoms = nbr.shape
    blocks = slots // BLOCK_SLOTS
    live = mask > 0
    halo_at = nbr - atoms
    list_row = halo_at >> 7
    list_lane = halo_at & (LANES - 1)
    atom_in = nbr
    block_id = jnp.zeros_like(nbr)
    for row in range(lists.shape[0]):
        table = jnp.broadcast_to(lists[row : row + 1, :], (slots, atoms))
        picked = jnp.take_along_axis(table, list_lane, axis=1)
        here = list_row == row
        atom_in = jnp.where(here, picked, atom_in)
        block_id = jnp.where(here, block_of[row], block_id)
    entry = block_id * atoms + atom_in
    bucket = entry >> 8
    low = ((entry & (ROWS - 1)) + 1).astype(f32)
    atom_id = (lax.broadcasted_iota(i32, (slots, atoms), 1) + 1).astype(f32)
    live_float = live.astype(f32)

    radius = jnp.sqrt(geom[0] * geom[0] + geom[1] * geom[1] + geom[2] * geom[2])
    units = [comp / radius for comp in geom]
    cut = 0.5 * (jnp.cos(math.pi * radius / cut_radius) + 1.0) * live_float
    cut_high = cut.astype(bf16).astype(f32)
    cut_low = cut - cut_high
    decayed = jnp.exp(-(5.0 / cut_radius) * radius)
    start_value = math.exp(-cut_radius)
    ramp = lax.broadcasted_iota(i32, (NR, 1), 0).astype(f32) / float(NR - 1)
    centers = start_value * (1.0 - ramp) + ramp
    width_coef = (2.0 / NR * (1.0 - start_value)) ** (-2)
    extras = [live_float, low, atom_id, cut_high, cut_low] + units
    zeros = jnp.zeros((16 - len(extras), atoms), f32)
    for slot in range(slots):
        gap = decayed[slot : slot + 1, :] - centers
        basis = cut[slot : slot + 1, :] * jnp.exp(-width_coef * gap * gap)
        feat[slot, 0:NR, :] = basis.astype(bf16)
        rows = [extra[slot : slot + 1, :] for extra in extras] + [zeros]
        feat[slot, NR : NR + 16, :] = jnp.concatenate(rows, axis=0).astype(bf16)

    members = [jnp.where(live & (bucket == b), 1.0, 0.0) for b in range(buckets)]
    lane_from = lax.broadcasted_iota(i32, (atoms, 2 * atoms), 0)
    lane_to = lax.broadcasted_iota(i32, (atoms, 2 * atoms), 1)
    before = jnp.where((lane_from < lane_to) | (lane_to >= atoms), 1.0, 0.0).astype(bf16)
    slot_to = lax.broadcasted_iota(i32, (slots, slots), 0)
    slot_from = lax.broadcasted_iota(i32, (slots, slots), 1)
    same = (slot_to // BLOCK_SLOTS) == (slot_from // BLOCK_SLOTS)
    earlier = jnp.where(same & (slot_from < slot_to), 1.0, 0.0).astype(bf16)
    block_row = lax.broadcasted_iota(i32, (blocks, slots), 0)
    block_slot = lax.broadcasted_iota(i32, (blocks, slots), 1)
    gather_block = jnp.where(block_slot // BLOCK_SLOTS == block_row, 1.0, 0.0).astype(bf16)
    lane = lax.broadcasted_iota(i32, (blocks, LANES), 1)
    rank = jnp.zeros((slots, atoms), f32)
    counts = jnp.zeros((blocks, LANES), f32)
    for b in range(buckets):
        sums = dot_nn(members[b].astype(bf16), before)
        row_total = sums[:, atoms:].astype(bf16)
        offset = sums[:, :atoms] + dot_nn(earlier, row_total)
        rank = jnp.where(members[b] > 0.0, offset, rank)
        counts = jnp.where(lane == b, dot_nn(gather_block, row_total), counts)
    place[...] = jnp.where(live, bucket * 1024 + rank.astype(i32), -1)
    count_vec[...] = counts.astype(i32)


def pack_edges(blocks, atoms, buckets, feat, place, count_sc, packed):
    wide = BLOCK_SLOTS * atoms

    def total_body(block, totals):
        return tuple(
            total + (((count_sc[block, b] + 7) >> 3) << 3) for b, total in enumerate(totals)
        )

    totals = lax.fori_loop(0, blocks, total_body, (jnp.int32(0),) * buckets)
    held = [(total + (UNIT - 1)) >> 8 for total in totals]
    bases = [jnp.int32(UNIT)]
    for total in totals:
        bases.append(bases[-1] + (((total + (2 * UNIT - 1)) >> 8) << 8))

    def picks(places, b, first):
        wanted = lax.broadcasted_iota(i32, (TILE, wide), 0) + (b * 1024 + first)
        return jnp.where(places == wanted, 1.0, 0.0).astype(bf16)

    def block_body(block, at):
        first = block * BLOCK_SLOTS
        places = jnp.concatenate(
            [place[pl.ds(first + t, 1), :] for t in range(BLOCK_SLOTS)], axis=1
        )
        feats = jnp.concatenate([feat[first + t] for t in range(BLOCK_SLOTS)], axis=1)
        following = []
        for b in range(buckets):
            number = count_sc[block, b]
            packed[pl.ds(pl.multiple_of(at[b], 8), TILE), :] = dot_nt(picks(places, b, 0), feats)

            @pl.when(number > TILE)
            def _(b=b, number=number):
                def tile_body(tile, carry):
                    feats = jnp.concatenate([feat[first + t] for t in range(BLOCK_SLOTS)], axis=1)
                    pick = picks(places, b, tile * TILE)
                    start = pl.multiple_of(at[b] + tile * TILE, 8)
                    packed[pl.ds(start, TILE), :] = dot_nt(pick, feats)
                    return carry

                lax.fori_loop(1, (number + (TILE - 1)) // TILE, tile_body, 0)

            following.append(at[b] + (((number + 7) >> 3) << 3))
        return tuple(following)

    ends = lax.fori_loop(0, blocks, block_body, tuple(bases[:buckets]))
    zeros = jnp.zeros((UNIT, LANES), f32)
    for end in ends:
        packed[pl.ds(pl.multiple_of(end, 8), UNIT), :] = zeros
    packed[0:UNIT, :] = zeros
    return held, bases


def edge_kernel(domains, buckets, block_of, *refs):
    refs = list(refs)
    count_ref, nbr_ref, mask_ref, geom_ref, list_ref, x_ref, vec_ref, cotx_ref, cotv_ref = refs[:9]
    halo_refs = refs[9 : 9 + domains - 1]
    at = 9 + domains - 1
    w_ref, v_ref = refs[at : at + 2]
    at += 2
    outx_ref, outv_ref, gown_ref = refs[at : at + 3]
    at += 3
    back_refs = refs[at : at + domains - 1]
    at += domains - 1
    gm_ref, gv_ref = refs[at : at + 2]
    at += 2
    (
        feat,
        place,
        count_vec,
        count_sc,
        packed,
        sem,
        wide_w,
        wb,
        wd,
        norm_table,
        tab,
        acc,
        atom_tab,
        proj,
        go,
        agg,
        gwd,
        heads,
    ) = refs[at : at + 18]
    rest = refs[at + 18 :]
    sides = [tuple(rest[side::2]) for side in range(2)]
    micro = pl.program_id(0)
    slots, atoms = nbr_ref.shape[1:]
    feat_width = x_ref.shape[2]
    cells, parts_w, quarter = w_ref.shape[:3]
    parts = [slice(axis * atoms, (axis + 1) * atoms) for axis in range(3)]

    def vector(index):
        both = [v_ref[2 * index + half : 2 * index + half + 1, :].astype(f32) for half in range(2)]
        return jnp.concatenate(both, axis=1)

    @pl.when(micro == 0)
    def _():
        feat[...] = jnp.zeros_like(feat)
        for ref in sides[1][6:]:
            ref[...] = jnp.zeros_like(ref)
        gwd[...] = jnp.zeros_like(gwd)
        for cell in range(cells):
            for part in range(parts_w):
                start = (cell * parts_w + part) * quarter
                wide_w[start : start + quarter, :] = w_ref[cell, part].astype(f32)

        def weight_block(first, stride, column, rows):
            halves = [
                wide_w[pl.ds(first + 2 * column + half, rows, stride=stride), :]
                for half in range(2)
            ]
            return jnp.concatenate(halves, axis=1)

        for slot, first, stride, count in (
            (W_Q, Q_AT, 2, 1),
            (W_K, K_AT, 2, 1),
            (W_V, V_AT, 6, 3),
            (W_VEC, VEC_AT, 6, 3),
            (W_O, O_AT, 6, 3),
        ):
            for column in range(count):
                wb[slot + column] = weight_block(first, stride, column, ROWS).astype(bf16)
        bias_row = lax.broadcasted_iota(i32, (LANES - NR, 1), 0) == 0
        for column in range(4):
            if column == 0:
                block = weight_block(DK_AT, 2, 0, NR)
            else:
                block = weight_block(DV_AT, 6, column - 1, NR)
            bias = jnp.where(bias_row, vector(10 + column), 0.0)
            cols = slice(column * ROWS, (column + 1) * ROWS)
            wd[:, cols] = (jnp.concatenate([block, bias], axis=0) * 0.5).astype(bf16)
        head_from = lax.broadcasted_iota(i32, (ROWS, ROWS), 0) // (feat_width // HEADS)
        head_to = lax.broadcasted_iota(i32, (ROWS, ROWS), 1) // (feat_width // HEADS)
        heads[...] = jnp.where(head_from == head_to, 0.5, 0.0).astype(bf16)

    geom = [geom_ref[0, axis] for axis in range(3)]
    edge_features(
        nbr_ref[0], mask_ref[0], geom, list_ref[0], block_of, buckets, feat, place, count_vec
    )
    copy = pltpu.make_async_copy(count_vec, count_sc, sem)
    copy.start()

    gain = vector(0)
    shift = vector(1)
    own_hat, unused = normalise(x_ref[0])
    vec_low = vec_ref[0].astype(bf16)
    for domain in range(2 * buckets):
        rows = slice(domain * atoms, (domain + 1) * atoms)
        here = slice((domain % 2) * atoms, (domain % 2 + 1) * atoms)
        if domain == 0:
            norm_table[rows, :] = (own_hat * gain + shift).astype(bf16)
        elif domain < domains:
            hat = halo_refs[domain - 1][0, 0].astype(f32)
            norm_table[rows, :] = (hat * gain + shift).astype(bf16)
        else:
            norm_table[rows, :] = jnp.zeros((atoms, feat_width), bf16)
        for axis in range(3):
            cols = slice((4 + axis) * ROWS, (5 + axis) * ROWS)
            if domain < domains:
                block = vec_low[axis] if domain == 0 else halo_refs[domain - 1][0, 1 + axis]
            else:
                block = jnp.zeros((atoms, feat_width), bf16)
            tab[domain // 2, here, cols] = block
    for b in range(buckets):
        rows = slice(b * ROWS, (b + 1) * ROWS)
        for column in range(4):
            cols = slice(column * ROWS, (column + 1) * ROWS)
            made = dot_nn(norm_table[rows, :], wb[W_K + column]) + vector(3 + column)
            tab[b, :, cols] = made.astype(bf16)

    live = (lax.broadcasted_iota(i32, (atoms, 1), 0) < count_ref[micro, 0]).astype(f32)
    query = dot_nn(norm_table[0:atoms, :], wb[W_Q]) + vector(2)
    atom_tab[:, 0:ROWS] = query.astype(bf16)
    vec_rows = vec_low.reshape(3 * atoms, feat_width)
    for part in range(3):
        proj[part] = dot_nn(vec_rows, wb[W_VEC + part])
    cot_x = cotx_ref[0] * live
    vec_dot = jnp.zeros((atoms, feat_width), f32)
    go_one = jnp.zeros((atoms, feat_width), f32)
    for axis in range(3):
        cot_v = cotv_ref[0, axis] * live
        vec_dot += proj[0, parts[axis], :] * proj[1, parts[axis], :]
        go_one += proj[2, parts[axis], :] * cot_v
        atom_tab[:, (2 + axis) * ROWS : (3 + axis) * ROWS] = cot_v.astype(bf16)
    go[0] = go_one.astype(bf16)
    go[1] = (vec_dot * cot_x).astype(bf16)
    go[2] = cot_x.astype(bf16)
    g_agg = dot_nt(go[0], wb[W_O])
    for part in range(1, 3):
        g_agg += dot_nt(go[part], wb[W_O + part])
    atom_tab[:, ROWS : 2 * ROWS] = g_agg.astype(bf16)
    agg[...] = jnp.zeros_like(agg)
    for b in range(buckets):
        acc[b] = jnp.zeros((ROWS, 7 * ROWS), f32)

    copy.wait()
    held, bases = pack_edges(
        slots // BLOCK_SLOTS, atoms, buckets, feat, place, count_sc, packed
    )
    firsts = [jnp.int32(0)]
    for number in held:
        firsts.append(firsts[-1] + number)
    total_units = firsts[-1]

    def bucket_of(unit):
        b = jnp.int32(0)
        for at in range(1, buckets):
            b = b + jnp.where(unit >= firsts[at], 1, 0)
        return b

    def rows_of(unit):
        start = jnp.int32(0)
        for at in range(buckets):
            inside = (unit >= firsts[at]) & (unit < firsts[at + 1])
            start = jnp.where(inside, bases[at] + (unit - firsts[at]) * UNIT, start)
        return pl.ds(pl.multiple_of(start, UNIT), UNIT)

    def block_cols(block):
        return slice(block * ROWS, (block + 1) * ROWS)

    def hits(side, rows):
        hit, atom_one = side[:2]
        full = packed[rows, :]
        lane_row = lax.broadcasted_iota(i32, (UNIT, ROWS), 1).astype(f32) + 1.0
        lane_atom = lax.broadcasted_iota(i32, (UNIT, LANES), 1).astype(f32) + 1.0
        hit[...] = jnp.where(full[:, NR + 1 : NR + 2] == lane_row, 1.0, 0.0).astype(bf16)
        atom_one[...] = jnp.where(full[:, NR + 2 : NR + 3] == lane_atom, 1.0, 0.0).astype(bf16)

    def spread(side, rows):
        cutb, dirs = side[3:5]
        full = packed[rows, :]
        for axis in range(3):
            column = full[:, NR + 5 + axis : NR + 6 + axis]
            dirs[axis] = jnp.broadcast_to(column, (UNIT, LANES))
        column = full[:, NR + 3 : NR + 4] + full[:, NR + 4 : NR + 5]
        cutb[...] = jnp.broadcast_to(column, (UNIT, LANES))

    def gather_steps(side, unit):
        hit, atom_one, work = side[:3]
        b = jnp.minimum(bucket_of(unit), buckets - 1)
        rows = rows_of(unit)

        def gather_table(block):
            work[:, block_cols(GATH + block)] = dot_nn(hit[...], tab[b, :, block_cols(block)])

        def gather_atom(block):
            made = dot_nn(atom_one[...], atom_tab[:, block_cols(block)])
            work[:, block_cols(PER_ATOM + block)] = made

        def filters(block):
            low = packed[rows, :].astype(bf16)
            work[:, block_cols(FILT + block)] = dot_nn(low, wd[:, block_cols(block)])

        return (
            [partial(gather_table, block) for block in range(7)]
            + [partial(gather_atom, block) for block in range(5)]
            + [partial(filters, block) for block in range(4)]
        )

    def mix(first, second):
        done = 0
        for at, step in enumerate(first):
            step()
            until = (at + 1) * len(second) // len(first)
            for other in second[done:until]:
                other()
            done = until

    chunks = [
        (slice(start, start + CHUNK), half)
        for start in range(0, UNIT, CHUNK)
        for half in range(2)
    ]

    def put(ref, block, here, half, value):
        ref[2 * block + half, here, :] = value.astype(bf16)

    def reader(work):
        def part(block, here, half):
            start = block * ROWS + half * LANES
            return work[here, start : start + LANES]

        def gate(here, block, half):
            value = part(FILT + block, here, half)
            turn = jnp.tanh(value)
            lift = 1.0 + turn
            silu = value * lift
            return silu, lift + silu * (1.0 - turn)

        return part, gate

    def heads_stage(side, here, half):
        work, pair = side[2], side[5]
        part, gate = reader(work)

        def keep(block, value):
            start = (KEPT + block) * ROWS + half * LANES
            work[here, start : start + LANES] = value

        there = slice(UNIT + here.start, UNIT + here.stop)
        silu, slope = gate(here, 0, half)
        query_e = part(PER_ATOM, here, half)
        key_e = part(GATH, here, half)
        gated = query_e * silu
        keep(0, gated)
        keep(1, query_e * key_e * slope)
        keep(2, key_e * silu)
        pair[half, here, :] = (gated * key_e).astype(bf16)
        silu, slope = gate(here, 1, half)
        cot_e = part(PER_ATOM + 1, here, half)
        value_e = part(GATH + 1, here, half)
        gated = value_e * silu
        keep(3, cot_e * silu)
        keep(4, cot_e * value_e * slope)
        keep(5, gated)
        pair[half, there, :] = (cot_e * gated).astype(bf16)

    def head_sums(side):
        work, pair = side[2], side[5]
        for at in range(2):
            rows = slice(at * UNIT, (at + 1) * UNIT)
            both = jnp.concatenate([pair[0, rows, :], pair[1, rows, :]], axis=1)
            work[:, block_cols(SUMS + at)] = dot_nn(both, heads[...])

    def vector_stage(side, here, half):
        dirs, dedge, dfilt, msg = side[4], *side[6:]
        part, gate = reader(side[2])
        cots = [part(PER_ATOM + 2 + axis, here, half) for axis in range(3)]
        vecs = [part(GATH + 4 + axis, here, half) for axis in range(3)]
        turns = [dirs[axis, here, :] for axis in range(3)]
        silu, slope = gate(here, 2, half)
        value_e = part(GATH + 2, here, half)
        gated = value_e * silu
        down = cots[0] * vecs[0] + cots[1] * vecs[1] + cots[2] * vecs[2]
        for axis in range(3):
            put(msg, 1 + axis, here, half, vecs[axis] * gated)
            put(dedge, 4 + axis, here, half, cots[axis] * gated)
        put(dedge, 2, here, half, down * silu)
        put(dfilt, 2, here, half, down * value_e * slope)
        silu, slope = gate(here, 3, half)
        value_e = part(GATH + 3, here, half)
        down = cots[0] * turns[0] + cots[1] * turns[1] + cots[2] * turns[2]
        put(dedge, 3, here, half, down * silu)
        put(dfilt, 3, here, half, down * value_e * slope)
        put(msg, 5, here, half, value_e * silu)

    def score_stage(side, here, half):
        cutb, dedge, dfilt, msg = side[3], *side[6:]
        part, unused = reader(side[2])
        cut = cutb[here, :]
        score = part(SUMS, here, half)
        turn = jnp.tanh(score)
        lift = 1.0 + turn
        silu = score * lift
        attention = silu * cut
        dscore = part(SUMS + 1, here, half) * cut * (lift + silu * (1.0 - turn))
        put(dedge, 0, here, half, dscore * part(KEPT, here, half))
        put(dfilt, 0, here, half, dscore * part(KEPT + 1, here, half))
        put(msg, 4, here, half, dscore * part(KEPT + 2, here, half))
        put(dedge, 1, here, half, attention * part(KEPT + 3, here, half))
        put(dfilt, 1, here, half, attention * part(KEPT + 4, here, half))
        put(msg, 0, here, half, attention * part(KEPT + 5, here, half))

    def both_halves(ref, block):
        return jnp.concatenate([ref[2 * block], ref[2 * block + 1]], axis=1)

    def scatter_steps(side, unit):
        dedge, dfilt, msg = side[6:]
        b = jnp.minimum(bucket_of(unit), buckets - 1)
        turned = packed[rows_of(unit), :].T

        def across(index):
            return turned[NR + index : NR + index + 1, :]

        sub_row = lax.broadcasted_iota(i32, (ROWS, UNIT), 0).astype(f32) + 1.0
        sub_atom = lax.broadcasted_iota(i32, (atoms, UNIT), 0).astype(f32) + 1.0
        hit_t = jnp.where(across(1) == sub_row, 1.0, 0.0).astype(bf16)
        atom_hit = across(2) == sub_atom
        atom_t = jnp.where(atom_hit, 1.0, 0.0).astype(bf16)
        feats_t = turned[0:FEATS, :].astype(bf16)
        turn = both_halves(msg, 5)

        def add_vector(axis):
            along = jnp.where(atom_hit, across(5 + axis), 0.0).astype(bf16)
            agg[:, block_cols(1 + axis)] += dot_nn(
                jnp.concatenate([atom_t, along], axis=1),
                jnp.concatenate([both_halves(msg, 1 + axis), turn], axis=0),
            )

        def add_table(block):
            acc[b, :, block_cols(block)] += dot_nn(hit_t, both_halves(dedge, block))

        def add_filter(block):
            gwd[:, block_cols(block)] += dot_nn(feats_t, both_halves(dfilt, block))

        def add_atom(block):
            agg[:, block_cols(block)] += dot_nn(atom_t, both_halves(msg, block))

        return (
            [partial(add_vector, axis) for axis in range(3)]
            + [partial(add_table, block) for block in (2, 3, 4, 5, 6, 0, 1)]
            + [partial(add_filter, block) for block in (2, 3, 0, 1)]
            + [partial(add_atom, block) for block in (0, 4)]
        )

    def on_chunks(stage, side):
        return [partial(stage, side, here, half) for here, half in chunks]

    hits(sides[0], rows_of(jnp.int32(0)))
    mix(gather_steps(sides[0], jnp.int32(0)), [])

    def pair_body(step, carry):
        for at in range(2):
            unit = 2 * step + at
            mine, other = sides[at], sides[1 - at]

            @pl.when(count_sc[0, 0] >= 0)
            def _(unit=unit, mine=mine, other=other):
                spread(mine, rows_of(unit))
                hits(other, rows_of(unit + 1))
                mix(scatter_steps(other, unit - 1), on_chunks(heads_stage, mine))

            @pl.when(count_sc[0, 0] >= 0)
            def _(unit=unit, mine=mine, other=other):
                head_sums(mine)
                mix(
                    gather_steps(other, unit + 1),
                    [step for two in zip(on_chunks(vector_stage, mine), on_chunks(score_stage, mine)) for step in two],
                )

        return carry

    steps = (total_units + 1) // 2
    lax.fori_loop(0, steps, pair_body, 0)
    mix(scatter_steps(sides[1], 2 * steps - 1), [])

    agg_low = agg[:, 0:ROWS].astype(bf16)
    outs = [dot_nn(agg_low, wb[W_O + part]) + vector(7 + part) for part in range(3)]
    outx_ref[0] = x_ref[0] + (vec_dot * outs[1] + outs[2]) * live
    g_dot = cot_x * outs[1]
    for axis in range(3):
        rows = parts[axis]
        vec_agg = agg[:, block_cols(1 + axis)]
        outv_ref[0, axis] = vec_ref[0, axis] + (proj[2, rows, :] * outs[0] + vec_agg) * live
        proj[2, rows, :] = cotv_ref[0, axis] * live * outs[0]
        first_part = proj[0, rows, :]
        proj[0, rows, :] = g_dot * proj[1, rows, :]
        proj[1, rows, :] = g_dot * first_part

    later = micro > 0

    def put_grad(first, stride, column, rows, value):
        for half in range(2):
            at = pl.ds(first + 2 * column + half, rows, stride=stride)
            before = jnp.where(later, wide_w[at, :], 0.0)
            wide_w[at, :] = value[:, half * LANES : (half + 1) * LANES] + before

    def put_vector(index, value):
        for half in range(2):
            row = slice(2 * index + half, 2 * index + half + 1)
            before = jnp.where(later, gv_ref[row, :], 0.0)
            gv_ref[row, :] = value[:, half * LANES : (half + 1) * LANES] + before

    def column_sum(value):
        return jnp.sum(value.astype(f32), axis=0, keepdims=True)

    put_vector(0, jnp.zeros((1, ROWS), f32))
    put_vector(1, jnp.zeros((1, ROWS), f32))
    g_vec = jnp.zeros((3 * atoms, feat_width), f32)
    for part_at in range(3):
        put_grad(O_AT, 6, part_at, ROWS, dot_tn(agg_low, go[part_at]))
        put_vector(7 + part_at, column_sum(go[part_at]))
        gp = proj[part_at].astype(bf16)
        put_grad(VEC_AT, 6, part_at, ROWS, dot_tn(vec_rows, gp))
        g_vec += dot_nt(gp, wb[W_VEC + part_at])

    g_query = agg[:, block_cols(4)].astype(bf16)
    put_grad(Q_AT, 2, 0, ROWS, dot_tn(norm_table[0:atoms, :], g_query))
    put_vector(2, column_sum(g_query))
    g_norm = dot_nt(g_query, wb[W_Q])

    sums = [jnp.zeros((ROWS, ROWS), f32) for column in range(4)]
    biases = [jnp.zeros((1, ROWS), f32) for column in range(4)]
    for b in range(buckets):
        rows = slice(b * ROWS, (b + 1) * ROWS)
        g_table = jnp.zeros((ROWS, ROWS), f32)
        for column in range(4):
            low = acc[b, :, block_cols(column)].astype(bf16)
            sums[column] += dot_tn(norm_table[rows, :], low)
            biases[column] += column_sum(low)
            g_table += dot_nt(low, wb[W_K + column])
        for half in range(2):
            domain = 2 * b + half
            if domain >= domains:
                continue
            here = slice(half * atoms, (half + 1) * atoms)
            if domain == 0:
                gown_ref[0, 0] = g_table[here, :] + g_norm
            else:
                back_refs[domain - 1][0, 0] = g_table[here, :].astype(bf16)
            for axis in range(3):
                block = acc[b, here, block_cols(4 + axis)]
                if domain == 0:
                    gown_ref[0, 1 + axis] = block + g_vec[parts[axis], :]
                else:
                    back_refs[domain - 1][0, 1 + axis] = block.astype(bf16)
    for column in range(4):
        if column == 0:
            put_grad(K_AT, 2, 0, ROWS, sums[column])
        else:
            put_grad(V_AT, 6, column - 1, ROWS, sums[column])
        put_vector(3 + column, biases[column])

    @pl.when(micro == pl.num_programs(0) - 1)
    def _():
        for column in range(4):
            block = gwd[0:NR, block_cols(column)] * 0.5
            first, stride, at = (DK_AT, 2, 0) if column == 0 else (DV_AT, 6, column - 1)
            for half in range(2):
                cols = slice(half * LANES, (half + 1) * LANES)
                wide_w[pl.ds(first + 2 * at + half, NR, stride=stride), :] = block[:, cols]
                row = 2 * (10 + column) + half
                bias = gwd[NR : NR + 1, column * ROWS + half * LANES :][:, :LANES]
                gv_ref[row : row + 1, :] = bias * 0.5
        for cell in range(cells):
            for part_at in range(parts_w):
                start = (cell * parts_w + part_at) * quarter
                gm_ref[part_at, cell] = wide_w[start : start + quarter, :].astype(bf16)


def core_mate(depth_at):
    return depth_at + 1 - 2 * (depth_at % 2)


def chip_mate(depth_at):
    return (depth_at + 2) % 4


def greet(cells, depth):
    barrier = pltpu.get_barrier_semaphore()
    cell_at, depth_at = lax.axis_index("cells"), lax.axis_index("depth")
    for by in range(1, cells):
        pl.semaphore_signal(barrier, inc=1, device_id={"cells": (cell_at + by) % cells})
    for by in range(1, depth):
        pl.semaphore_signal(barrier, inc=1, device_id={"depth": (depth_at + by) % depth})
    pl.semaphore_wait(barrier, cells + depth - 2)


def remote(source, target, send, receive, device):
    return pltpu.make_async_remote_copy(
        src_ref=source, dst_ref=target, send_sem=send, recv_sem=receive, device_id=device
    )


def fetch_kernel(cells, depth, micros, sources, faces, *refs):
    own_ref, lists_ref, w_ref, v_ref = refs[:4]
    halo_refs = refs[4 : 4 + len(sources)]
    got_lists, got_w, got_v = refs[4 + len(sources) : 7 + len(sources)]
    halo_send, halo_recv, list_send, list_recv, v_send, v_recv, w_send, w_recv = refs[
        7 + len(sources) :
    ]
    cell_at, depth_at = lax.axis_index("cells"), lax.axis_index("depth")
    sizes = {"cells": cells, "depth": depth}
    places = {"cells": cell_at, "depth": depth_at}
    got_w[cell_at] = w_ref[...]
    got_v[cell_at] = v_ref[...]
    greet(cells, depth)

    def ahead(axis, by):
        return {axis: (places[axis] + by) % sizes[axis]}

    started = []

    def start(*args):
        copy = remote(*args)
        copy.start()
        started.append(copy)
        return copy

    first = []
    for by in range(1, cells):
        there = ahead("cells", by)
        first.append(
            start(
                w_ref.at[depth_at],
                got_w.at[cell_at, depth_at],
                w_send.at[0, by],
                w_recv.at[0, by],
                there,
            )
        )
    lists = [
        start(
            lists_ref.at[face],
            got_lists.at[face],
            list_send.at[face],
            list_recv.at[face],
            ahead(axis, by),
        )
        for face, (axis, by) in enumerate(faces)
    ]
    vectors = [
        start(v_ref, got_v.at[cell_at], v_send.at[by], v_recv.at[by], ahead("cells", by))
        for by in range(1, cells)
    ]
    halos = []
    for micro in range(micros):
        for index, (axis, by) in enumerate(sources):
            halos.append(
                start(
                    own_ref.at[micro],
                    halo_refs[index].at[micro],
                    halo_send.at[micro, index],
                    halo_recv.at[micro, index],
                    ahead(axis, by),
                )
            )
    mate, other = core_mate(depth_at), chip_mate(depth_at)
    across = []
    last = []
    for by in range(1, cells):
        first[by - 1].wait_recv()
        piece = got_w.at[(cell_at + cells - by) % cells, depth_at]
        across.append(
            start(piece, piece, w_send.at[1, by], w_recv.at[1, by], {"depth": other})
        )
        last.append(start(piece, piece, w_send.at[2, by], w_recv.at[2, by], {"depth": mate}))
    for by in range(1, cells):
        across[by - 1].wait_recv()
        piece = got_w.at[(cell_at + cells - by) % cells, other]
        last.append(start(piece, piece, w_send.at[3, by], w_recv.at[3, by], {"depth": mate}))
    for copy in lists + vectors + last + halos:
        copy.wait_recv()
    for copy in started:
        copy.wait_send()


def close_kernel(cells, depth, micros, sources, *refs):
    x_ref, cotx_ref, cotv_ref, gain_ref, gvec_in, part_ref = refs[:6]
    refs = refs[6:]
    gown_ref = refs[0]
    back_refs = refs[1 : 1 + len(sources)]
    refs = refs[1 + len(sources) :]
    gx_ref, gvec_ref, summ_ref, sumv_ref = refs[:4]
    came, one_in, two_out, two_in, three_out, three_in, held, quad, octo = refs[4:13]
    halo_send, halo_recv, m_send, m_recv, c_send, c_recv, d_send, d_recv, e_send, e_recv, f_send, f_recv = refs[13:]
    cell_at, depth_at = lax.axis_index("cells"), lax.axis_index("depth")
    sizes = {"cells": cells, "depth": depth}
    places = {"cells": cell_at, "depth": depth_at}
    greet(cells, depth)

    def ahead(axis, by):
        return {axis: (places[axis] + by) % sizes[axis]}

    started = []

    def start(*args):
        copy = remote(*args)
        copy.start()
        started.append(copy)
        return copy

    mate, other = core_mate(depth_at), chip_mate(depth_at)
    mate_other = chip_mate(mate)
    one_far = start(
        part_ref.at[mate_other], one_in.at[1], m_send.at[0], m_recv.at[0], {"depth": mate}
    )
    one_near = start(part_ref.at[mate], one_in.at[0], m_send.at[1], m_recv.at[1], {"depth": mate})
    halos = []
    for micro in range(micros):
        for index, (axis, by) in enumerate(sources):
            halos.append(
                start(
                    back_refs[index].at[micro],
                    came.at[micro, index],
                    halo_send.at[micro, index],
                    halo_recv.at[micro, index],
                    ahead(axis, -by),
                )
            )
    one_far.wait_recv()
    two_out[...] = (part_ref[other].astype(f32) + one_in[1].astype(f32)).astype(bf16)
    two = start(two_out, two_in, m_send.at[2], m_recv.at[2], {"depth": other})
    one_near.wait_recv()
    two.wait_recv()
    for cell in range(cells):
        total = (
            part_ref[depth_at, cell].astype(f32)
            + one_in[0, cell].astype(f32)
            + two_in[cell].astype(f32)
        )
        three_out[cell] = total.astype(bf16)
    three = []
    for by in range(1, cells):
        there = (cell_at + by) % cells
        three.append(
            start(
                three_out.at[there],
                three_in.at[by],
                c_send.at[by],
                c_recv.at[by],
                {"cells": there},
            )
        )

    for copy in halos:
        copy.wait_recv()
    gain = jnp.concatenate([gain_ref[half : half + 1, :].astype(f32) for half in range(2)], axis=1)
    norm_grads = [jnp.zeros((1, gain.shape[1]), f32) for part in range(2)]
    for micro in range(micros):
        total = [gown_ref[micro, part] for part in range(4)]
        for index in range(len(sources)):
            for part in range(4):
                total[part] = total[part] + came[micro, index, part].astype(f32)
        hat, spread = normalise(x_ref[micro])
        norm_grads[0] += jnp.sum(total[0] * hat, axis=0, keepdims=True)
        norm_grads[1] += jnp.sum(total[0], axis=0, keepdims=True)
        g_hat = total[0] * gain
        g_x = spread * (g_hat - lane_mean(g_hat) - hat * lane_mean(g_hat * hat))
        gx_ref[micro] = cotx_ref[micro] + g_x
        for axis in range(3):
            gvec_ref[micro, axis] = cotv_ref[micro, axis] + total[1 + axis]
    held[...] = gvec_in[...]
    for part in range(2):
        for half in range(2):
            row = 2 * part + half
            held[row : row + 1, :] = norm_grads[part][:, half * LANES : (half + 1) * LANES]
    quad[depth_at] = held[...]
    four = [
        start(held, quad.at[depth_at], d_send.at[by], d_recv.at[by], ahead("depth", by))
        for by in range(1, depth)
    ]

    for copy in three:
        copy.wait_recv()
    final = three_out[cell_at].astype(f32)
    for by in range(1, cells):
        final = final + three_in[by].astype(f32)
    summ_ref[depth_at] = final
    share = [
        start(
            summ_ref.at[depth_at],
            summ_ref.at[depth_at],
            e_send.at[by],
            e_recv.at[by],
            ahead("depth", by),
        )
        for by in range(1, depth)
    ]
    for copy in four:
        copy.wait_recv()
    total = quad[0]
    for at in range(1, depth):
        total = total + quad[at]
    octo[cell_at] = total
    eight = [
        start(
            octo.at[cell_at],
            octo.at[cell_at],
            f_send.at[by],
            f_recv.at[by],
            ahead("cells", by),
        )
        for by in range(1, cells)
    ]
    for copy in eight:
        copy.wait_recv()
    total = octo[0]
    for cell in range(1, cells):
        total = total + octo[cell]
    sumv_ref[...] = total
    for copy in share:
        copy.wait_recv()
    for copy in started:
        copy.wait_send()


def adam_update(weight, grad, first, second):
    first_new = beta_one * first + (1.0 - beta_one) * grad
    second_new = beta_two * second + (1.0 - beta_two) * grad * grad
    first_hat = first_new / (1.0 - beta_one**STEP)
    second_hat = second_new / (1.0 - beta_two**STEP)
    weight_new = weight - learn_rate * (
        first_hat / (jnp.sqrt(second_hat) + adam_eps) + decay_rate * weight
    )
    return (weight_new, first_new, second_new)


def shards(
    x_in,
    vec_in,
    cot_x,
    cot_vec,
    mats,
    vecs,
    mats_first,
    mats_second,
    vecs_first,
    vecs_second,
    atom_count,
    neighbours,
    edge_mask,
    edge_vec,
    send_list,
):
    micros, atoms, width = x_in.shape
    slots = neighbours.shape[1]
    halo = send_list.shape[-1]
    per_face = halo // LANES
    cells, depth = lax.axis_size("cells"), lax.axis_size("depth")
    faces = [("cells", 1), ("cells", -1), ("cells", FOLD), ("cells", -FOLD), ("depth", 1), ("depth", -1)]
    sizes = {"cells": cells, "depth": depth}
    sources = []
    face_source = []
    for axis, by in faces:
        key = (axis, by % sizes[axis])
        if key not in sources:
            sources.append(key)
        face_source.append(sources.index(key))
    domains = 1 + len(sources)
    buckets = (domains * atoms + ROWS - 1) // ROWS
    block_of = [1 + face_source[row // per_face] for row in range(6 * per_face)]

    whole = pl.BlockSpec(memory_space=pltpu.VMEM)
    scalars = pl.BlockSpec(memory_space=pltpu.SMEM)

    any_space = pl.BlockSpec(memory_space=pl.ANY)
    count = len(sources)
    quarter = mats.shape[0] // LANES // depth
    v_rows = -(-vecs.shape[0] // LANES)
    v_low = jnp.pad(vecs.astype(bf16), (0, v_rows * LANES - vecs.shape[0])).reshape(v_rows, LANES)
    faces_first = jnp.moveaxis(
        send_list.reshape(micros, 6, per_face, LANES), 1, 0
    ).reshape(6, micros * per_face, LANES)

    own, w_low = pl.pallas_call(
        norm_kernel,
        out_shape=(
            jax.ShapeDtypeStruct((micros, 4, atoms, width), bf16),
            jax.ShapeDtypeStruct((depth, quarter, LANES), bf16),
        ),
        in_specs=[whole] * 3,
        out_specs=[whole] * 2,
        name="norm",
    )(x_in, vec_in, mats.reshape(-1, LANES))

    dma = pltpu.SemaphoreType.DMA
    fetched = pl.pallas_call(
        partial(fetch_kernel, cells, depth, micros, sources, faces),
        out_shape=tuple(
            [jax.ShapeDtypeStruct((micros, 4, atoms, width), bf16)] * count
            + [
                jax.ShapeDtypeStruct(faces_first.shape, i32),
                jax.ShapeDtypeStruct((cells, depth, quarter, LANES), bf16),
                jax.ShapeDtypeStruct((cells, v_rows, LANES), bf16),
            ]
        ),
        in_specs=[any_space] + [whole] * 3,
        out_specs=[any_space] * count + [whole] * 3,
        scratch_shapes=[
            dma((micros, count)),
            dma((micros, count)),
            dma((6,)),
            dma((6,)),
            dma((cells,)),
            dma((cells,)),
            dma((4, cells)),
            dma((4, cells)),
        ],
        compiler_params=pltpu.CompilerParams(
            collective_id=0, has_side_effects=True, vmem_limit_bytes=VMEM_LIMIT
        ),
        name="fetch",
    )(own, faces_first, w_low, v_low)
    halos = fetched[:count]
    got_lists, w_all, v_all = fetched[count:]
    list_rows = jnp.moveaxis(
        got_lists.reshape(6, micros, per_face, LANES), 1, 0
    ).reshape(micros, 6 * per_face, LANES)
    v_all = v_all.reshape(cells, v_rows * LANES)[:, : vecs.shape[0]].reshape(-1, LANES)
    w_rows, v_rows = cells * depth * quarter, v_all.shape[0]

    limit = slots * atoms + buckets * (slots // BLOCK_SLOTS) * 8 + buckets * 2 * UNIT
    capacity = (limit + UNIT - 1) // UNIT * UNIT + 4 * UNIT

    def by_micro(array):
        zeros = (0,) * (len(array.shape) - 1)
        return pl.BlockSpec((1,) + tuple(array.shape[1:]), lambda i: (i,) + zeros)

    per_micro = [neighbours, edge_mask, edge_vec, list_rows, x_in, vec_in, cot_x, cot_vec, *halos]
    out_blocks = [
        jax.ShapeDtypeStruct((micros, atoms, width), f32),
        jax.ShapeDtypeStruct((micros, 3, atoms, width), f32),
        jax.ShapeDtypeStruct((micros, 4, atoms, width), f32),
    ] + [jax.ShapeDtypeStruct((micros, 4, atoms, width), bf16)] * count
    results = pl.pallas_call(
        partial(edge_kernel, domains, buckets, block_of),
        out_shape=tuple(
            out_blocks
            + [
                jax.ShapeDtypeStruct((depth, cells, quarter, LANES), bf16),
                jax.ShapeDtypeStruct((v_rows, LANES), f32),
            ]
        ),
        grid=(micros,),
        in_specs=[scalars] + [by_micro(array) for array in per_micro] + [whole] * 2,
        out_specs=[by_micro(block) for block in out_blocks] + [whole] * 2,
        scratch_shapes=[
            pltpu.VMEM((slots, LANES, LANES), bf16),
            pltpu.VMEM((slots, atoms), i32),
            pltpu.VMEM((slots // BLOCK_SLOTS, LANES), i32),
            pltpu.SMEM((slots // BLOCK_SLOTS, LANES), i32),
            pltpu.VMEM((capacity, LANES), f32),
            pltpu.SemaphoreType.DMA(()),
            pltpu.VMEM((w_rows, LANES), f32),
            pltpu.VMEM((11, ROWS, ROWS), bf16),
            pltpu.VMEM((LANES, 4 * ROWS), bf16),
            pltpu.VMEM((buckets * ROWS, ROWS), bf16),
            pltpu.VMEM((buckets, ROWS, 7 * ROWS), bf16),
            pltpu.VMEM((buckets, ROWS, 7 * ROWS), f32),
            pltpu.VMEM((atoms, 5 * ROWS), bf16),
            pltpu.VMEM((3, 3 * atoms, ROWS), f32),
            pltpu.VMEM((3, atoms, ROWS), bf16),
            pltpu.VMEM((atoms, 5 * ROWS), f32),
            pltpu.VMEM((FEATS, 4 * ROWS), f32),
            pltpu.VMEM((ROWS, ROWS), bf16),
        ]
        + [
            scratch
            for scratch in (
                pltpu.VMEM((UNIT, ROWS), bf16),
                pltpu.VMEM((UNIT, LANES), bf16),
                pltpu.VMEM((UNIT, WORK * ROWS), f32),
                pltpu.VMEM((UNIT, LANES), f32),
                pltpu.VMEM((3, UNIT, LANES), f32),
                pltpu.VMEM((2, 2 * UNIT, LANES), bf16),
                pltpu.VMEM((14, UNIT, LANES), bf16),
                pltpu.VMEM((8, UNIT, LANES), bf16),
                pltpu.VMEM((12, UNIT, LANES), bf16),
            )
            for side in range(2)
        ],
        compiler_params=pltpu.CompilerParams(vmem_limit_bytes=VMEM_LIMIT),
        name="edges",
    )(atom_count, *per_micro, w_all, v_all)
    out_x, out_vec, g_own = results[:3]
    backs = results[3 : 3 + count]
    part_m, part_v = results[3 + count :]
    grad_x, grad_vec, sum_mats, sum_vecs = pl.pallas_call(
        partial(close_kernel, cells, depth, micros, sources),
        out_shape=(
            jax.ShapeDtypeStruct(x_in.shape, f32),
            jax.ShapeDtypeStruct(vec_in.shape, f32),
            jax.ShapeDtypeStruct((depth, quarter, LANES), f32),
            jax.ShapeDtypeStruct((v_rows, LANES), f32),
        ),
        in_specs=[whole] * 7 + [any_space] * count,
        out_specs=[whole] * 4,
        scratch_shapes=[
            pltpu.VMEM((micros, count, 4, atoms, width), bf16),
            pltpu.VMEM((2, cells, quarter, LANES), bf16),
            pltpu.VMEM((cells, quarter, LANES), bf16),
            pltpu.VMEM((cells, quarter, LANES), bf16),
            pltpu.VMEM((cells, quarter, LANES), bf16),
            pltpu.VMEM((cells, quarter, LANES), bf16),
            pltpu.VMEM((v_rows, LANES), f32),
            pltpu.VMEM((depth, v_rows, LANES), f32),
            pltpu.VMEM((cells, v_rows, LANES), f32),
            dma((micros, count)),
            dma((micros, count)),
            dma((3,)),
            dma((3,)),
            dma((cells,)),
            dma((cells,)),
            dma((depth,)),
            dma((depth,)),
            dma((depth,)),
            dma((depth,)),
            dma((cells,)),
            dma((cells,)),
        ],
        compiler_params=pltpu.CompilerParams(
            collective_id=1, has_side_effects=True, vmem_limit_bytes=VMEM_LIMIT
        ),
        name="close",
    )(
        x_in,
        cot_x,
        cot_vec,
        v_all,
        part_v,
        part_m,
        g_own,
        *backs,
    )
    sum_mats = sum_mats.reshape(-1)
    sum_vecs = lax.dynamic_slice_in_dim(
        sum_vecs.reshape(-1), lax.axis_index("cells") * vecs.shape[0], vecs.shape[0]
    )
    new_mats, mats_one, mats_two = adam_update(mats, sum_mats, mats_first, mats_second)
    new_vecs, vecs_one, vecs_two = adam_update(vecs, sum_vecs, vecs_first, vecs_second)
    return (
        out_x,
        out_vec,
        grad_x,
        grad_vec,
        sum_mats,
        sum_vecs,
        new_mats,
        new_vecs,
        mats_one,
        mats_two,
        vecs_one,
        vecs_two,
    )


def solution(mesh):
    by_atom = ("cells", "depth")
    shard = P("cells")
    in_specs = (
        P(None, by_atom, None),
        P(None, None, by_atom, None),
        P(None, by_atom, None),
        P(None, None, by_atom, None),
        shard,
        shard,
        shard,
        shard,
        shard,
        shard,
        P(None, by_atom),
        P(None, None, by_atom),
        P(None, None, by_atom),
        P(None, None, None, by_atom),
        P(None, by_atom, None),
    )
    out_specs = (
        P(None, by_atom, None),
        P(None, None, by_atom, None),
        P(None, by_atom, None),
        P(None, None, by_atom, None),
    ) + (shard,) * 8
    return jax.shard_map(shards, mesh=mesh, in_specs=in_specs, out_specs=out_specs, check_vma=False)
```

```python
from functools import partial
import math

import jax
import jax.numpy as jnp
from jax import lax
from jax.experimental import pallas as pl
from jax.experimental.pallas import tpu as pltpu
from jax.sharding import PartitionSpec as P

HEADS = 8
NR = 32
FOLD = 4
STEP = 3

LANES = 128
ROWS = 256
UNIT = 256
BLOCK_SLOTS = 4
TILE = 192

norm_eps = 1e-05
cut_radius = 5.0
beta_one = 0.5
beta_two = 0.5
learn_rate = 0.05
decay_rate = 0.01
adam_eps = 1e-08

f32 = jnp.float32
bf16 = jnp.bfloat16
i32 = jnp.int32

VMEM_LIMIT = 60 * 1024 * 1024


def dot_nn(left, right):
    return lax.dot_general(left, right, (((1,), (0,)), ((), ())), preferred_element_type=f32)


def dot_nt(left, right):
    return lax.dot_general(left, right, (((1,), (1,)), ((), ())), preferred_element_type=f32)


def dot_tn(left, right):
    return lax.dot_general(left, right, (((0,), (0,)), ((), ())), preferred_element_type=f32)


def lane_mean(block):
    return jnp.sum(block, axis=-1, keepdims=True) * (1.0 / block.shape[-1])


def normalise(block):
    centered = block - lane_mean(block)
    spread = lax.rsqrt(lane_mean(centered * centered) + norm_eps)
    return centered * spread, spread


def norm_kernel(x_ref, vec_ref, mats_ref, own_ref, low_ref):
    quarter = low_ref.shape[1]
    for part in range(low_ref.shape[0]):
        low_ref[part] = mats_ref[part * quarter : (part + 1) * quarter, :].astype(bf16)
    for micro in range(x_ref.shape[0]):
        own_ref[micro, 0] = normalise(x_ref[micro])[0].astype(bf16)
        own_ref[micro, 1:] = vec_ref[micro].astype(bf16)


Q_AT, K_AT, V_AT, VEC_AT, O_AT, DK_AT, DV_AT = 0, 512, 1024, 2560, 4096, 5632, 5696
W_Q, W_K, W_V, W_VEC, W_O = 0, 1, 2, 5, 8
FEATS = 48
CHUNK = 16
GATH, PER_ATOM, FILT, SUMS, KEPT, WORK = 0, 7, 12, 16, 18, 24


def edge_features(nbr, mask, geom, lists, block_of, buckets, feat, place, count_vec):
    slots, atoms = nbr.shape
    blocks = slots // BLOCK_SLOTS
    live = mask > 0
    halo_at = nbr - atoms
    list_row = halo_at >> 7
    list_lane = halo_at & (LANES - 1)
    atom_in = nbr
    block_id = jnp.zeros_like(nbr)
    for row in range(lists.shape[0]):
        table = jnp.broadcast_to(lists[row : row + 1, :], (slots, atoms))
        picked = jnp.take_along_axis(table, list_lane, axis=1)
        here = list_row == row
        atom_in = jnp.where(here, picked, atom_in)
        block_id = jnp.where(here, block_of[row], block_id)
    entry = block_id * atoms + atom_in
    bucket = entry >> 8
    low = ((entry & (ROWS - 1)) + 1).astype(f32)
    atom_id = (lax.broadcasted_iota(i32, (slots, atoms), 1) + 1).astype(f32)
    live_float = live.astype(f32)

    radius = jnp.sqrt(geom[0] * geom[0] + geom[1] * geom[1] + geom[2] * geom[2])
    units = [comp / radius for comp in geom]
    cut = 0.5 * (jnp.cos(math.pi * radius / cut_radius) + 1.0) * live_float
    cut_high = cut.astype(bf16).astype(f32)
    cut_low = cut - cut_high
    decayed = jnp.exp(-(5.0 / cut_radius) * radius)
    start_value = math.exp(-cut_radius)
    ramp = lax.broadcasted_iota(i32, (NR, 1), 0).astype(f32) / float(NR - 1)
    centers = start_value * (1.0 - ramp) + ramp
    width_coef = (2.0 / NR * (1.0 - start_value)) ** (-2)
    extras = [live_float, low, atom_id, cut_high, cut_low] + units
    zeros = jnp.zeros((16 - len(extras), atoms), f32)
    for slot in range(slots):
        gap = decayed[slot : slot + 1, :] - centers
        basis = cut[slot : slot + 1, :] * jnp.exp(-width_coef * gap * gap)
        feat[slot, 0:NR, :] = basis.astype(bf16)
        rows = [extra[slot : slot + 1, :] for extra in extras] + [zeros]
        feat[slot, NR : NR + 16, :] = jnp.concatenate(rows, axis=0).astype(bf16)

    members = [jnp.where(live & (bucket == b), 1.0, 0.0) for b in range(buckets)]
    lane_from = lax.broadcasted_iota(i32, (atoms, 2 * atoms), 0)
    lane_to = lax.broadcasted_iota(i32, (atoms, 2 * atoms), 1)
    before = jnp.where((lane_from < lane_to) | (lane_to >= atoms), 1.0, 0.0).astype(bf16)
    slot_to = lax.broadcasted_iota(i32, (slots, slots), 0)
    slot_from = lax.broadcasted_iota(i32, (slots, slots), 1)
    same = (slot_to // BLOCK_SLOTS) == (slot_from // BLOCK_SLOTS)
    earlier = jnp.where(same & (slot_from < slot_to), 1.0, 0.0).astype(bf16)
    block_row = lax.broadcasted_iota(i32, (blocks, slots), 0)
    block_slot = lax.broadcasted_iota(i32, (blocks, slots), 1)
    gather_block = jnp.where(block_slot // BLOCK_SLOTS == block_row, 1.0, 0.0).astype(bf16)
    lane = lax.broadcasted_iota(i32, (blocks, LANES), 1)
    rank = jnp.zeros((slots, atoms), f32)
    counts = jnp.zeros((blocks, LANES), f32)
    for b in range(buckets):
        sums = dot_nn(members[b].astype(bf16), before)
        row_total = sums[:, atoms:].astype(bf16)
        offset = sums[:, :atoms] + dot_nn(earlier, row_total)
        rank = jnp.where(members[b] > 0.0, offset, rank)
        counts = jnp.where(lane == b, dot_nn(gather_block, row_total), counts)
    place[...] = jnp.where(live, bucket * 1024 + rank.astype(i32), -1)
    count_vec[...] = counts.astype(i32)


def pack_edges(blocks, atoms, buckets, feat, place, count_sc, packed):
    wide = BLOCK_SLOTS * atoms

    def total_body(block, totals):
        return tuple(
            total + (((count_sc[block, b] + 7) >> 3) << 3) for b, total in enumerate(totals)
        )

    totals = lax.fori_loop(0, blocks, total_body, (jnp.int32(0),) * buckets)
    held = [(total + (UNIT - 1)) >> 8 for total in totals]
    bases = [jnp.int32(UNIT)]
    for total in totals:
        bases.append(bases[-1] + (((total + (2 * UNIT - 1)) >> 8) << 8))

    def picks(places, b, first):
        wanted = lax.broadcasted_iota(i32, (TILE, wide), 0) + (b * 1024 + first)
        return jnp.where(places == wanted, 1.0, 0.0).astype(bf16)

    def block_body(block, at):
        first = block * BLOCK_SLOTS
        places = jnp.concatenate(
            [place[pl.ds(first + t, 1), :] for t in range(BLOCK_SLOTS)], axis=1
        )
        feats = jnp.concatenate([feat[first + t] for t in range(BLOCK_SLOTS)], axis=1)
        following = []
        for b in range(buckets):
            number = count_sc[block, b]
            packed[pl.ds(pl.multiple_of(at[b], 8), TILE), :] = dot_nt(picks(places, b, 0), feats)

            @pl.when(number > TILE)
            def _(b=b, number=number):
                def tile_body(tile, carry):
                    feats = jnp.concatenate([feat[first + t] for t in range(BLOCK_SLOTS)], axis=1)
                    pick = picks(places, b, tile * TILE)
                    start = pl.multiple_of(at[b] + tile * TILE, 8)
                    packed[pl.ds(start, TILE), :] = dot_nt(pick, feats)
                    return carry

                lax.fori_loop(1, (number + (TILE - 1)) // TILE, tile_body, 0)

            following.append(at[b] + (((number + 7) >> 3) << 3))
        return tuple(following)

    ends = lax.fori_loop(0, blocks, block_body, tuple(bases[:buckets]))
    zeros = jnp.zeros((UNIT, LANES), f32)
    for end in ends:
        packed[pl.ds(pl.multiple_of(end, 8), UNIT), :] = zeros
    packed[0:UNIT, :] = zeros
    return held, bases


def edge_kernel(domains, buckets, block_of, *refs):
    refs = list(refs)
    count_ref, nbr_ref, mask_ref, geom_ref, list_ref, x_ref, vec_ref, cotx_ref, cotv_ref = refs[:9]
    halo_refs = refs[9 : 9 + domains - 1]
    at = 9 + domains - 1
    w_ref, v_ref = refs[at : at + 2]
    at += 2
    outx_ref, outv_ref, gown_ref = refs[at : at + 3]
    at += 3
    back_refs = refs[at : at + domains - 1]
    at += domains - 1
    gm_ref, gv_ref = refs[at : at + 2]
    at += 2
    (
        feat,
        place,
        count_vec,
        count_sc,
        packed,
        sem,
        wide_w,
        wb,
        wd,
        norm_table,
        tab,
        acc,
        atom_tab,
        proj,
        go,
        agg,
        gwd,
        heads,
    ) = refs[at : at + 18]
    rest = refs[at + 18 :]
    sides = [tuple(rest[side::2]) for side in range(2)]
    micro = pl.program_id(0)
    slots, atoms = nbr_ref.shape[1:]
    feat_width = x_ref.shape[2]
    cells, parts_w, quarter = w_ref.shape[:3]
    parts = [slice(axis * atoms, (axis + 1) * atoms) for axis in range(3)]

    def vector(index):
        both = [v_ref[2 * index + half : 2 * index + half + 1, :].astype(f32) for half in range(2)]
        return jnp.concatenate(both, axis=1)

    @pl.when(micro == 0)
    def _():
        feat[...] = jnp.zeros_like(feat)
        for ref in sides[1][6:]:
            ref[...] = jnp.zeros_like(ref)
        gwd[...] = jnp.zeros_like(gwd)
        for cell in range(cells):
            for part in range(parts_w):
                start = (cell * parts_w + part) * quarter
                wide_w[start : start + quarter, :] = w_ref[cell, part].astype(f32)

        def weight_block(first, stride, column, rows):
            halves = [
                wide_w[pl.ds(first + 2 * column + half, rows, stride=stride), :]
                for half in range(2)
            ]
            return jnp.concatenate(halves, axis=1)

        for slot, first, stride, count in (
            (W_Q, Q_AT, 2, 1),
            (W_K, K_AT, 2, 1),
            (W_V, V_AT, 6, 3),
            (W_VEC, VEC_AT, 6, 3),
            (W_O, O_AT, 6, 3),
        ):
            for column in range(count):
                wb[slot + column] = weight_block(first, stride, column, ROWS).astype(bf16)
        bias_row = lax.broadcasted_iota(i32, (LANES - NR, 1), 0) == 0
        for column in range(4):
            if column == 0:
                block = weight_block(DK_AT, 2, 0, NR)
            else:
                block = weight_block(DV_AT, 6, column - 1, NR)
            bias = jnp.where(bias_row, vector(10 + column), 0.0)
            cols = slice(column * ROWS, (column + 1) * ROWS)
            wd[:, cols] = (jnp.concatenate([block, bias], axis=0) * 0.5).astype(bf16)
        head_from = lax.broadcasted_iota(i32, (ROWS, ROWS), 0) // (feat_width // HEADS)
        head_to = lax.broadcasted_iota(i32, (ROWS, ROWS), 1) // (feat_width // HEADS)
        heads[...] = jnp.where(head_from == head_to, 0.5, 0.0).astype(bf16)

    geom = [geom_ref[0, axis] for axis in range(3)]
    edge_features(
        nbr_ref[0], mask_ref[0], geom, list_ref[0], block_of, buckets, feat, place, count_vec
    )
    copy = pltpu.make_async_copy(count_vec, count_sc, sem)
    copy.start()

    gain = vector(0)
    shift = vector(1)
    own_hat, unused = normalise(x_ref[0])
    vec_low = vec_ref[0].astype(bf16)
    for domain in range(2 * buckets):
        rows = slice(domain * atoms, (domain + 1) * atoms)
        here = slice((domain % 2) * atoms, (domain % 2 + 1) * atoms)
        if domain == 0:
            norm_table[rows, :] = (own_hat * gain + shift).astype(bf16)
        elif domain < domains:
            hat = halo_refs[domain - 1][0, 0].astype(f32)
            norm_table[rows, :] = (hat * gain + shift).astype(bf16)
        else:
            norm_table[rows, :] = jnp.zeros((atoms, feat_width), bf16)
        for axis in range(3):
            cols = slice((4 + axis) * ROWS, (5 + axis) * ROWS)
            if domain < domains:
                block = vec_low[axis] if domain == 0 else halo_refs[domain - 1][0, 1 + axis]
            else:
                block = jnp.zeros((atoms, feat_width), bf16)
            tab[domain // 2, here, cols] = block
    for b in range(buckets):
        rows = slice(b * ROWS, (b + 1) * ROWS)
        for column in range(4):
            cols = slice(column * ROWS, (column + 1) * ROWS)
            made = dot_nn(norm_table[rows, :], wb[W_K + column]) + vector(3 + column)
            tab[b, :, cols] = made.astype(bf16)

    live = (lax.broadcasted_iota(i32, (atoms, 1), 0) < count_ref[micro, 0]).astype(f32)
    query = dot_nn(norm_table[0:atoms, :], wb[W_Q]) + vector(2)
    atom_tab[:, 0:ROWS] = query.astype(bf16)
    vec_rows = vec_low.reshape(3 * atoms, feat_width)
    for part in range(3):
        proj[part] = dot_nn(vec_rows, wb[W_VEC + part])
    cot_x = cotx_ref[0] * live
    vec_dot = jnp.zeros((atoms, feat_width), f32)
    go_one = jnp.zeros((atoms, feat_width), f32)
    for axis in range(3):
        cot_v = cotv_ref[0, axis] * live
        vec_dot += proj[0, parts[axis], :] * proj[1, parts[axis], :]
        go_one += proj[2, parts[axis], :] * cot_v
        atom_tab[:, (2 + axis) * ROWS : (3 + axis) * ROWS] = cot_v.astype(bf16)
    go[0] = go_one.astype(bf16)
    go[1] = (vec_dot * cot_x).astype(bf16)
    go[2] = cot_x.astype(bf16)
    g_agg = dot_nt(go[0], wb[W_O])
    for part in range(1, 3):
        g_agg += dot_nt(go[part], wb[W_O + part])
    atom_tab[:, ROWS : 2 * ROWS] = g_agg.astype(bf16)
    agg[...] = jnp.zeros_like(agg)
    for b in range(buckets):
        acc[b] = jnp.zeros((ROWS, 7 * ROWS), f32)

    copy.wait()
    held, bases = pack_edges(
        slots // BLOCK_SLOTS, atoms, buckets, feat, place, count_sc, packed
    )
    firsts = [jnp.int32(0)]
    for number in held:
        firsts.append(firsts[-1] + number)
    total_units = firsts[-1]

    def bucket_of(unit):
        b = jnp.int32(0)
        for at in range(1, buckets):
            b = b + jnp.where(unit >= firsts[at], 1, 0)
        return b

    def rows_of(unit):
        start = jnp.int32(0)
        for at in range(buckets):
            inside = (unit >= firsts[at]) & (unit < firsts[at + 1])
            start = jnp.where(inside, bases[at] + (unit - firsts[at]) * UNIT, start)
        return pl.ds(pl.multiple_of(start, UNIT), UNIT)

    def block_cols(block):
        return slice(block * ROWS, (block + 1) * ROWS)

    def hits(side, rows):
        hit, atom_one = side[:2]
        full = packed[rows, :]
        lane_row = lax.broadcasted_iota(i32, (UNIT, ROWS), 1).astype(f32) + 1.0
        lane_atom = lax.broadcasted_iota(i32, (UNIT, LANES), 1).astype(f32) + 1.0
        hit[...] = jnp.where(full[:, NR + 1 : NR + 2] == lane_row, 1.0, 0.0).astype(bf16)
        atom_one[...] = jnp.where(full[:, NR + 2 : NR + 3] == lane_atom, 1.0, 0.0).astype(bf16)

    def spread(side, rows):
        cutb, dirs = side[3:5]
        full = packed[rows, :]
        for axis in range(3):
            column = full[:, NR + 5 + axis : NR + 6 + axis]
            dirs[axis] = jnp.broadcast_to(column, (UNIT, LANES))
        column = full[:, NR + 3 : NR + 4] + full[:, NR + 4 : NR + 5]
        cutb[...] = jnp.broadcast_to(column, (UNIT, LANES))

    def gather_steps(side, unit):
        hit, atom_one, work = side[:3]
        b = jnp.minimum(bucket_of(unit), buckets - 1)
        rows = rows_of(unit)

        def gather_table(block):
            work[:, block_cols(GATH + block)] = dot_nn(hit[...], tab[b, :, block_cols(block)])

        def gather_atom(block):
            made = dot_nn(atom_one[...], atom_tab[:, block_cols(block)])
            work[:, block_cols(PER_ATOM + block)] = made

        def filters(block):
            low = packed[rows, :].astype(bf16)
            work[:, block_cols(FILT + block)] = dot_nn(low, wd[:, block_cols(block)])

        return (
            [partial(gather_table, block) for block in range(7)]
            + [partial(gather_atom, block) for block in range(5)]
            + [partial(filters, block) for block in range(4)]
        )

    def mix(first, second):
        done = 0
        for at, step in enumerate(first):
            step()
            until = (at + 1) * len(second) // len(first)
            for other in second[done:until]:
                other()
            done = until

    chunks = [
        (slice(start, start + CHUNK), half)
        for start in range(0, UNIT, CHUNK)
        for half in range(2)
    ]

    def put(ref, block, here, half, value):
        ref[2 * block + half, here, :] = value.astype(bf16)

    def reader(work):
        def part(block, here, half):
            start = block * ROWS + half * LANES
            return work[here, start : start + LANES]

        def gate(here, block, half):
            value = part(FILT + block, here, half)
            turn = jnp.tanh(value)
            lift = 1.0 + turn
            silu = value * lift
            return silu, lift + silu * (1.0 - turn)

        return part, gate

    def heads_stage(side, here, half):
        work, pair = side[2], side[5]
        part, gate = reader(work)

        def keep(block, value):
            start = (KEPT + block) * ROWS + half * LANES
            work[here, start : start + LANES] = value

        there = slice(UNIT + here.start, UNIT + here.stop)
        silu, slope = gate(here, 0, half)
        query_e = part(PER_ATOM, here, half)
        key_e = part(GATH, here, half)
        gated = query_e * silu
        keep(0, gated)
        keep(1, query_e * key_e * slope)
        keep(2, key_e * silu)
        pair[half, here, :] = (gated * key_e).astype(bf16)
        silu, slope = gate(here, 1, half)
        cot_e = part(PER_ATOM + 1, here, half)
        value_e = part(GATH + 1, here, half)
        gated = value_e * silu
        keep(3, cot_e * silu)
        keep(4, cot_e * value_e * slope)
        keep(5, gated)
        pair[half, there, :] = (cot_e * gated).astype(bf16)

    def head_sums(side):
        work, pair = side[2], side[5]
        for at in range(2):
            rows = slice(at * UNIT, (at + 1) * UNIT)
            both = jnp.concatenate([pair[0, rows, :], pair[1, rows, :]], axis=1)
            work[:, block_cols(SUMS + at)] = dot_nn(both, heads[...])

    def vector_stage(side, here, half):
        dirs, dedge, dfilt, msg = side[4], *side[6:]
        part, gate = reader(side[2])
        cots = [part(PER_ATOM + 2 + axis, here, half) for axis in range(3)]
        vecs = [part(GATH + 4 + axis, here, half) for axis in range(3)]
        turns = [dirs[axis, here, :] for axis in range(3)]
        silu, slope = gate(here, 2, half)
        value_e = part(GATH + 2, here, half)
        gated = value_e * silu
        down = cots[0] * vecs[0] + cots[1] * vecs[1] + cots[2] * vecs[2]
        for axis in range(3):
            put(msg, 1 + axis, here, half, vecs[axis] * gated)
            put(dedge, 4 + axis, here, half, cots[axis] * gated)
        put(dedge, 2, here, half, down * silu)
        put(dfilt, 2, here, half, down * value_e * slope)
        silu, slope = gate(here, 3, half)
        value_e = part(GATH + 3, here, half)
        down = cots[0] * turns[0] + cots[1] * turns[1] + cots[2] * turns[2]
        put(dedge, 3, here, half, down * silu)
        put(dfilt, 3, here, half, down * value_e * slope)
        put(msg, 5, here, half, value_e * silu)

    def score_stage(side, here, half):
        cutb, dedge, dfilt, msg = side[3], *side[6:]
        part, unused = reader(side[2])
        cut = cutb[here, :]
        score = part(SUMS, here, half)
        turn = jnp.tanh(score)
        lift = 1.0 + turn
        silu = score * lift
        attention = silu * cut
        dscore = part(SUMS + 1, here, half) * cut * (lift + silu * (1.0 - turn))
        put(dedge, 0, here, half, dscore * part(KEPT, here, half))
        put(dfilt, 0, here, half, dscore * part(KEPT + 1, here, half))
        put(msg, 4, here, half, dscore * part(KEPT + 2, here, half))
        put(dedge, 1, here, half, attention * part(KEPT + 3, here, half))
        put(dfilt, 1, here, half, attention * part(KEPT + 4, here, half))
        put(msg, 0, here, half, attention * part(KEPT + 5, here, half))

    def both_halves(ref, block):
        return jnp.concatenate([ref[2 * block], ref[2 * block + 1]], axis=1)

    def scatter_steps(side, unit):
        dedge, dfilt, msg = side[6:]
        b = jnp.minimum(bucket_of(unit), buckets - 1)
        turned = packed[rows_of(unit), :].T

        def across(index):
            return turned[NR + index : NR + index + 1, :]

        sub_row = lax.broadcasted_iota(i32, (ROWS, UNIT), 0).astype(f32) + 1.0
        sub_atom = lax.broadcasted_iota(i32, (atoms, UNIT), 0).astype(f32) + 1.0
        hit_t = jnp.where(across(1) == sub_row, 1.0, 0.0).astype(bf16)
        atom_hit = across(2) == sub_atom
        atom_t = jnp.where(atom_hit, 1.0, 0.0).astype(bf16)
        feats_t = turned[0:FEATS, :].astype(bf16)
        turn = both_halves(msg, 5)

        def add_vector(axis):
            along = jnp.where(atom_hit, across(5 + axis), 0.0).astype(bf16)
            agg[:, block_cols(1 + axis)] += dot_nn(
                jnp.concatenate([atom_t, along], axis=1),
                jnp.concatenate([both_halves(msg, 1 + axis), turn], axis=0),
            )

        def add_table(block):
            acc[b, :, block_cols(block)] += dot_nn(hit_t, both_halves(dedge, block))

        def add_filter(block):
            gwd[:, block_cols(block)] += dot_nn(feats_t, both_halves(dfilt, block))

        def add_atom(block):
            agg[:, block_cols(block)] += dot_nn(atom_t, both_halves(msg, block))

        return (
            [partial(add_vector, axis) for axis in range(3)]
            + [partial(add_table, block) for block in (2, 3, 4, 5, 6, 0, 1)]
            + [partial(add_filter, block) for block in (2, 3, 0, 1)]
            + [partial(add_atom, block) for block in (0, 4)]
        )

    def on_chunks(stage, side):
        return [partial(stage, side, here, half) for here, half in chunks]

    hits(sides[0], rows_of(jnp.int32(0)))
    mix(gather_steps(sides[0], jnp.int32(0)), [])

    def pair_body(step, carry):
        for at in range(2):
            unit = 2 * step + at
            mine, other = sides[at], sides[1 - at]

            @pl.when(count_sc[0, 0] >= 0)
            def _(unit=unit, mine=mine, other=other):
                spread(mine, rows_of(unit))
                hits(other, rows_of(unit + 1))
                mix(scatter_steps(other, unit - 1), on_chunks(heads_stage, mine))

            @pl.when(count_sc[0, 0] >= 0)
            def _(unit=unit, mine=mine, other=other):
                head_sums(mine)
                mix(
                    gather_steps(other, unit + 1),
                    [step for two in zip(on_chunks(vector_stage, mine), on_chunks(score_stage, mine)) for step in two],
                )

        return carry

    steps = (total_units + 1) // 2
    lax.fori_loop(0, steps, pair_body, 0)
    mix(scatter_steps(sides[1], 2 * steps - 1), [])

    agg_low = agg[:, 0:ROWS].astype(bf16)
    outs = [dot_nn(agg_low, wb[W_O + part]) + vector(7 + part) for part in range(3)]
    outx_ref[0] = x_ref[0] + (vec_dot * outs[1] + outs[2]) * live
    g_dot = cot_x * outs[1]
    for axis in range(3):
        rows = parts[axis]
        vec_agg = agg[:, block_cols(1 + axis)]
        outv_ref[0, axis] = vec_ref[0, axis] + (proj[2, rows, :] * outs[0] + vec_agg) * live
        proj[2, rows, :] = cotv_ref[0, axis] * live * outs[0]
        first_part = proj[0, rows, :]
        proj[0, rows, :] = g_dot * proj[1, rows, :]
        proj[1, rows, :] = g_dot * first_part

    later = micro > 0

    def put_grad(first, stride, column, rows, value):
        for half in range(2):
            at = pl.ds(first + 2 * column + half, rows, stride=stride)
            before = jnp.where(later, wide_w[at, :], 0.0)
            wide_w[at, :] = value[:, half * LANES : (half + 1) * LANES] + before

    def put_vector(index, value):
        for half in range(2):
            row = slice(2 * index + half, 2 * index + half + 1)
            before = jnp.where(later, gv_ref[row, :], 0.0)
            gv_ref[row, :] = value[:, half * LANES : (half + 1) * LANES] + before

    def column_sum(value):
        return jnp.sum(value.astype(f32), axis=0, keepdims=True)

    put_vector(0, jnp.zeros((1, ROWS), f32))
    put_vector(1, jnp.zeros((1, ROWS), f32))
    g_vec = jnp.zeros((3 * atoms, feat_width), f32)
    for part_at in range(3):
        put_grad(O_AT, 6, part_at, ROWS, dot_tn(agg_low, go[part_at]))
        put_vector(7 + part_at, column_sum(go[part_at]))
        gp = proj[part_at].astype(bf16)
        put_grad(VEC_AT, 6, part_at, ROWS, dot_tn(vec_rows, gp))
        g_vec += dot_nt(gp, wb[W_VEC + part_at])

    g_query = agg[:, block_cols(4)].astype(bf16)
    put_grad(Q_AT, 2, 0, ROWS, dot_tn(norm_table[0:atoms, :], g_query))
    put_vector(2, column_sum(g_query))
    g_norm = dot_nt(g_query, wb[W_Q])

    sums = [jnp.zeros((ROWS, ROWS), f32) for column in range(4)]
    biases = [jnp.zeros((1, ROWS), f32) for column in range(4)]
    for b in range(buckets):
        rows = slice(b * ROWS, (b + 1) * ROWS)
        g_table = jnp.zeros((ROWS, ROWS), f32)
        for column in range(4):
            low = acc[b, :, block_cols(column)].astype(bf16)
            sums[column] += dot_tn(norm_table[rows, :], low)
            biases[column] += column_sum(low)
            g_table += dot_nt(low, wb[W_K + column])
        for half in range(2):
            domain = 2 * b + half
            if domain >= domains:
                continue
            here = slice(half * atoms, (half + 1) * atoms)
            if domain == 0:
                gown_ref[0, 0] = g_table[here, :] + g_norm
            else:
                back_refs[domain - 1][0, 0] = g_table[here, :].astype(bf16)
            for axis in range(3):
                block = acc[b, here, block_cols(4 + axis)]
                if domain == 0:
                    gown_ref[0, 1 + axis] = block + g_vec[parts[axis], :]
                else:
                    back_refs[domain - 1][0, 1 + axis] = block.astype(bf16)
    for column in range(4):
        if column == 0:
            put_grad(K_AT, 2, 0, ROWS, sums[column])
        else:
            put_grad(V_AT, 6, column - 1, ROWS, sums[column])
        put_vector(3 + column, biases[column])

    @pl.when(micro == pl.num_programs(0) - 1)
    def _():
        for column in range(4):
            block = gwd[0:NR, block_cols(column)] * 0.5
            first, stride, at = (DK_AT, 2, 0) if column == 0 else (DV_AT, 6, column - 1)
            for half in range(2):
                cols = slice(half * LANES, (half + 1) * LANES)
                wide_w[pl.ds(first + 2 * at + half, NR, stride=stride), :] = block[:, cols]
                row = 2 * (10 + column) + half
                bias = gwd[NR : NR + 1, column * ROWS + half * LANES :][:, :LANES]
                gv_ref[row : row + 1, :] = bias * 0.5
        for cell in range(cells):
            for part_at in range(parts_w):
                start = (cell * parts_w + part_at) * quarter
                gm_ref[part_at, cell] = wide_w[start : start + quarter, :].astype(bf16)


def core_mate(depth_at):
    return depth_at + 1 - 2 * (depth_at % 2)


def chip_mate(depth_at):
    return (depth_at + 2) % 4


def greet(cells, depth):
    barrier = pltpu.get_barrier_semaphore()
    cell_at, depth_at = lax.axis_index("cells"), lax.axis_index("depth")
    for by in range(1, cells):
        pl.semaphore_signal(barrier, inc=1, device_id={"cells": (cell_at + by) % cells})
    for by in range(1, depth):
        pl.semaphore_signal(barrier, inc=1, device_id={"depth": (depth_at + by) % depth})
    pl.semaphore_wait(barrier, cells + depth - 2)


def remote(source, target, send, receive, device):
    return pltpu.make_async_remote_copy(
        src_ref=source, dst_ref=target, send_sem=send, recv_sem=receive, device_id=device
    )


def fetch_kernel(cells, depth, micros, sources, faces, *refs):
    own_ref, lists_ref, w_ref, v_ref = refs[:4]
    halo_refs = refs[4 : 4 + len(sources)]
    got_lists, got_w, got_v = refs[4 + len(sources) : 7 + len(sources)]
    (
        halo_send,
        halo_recv,
        list_send,
        list_recv,
        v_send,
        v_recv,
        w_send,
        w_recv,
    ) = refs[7 + len(sources) :]
    cell_at, depth_at = lax.axis_index("cells"), lax.axis_index("depth")
    sizes = {"cells": cells, "depth": depth}
    places = {"cells": cell_at, "depth": depth_at}
    got_w[cell_at] = w_ref[...]
    got_v[cell_at] = v_ref[...]
    greet(cells, depth)

    def ahead(axis, by):
        return {axis: (places[axis] + by) % sizes[axis]}

    started = []

    def start(*args):
        copy = remote(*args)
        copy.start()
        started.append(copy)
        return copy

    half = cells // 2
    base, place = cell_at // half * half, cell_at % half

    def beside(by):
        return base + (place + by) % half

    def from_beside(by):
        return base + (place + half - by) % half

    opposite = (cell_at + half) % cells

    def send_weight(source_cell, order, target):
        piece = got_w.at[source_cell, depth_at]
        return start(piece, piece, w_send.at[0, order], w_recv.at[0, order], {"cells": target})

    origins = {by: from_beside(by) for by in range(1, half)}
    origins[half] = opposite
    for by in range(1, half):
        origins[half + by] = (from_beside(by) + half) % cells
    first = {half: send_weight(cell_at, half, opposite)}
    for by in range(1, half):
        first[by] = send_weight(cell_at, by, beside(by))
    lists = [
        start(
            lists_ref.at[face],
            got_lists.at[face],
            list_send.at[face],
            list_recv.at[face],
            ahead(axis, by),
        )
        for face, (axis, by) in enumerate(faces)
    ]
    vectors = [
        start(v_ref, got_v.at[cell_at], v_send.at[by], v_recv.at[by], ahead("cells", by))
        for by in range(1, cells)
    ]
    order = [half, *range(1, half), *range(half + 1, cells)]
    first[half].wait_recv()
    for by in range(1, half):
        first[half + by] = send_weight(opposite, half + by, beside(by))
    halos = []
    for micro in range(micros):
        for index, (axis, by) in enumerate(sources):
            halos.append(
                start(
                    own_ref.at[micro],
                    halo_refs[index].at[micro],
                    halo_send.at[micro, index],
                    halo_recv.at[micro, index],
                    ahead(axis, by),
                )
            )
        if micro > 0:
            continue
        mate, other = core_mate(depth_at), chip_mate(depth_at)
        across = []
        last = []
        for by in order:
            if by != half:
                first[by].wait_recv()
            piece = got_w.at[origins[by], depth_at]
            across.append(
                start(piece, piece, w_send.at[1, by], w_recv.at[1, by], {"depth": other})
            )
            last.append(
                start(piece, piece, w_send.at[2, by], w_recv.at[2, by], {"depth": mate})
            )
    for at, by in enumerate(order):
        across[at].wait_recv()
        piece = got_w.at[origins[by], other]
        last.append(start(piece, piece, w_send.at[3, by], w_recv.at[3, by], {"depth": mate}))
    for copy in lists + vectors + last + halos:
        copy.wait_recv()
    for copy in started:
        copy.wait_send()


def close_kernel(cells, depth, micros, sources, *refs):
    count = len(sources)
    x_ref, cotx_ref, cotv_ref, gain_ref, gvec_in, part_ref, gown_ref = refs[:7]
    back_refs = refs[7 : 7 + count]
    gx_ref, gvec_ref, summ_ref, sumv_ref = refs[7 + count : 11 + count]
    (
        came,
        one_in,
        two_out,
        two_in,
        three_out,
        three_in,
        four_out,
        four_in,
        held,
        quad,
        octo,
        halo_send,
        halo_recv,
        m_send,
        m_recv,
        c_send,
        c_recv,
        d_send,
        d_recv,
        e_send,
        e_recv,
        f_send,
        f_recv,
    ) = refs[11 + count :]
    cell_at, depth_at = lax.axis_index("cells"), lax.axis_index("depth")
    sizes = {"cells": cells, "depth": depth}
    places = {"cells": cell_at, "depth": depth_at}
    greet(cells, depth)

    def ahead(axis, by):
        return {axis: (places[axis] + by) % sizes[axis]}

    started = []

    def start(*args):
        copy = remote(*args)
        copy.start()
        started.append(copy)
        return copy

    def go_home(micro, piece):
        parts = pl.ds(0, 1) if piece == 0 else pl.ds(1, 3)
        return [
            start(
                back_refs[index].at[micro, parts],
                came.at[micro, index, parts],
                halo_send.at[micro, index, piece],
                halo_recv.at[micro, index, piece],
                ahead(axis, -by),
            )
            for index, (axis, by) in enumerate(sources)
        ]

    mate, other = core_mate(depth_at), chip_mate(depth_at)
    mate_other = chip_mate(mate)
    one_far = start(
        part_ref.at[mate_other], one_in.at[1], m_send.at[0], m_recv.at[0], {"depth": mate}
    )
    one_near = start(part_ref.at[mate], one_in.at[0], m_send.at[1], m_recv.at[1], {"depth": mate})
    scalars = [go_home(micro, 0) for micro in range(micros)]
    vectors = [go_home(0, 1)]
    one_far.wait_recv()
    two_out[...] = (part_ref[other].astype(f32) + one_in[1].astype(f32)).astype(bf16)
    two = start(two_out, two_in, m_send.at[2], m_recv.at[2], {"depth": other})
    one_near.wait_recv()
    two.wait_recv()
    for cell in range(cells):
        total = (
            part_ref[depth_at, cell].astype(f32)
            + one_in[0, cell].astype(f32)
            + two_in[cell].astype(f32)
        )
        three_out[cell] = total.astype(bf16)
    half = cells // 2
    base, place = cell_at // half * half, cell_at % half
    opposite = (cell_at + half) % cells
    three = []
    for by in range(1, half):
        there = base + (place + by) % half
        for side in range(2):
            order = side * half + by
            three.append(
                start(
                    three_out.at[(there + side * half) % cells],
                    three_in.at[order],
                    c_send.at[order],
                    c_recv.at[order],
                    {"cells": there},
                )
            )
    for micro in range(1, micros):
        vectors.append(go_home(micro, 1))

    def back_sum(micro, part):
        total = gown_ref[micro, part]
        for index in range(count):
            total = total + came[micro, index, part].astype(f32)
        return total

    gain = jnp.concatenate([gain_ref[side : side + 1, :].astype(f32) for side in range(2)], axis=1)
    norm_grads = [jnp.zeros((1, gain.shape[1]), f32) for part in range(2)]
    for micro in range(micros):
        for copy in scalars[micro]:
            copy.wait_recv()
        total = back_sum(micro, 0)
        hat, spread = normalise(x_ref[micro])
        norm_grads[0] += jnp.sum(total * hat, axis=0, keepdims=True)
        norm_grads[1] += jnp.sum(total, axis=0, keepdims=True)
        g_hat = total * gain
        g_x = spread * (g_hat - lane_mean(g_hat) - hat * lane_mean(g_hat * hat))
        gx_ref[micro] = cotx_ref[micro] + g_x
    held[...] = gvec_in[...]
    for part in range(2):
        for side in range(2):
            row = 2 * part + side
            held[row : row + 1, :] = norm_grads[part][:, side * LANES : (side + 1) * LANES]
    quad[depth_at] = held[...]
    four = [
        start(held, quad.at[depth_at], d_send.at[by], d_recv.at[by], ahead("depth", by))
        for by in range(1, depth)
    ]

    for copy in three:
        copy.wait_recv()
    sums = [three_out[cell_at].astype(f32), three_out[opposite].astype(f32)]
    for side in range(2):
        for by in range(1, half):
            sums[side] = sums[side] + three_in[side * half + by].astype(f32)
    four_out[...] = sums[1].astype(bf16)
    crossing = start(four_out, four_in, c_send.at[0], c_recv.at[0], {"cells": opposite})
    for copy in four:
        copy.wait_recv()
    total = quad[0]
    for at in range(1, depth):
        total = total + quad[at]
    octo[cell_at] = total
    eight = [
        start(
            octo.at[cell_at],
            octo.at[cell_at],
            f_send.at[by],
            f_recv.at[by],
            ahead("cells", by),
        )
        for by in range(1, cells)
    ]
    crossing.wait_recv()
    summ_ref[depth_at] = sums[0] + four_in[...].astype(f32)
    share = [
        start(
            summ_ref.at[depth_at],
            summ_ref.at[depth_at],
            e_send.at[by],
            e_recv.at[by],
            ahead("depth", by),
        )
        for by in range(1, depth)
    ]
    for micro in range(micros):
        for copy in vectors[micro]:
            copy.wait_recv()
        for axis in range(3):
            gvec_ref[micro, axis] = cotv_ref[micro, axis] + back_sum(micro, 1 + axis)
    for copy in eight:
        copy.wait_recv()
    total = octo[0]
    for cell in range(1, cells):
        total = total + octo[cell]
    sumv_ref[...] = total
    for copy in share:
        copy.wait_recv()
    for copy in started:
        copy.wait_send()


def adam_update(weight, grad, first, second):
    first_new = beta_one * first + (1.0 - beta_one) * grad
    second_new = beta_two * second + (1.0 - beta_two) * grad * grad
    first_hat = first_new / (1.0 - beta_one**STEP)
    second_hat = second_new / (1.0 - beta_two**STEP)
    weight_new = weight - learn_rate * (
        first_hat / (jnp.sqrt(second_hat) + adam_eps) + decay_rate * weight
    )
    return (weight_new, first_new, second_new)


def shards(
    x_in,
    vec_in,
    cot_x,
    cot_vec,
    mats,
    vecs,
    mats_first,
    mats_second,
    vecs_first,
    vecs_second,
    atom_count,
    neighbours,
    edge_mask,
    edge_vec,
    send_list,
):
    micros, atoms, width = x_in.shape
    slots = neighbours.shape[1]
    halo = send_list.shape[-1]
    per_face = halo // LANES
    cells, depth = lax.axis_size("cells"), lax.axis_size("depth")
    faces = [("cells", 1), ("cells", -1), ("cells", FOLD), ("cells", -FOLD), ("depth", 1), ("depth", -1)]
    sizes = {"cells": cells, "depth": depth}
    sources = []
    face_source = []
    for axis, by in faces:
        key = (axis, by % sizes[axis])
        if key not in sources:
            sources.append(key)
        face_source.append(sources.index(key))
    domains = 1 + len(sources)
    buckets = (domains * atoms + ROWS - 1) // ROWS
    block_of = [1 + face_source[row // per_face] for row in range(6 * per_face)]

    whole = pl.BlockSpec(memory_space=pltpu.VMEM)
    scalars = pl.BlockSpec(memory_space=pltpu.SMEM)

    any_space = pl.BlockSpec(memory_space=pl.ANY)
    count = len(sources)
    quarter = mats.shape[0] // LANES // depth
    v_rows = -(-vecs.shape[0] // LANES)
    v_low = jnp.pad(vecs.astype(bf16), (0, v_rows * LANES - vecs.shape[0])).reshape(v_rows, LANES)
    faces_first = jnp.moveaxis(
        send_list.reshape(micros, 6, per_face, LANES), 1, 0
    ).reshape(6, micros * per_face, LANES)

    own, w_low = pl.pallas_call(
        norm_kernel,
        out_shape=(
            jax.ShapeDtypeStruct((micros, 4, atoms, width), bf16),
            jax.ShapeDtypeStruct((depth, quarter, LANES), bf16),
        ),
        in_specs=[whole] * 3,
        out_specs=[whole] * 2,
        name="norm",
    )(x_in, vec_in, mats.reshape(-1, LANES))

    dma = pltpu.SemaphoreType.DMA
    fetched = pl.pallas_call(
        partial(fetch_kernel, cells, depth, micros, sources, faces),
        out_shape=tuple(
            [jax.ShapeDtypeStruct((micros, 4, atoms, width), bf16)] * count
            + [
                jax.ShapeDtypeStruct(faces_first.shape, i32),
                jax.ShapeDtypeStruct((cells, depth, quarter, LANES), bf16),
                jax.ShapeDtypeStruct((cells, v_rows, LANES), bf16),
            ]
        ),
        in_specs=[any_space] + [whole] * 3,
        out_specs=[any_space] * count + [whole] * 3,
        scratch_shapes=[
            dma((micros, count)),
            dma((micros, count)),
            dma((6,)),
            dma((6,)),
            dma((cells,)),
            dma((cells,)),
            dma((4, cells)),
            dma((4, cells)),
        ],
        compiler_params=pltpu.CompilerParams(
            collective_id=0, has_side_effects=True, vmem_limit_bytes=VMEM_LIMIT
        ),
        name="fetch",
    )(own, faces_first, w_low, v_low)
    halos = fetched[:count]
    got_lists, w_all, v_all = fetched[count:]
    list_rows = jnp.moveaxis(
        got_lists.reshape(6, micros, per_face, LANES), 1, 0
    ).reshape(micros, 6 * per_face, LANES)
    v_all = v_all.reshape(cells, v_rows * LANES)[:, : vecs.shape[0]].reshape(-1, LANES)
    w_rows, v_rows = cells * depth * quarter, v_all.shape[0]

    limit = slots * atoms + buckets * (slots // BLOCK_SLOTS) * 8 + buckets * 2 * UNIT
    capacity = (limit + UNIT - 1) // UNIT * UNIT + 4 * UNIT

    def by_micro(array):
        zeros = (0,) * (len(array.shape) - 1)
        return pl.BlockSpec((1,) + tuple(array.shape[1:]), lambda i: (i,) + zeros)

    per_micro = [neighbours, edge_mask, edge_vec, list_rows, x_in, vec_in, cot_x, cot_vec, *halos]
    out_blocks = [
        jax.ShapeDtypeStruct((micros, atoms, width), f32),
        jax.ShapeDtypeStruct((micros, 3, atoms, width), f32),
        jax.ShapeDtypeStruct((micros, 4, atoms, width), f32),
    ] + [jax.ShapeDtypeStruct((micros, 4, atoms, width), bf16)] * count
    results = pl.pallas_call(
        partial(edge_kernel, domains, buckets, block_of),
        out_shape=tuple(
            out_blocks
            + [
                jax.ShapeDtypeStruct((depth, cells, quarter, LANES), bf16),
                jax.ShapeDtypeStruct((v_rows, LANES), f32),
            ]
        ),
        grid=(micros,),
        in_specs=[scalars] + [by_micro(array) for array in per_micro] + [whole] * 2,
        out_specs=[by_micro(block) for block in out_blocks] + [whole] * 2,
        scratch_shapes=[
            pltpu.VMEM((slots, LANES, LANES), bf16),
            pltpu.VMEM((slots, atoms), i32),
            pltpu.VMEM((slots // BLOCK_SLOTS, LANES), i32),
            pltpu.SMEM((slots // BLOCK_SLOTS, LANES), i32),
            pltpu.VMEM((capacity, LANES), f32),
            pltpu.SemaphoreType.DMA(()),
            pltpu.VMEM((w_rows, LANES), f32),
            pltpu.VMEM((11, ROWS, ROWS), bf16),
            pltpu.VMEM((LANES, 4 * ROWS), bf16),
            pltpu.VMEM((buckets * ROWS, ROWS), bf16),
            pltpu.VMEM((buckets, ROWS, 7 * ROWS), bf16),
            pltpu.VMEM((buckets, ROWS, 7 * ROWS), f32),
            pltpu.VMEM((atoms, 5 * ROWS), bf16),
            pltpu.VMEM((3, 3 * atoms, ROWS), f32),
            pltpu.VMEM((3, atoms, ROWS), bf16),
            pltpu.VMEM((atoms, 5 * ROWS), f32),
            pltpu.VMEM((FEATS, 4 * ROWS), f32),
            pltpu.VMEM((ROWS, ROWS), bf16),
        ]
        + [
            scratch
            for scratch in (
                pltpu.VMEM((UNIT, ROWS), bf16),
                pltpu.VMEM((UNIT, LANES), bf16),
                pltpu.VMEM((UNIT, WORK * ROWS), f32),
                pltpu.VMEM((UNIT, LANES), f32),
                pltpu.VMEM((3, UNIT, LANES), f32),
                pltpu.VMEM((2, 2 * UNIT, LANES), bf16),
                pltpu.VMEM((14, UNIT, LANES), bf16),
                pltpu.VMEM((8, UNIT, LANES), bf16),
                pltpu.VMEM((12, UNIT, LANES), bf16),
            )
            for side in range(2)
        ],
        compiler_params=pltpu.CompilerParams(vmem_limit_bytes=VMEM_LIMIT),
        name="edges",
    )(atom_count, *per_micro, w_all, v_all)
    out_x, out_vec, g_own = results[:3]
    backs = results[3 : 3 + count]
    part_m, part_v = results[3 + count :]
    grad_x, grad_vec, sum_mats, sum_vecs = pl.pallas_call(
        partial(close_kernel, cells, depth, micros, sources),
        out_shape=(
            jax.ShapeDtypeStruct(x_in.shape, f32),
            jax.ShapeDtypeStruct(vec_in.shape, f32),
            jax.ShapeDtypeStruct((depth, quarter, LANES), f32),
            jax.ShapeDtypeStruct((v_rows, LANES), f32),
        ),
        in_specs=[whole] * 7 + [any_space] * count,
        out_specs=[whole] * 4,
        scratch_shapes=[
            pltpu.VMEM((micros, count, 4, atoms, width), bf16),
            pltpu.VMEM((2, cells, quarter, LANES), bf16),
            pltpu.VMEM((cells, quarter, LANES), bf16),
            pltpu.VMEM((cells, quarter, LANES), bf16),
            pltpu.VMEM((cells, quarter, LANES), bf16),
            pltpu.VMEM((cells, quarter, LANES), bf16),
            pltpu.VMEM((quarter, LANES), bf16),
            pltpu.VMEM((quarter, LANES), bf16),
            pltpu.VMEM((v_rows, LANES), f32),
            pltpu.VMEM((depth, v_rows, LANES), f32),
            pltpu.VMEM((cells, v_rows, LANES), f32),
            dma((micros, count, 2)),
            dma((micros, count, 2)),
            dma((3,)),
            dma((3,)),
            dma((cells,)),
            dma((cells,)),
            dma((depth,)),
            dma((depth,)),
            dma((depth,)),
            dma((depth,)),
            dma((cells,)),
            dma((cells,)),
        ],
        compiler_params=pltpu.CompilerParams(
            collective_id=1, has_side_effects=True, vmem_limit_bytes=VMEM_LIMIT
        ),
        name="close",
    )(
        x_in,
        cot_x,
        cot_vec,
        v_all,
        part_v,
        part_m,
        g_own,
        *backs,
    )
    sum_mats = sum_mats.reshape(-1)
    sum_vecs = lax.dynamic_slice_in_dim(
        sum_vecs.reshape(-1), lax.axis_index("cells") * vecs.shape[0], vecs.shape[0]
    )
    new_mats, mats_one, mats_two = adam_update(mats, sum_mats, mats_first, mats_second)
    new_vecs, vecs_one, vecs_two = adam_update(vecs, sum_vecs, vecs_first, vecs_second)
    return (
        out_x,
        out_vec,
        grad_x,
        grad_vec,
        sum_mats,
        sum_vecs,
        new_mats,
        new_vecs,
        mats_one,
        mats_two,
        vecs_one,
        vecs_two,
    )


def solution(mesh):
    by_atom = ("cells", "depth")
    shard = P("cells")
    in_specs = (
        P(None, by_atom, None),
        P(None, None, by_atom, None),
        P(None, by_atom, None),
        P(None, None, by_atom, None),
        shard,
        shard,
        shard,
        shard,
        shard,
        shard,
        P(None, by_atom),
        P(None, None, by_atom),
        P(None, None, by_atom),
        P(None, None, None, by_atom),
        P(None, by_atom, None),
    )
    out_specs = (
        P(None, by_atom, None),
        P(None, None, by_atom, None),
        P(None, by_atom, None),
        P(None, None, by_atom, None),
    ) + (shard,) * 8
    return jax.shard_map(shards, mesh=mesh, in_specs=in_specs, out_specs=out_specs, check_vma=False)
```

```python
from functools import partial
import math

import jax
import jax.numpy as jnp
from jax import lax
from jax.experimental import pallas as pl
from jax.experimental.pallas import tpu as pltpu
from jax.sharding import PartitionSpec as P

HEADS = 8
NR = 32
FOLD = 4
STEP = 3

LANES = 128
ROWS = 256
UNIT = 256
BLOCK_SLOTS = 4
TILES = ((0.3, 192), (0.625, 128), (1.0, 80))

norm_eps = 1e-05
cut_radius = 5.0
beta_one = 0.5
beta_two = 0.5
learn_rate = 0.05
decay_rate = 0.01
adam_eps = 1e-08

f32 = jnp.float32
bf16 = jnp.bfloat16
i32 = jnp.int32

VMEM_LIMIT = 60 * 1024 * 1024


def dot_nn(left, right):
    return lax.dot_general(left, right, (((1,), (0,)), ((), ())), preferred_element_type=f32)


def dot_nt(left, right):
    return lax.dot_general(left, right, (((1,), (1,)), ((), ())), preferred_element_type=f32)


def dot_tn(left, right):
    return lax.dot_general(left, right, (((0,), (0,)), ((), ())), preferred_element_type=f32)


def lane_mean(block):
    return jnp.sum(block, axis=-1, keepdims=True) * (1.0 / block.shape[-1])


def normalise(block):
    centered = block - lane_mean(block)
    spread = lax.rsqrt(lane_mean(centered * centered) + norm_eps)
    return centered * spread, spread


def norm_kernel(x_ref, vec_ref, mats_ref, list_ref, own_ref, low_ref, lists_ref):
    micros, faces, halo = list_ref.shape
    per_face = halo // LANES
    for face in range(faces):
        for row in range(micros * per_face):
            lanes = slice(row % per_face * LANES, (row % per_face + 1) * LANES)
            lists_ref[face, row : row + 1, :] = list_ref[row // per_face, face : face + 1, lanes]
    quarter = low_ref.shape[1]
    for part in range(low_ref.shape[0]):
        low_ref[part] = mats_ref[part * quarter : (part + 1) * quarter, :].astype(bf16)
    for micro in range(x_ref.shape[0]):
        own_ref[micro, 0] = normalise(x_ref[micro])[0].astype(bf16)
        own_ref[micro, 1:] = vec_ref[micro].astype(bf16)


Q_AT, K_AT, V_AT, VEC_AT, O_AT, DK_AT, DV_AT = 0, 512, 1024, 2560, 4096, 5632, 5696
W_Q, W_K, W_V, W_VEC, W_O = 0, 1, 2, 5, 8
FEATS = 48
CHUNK = 16
GATH, PER_ATOM, FILT, SUMS, KEPT, WORK = 0, 7, 12, 16, 18, 24


def edge_features(nbr, mask, geom, lists, block_of, buckets, feat, place, count_vec):
    slots, atoms = nbr.shape
    blocks = slots // BLOCK_SLOTS
    live = mask > 0
    halo_at = nbr - atoms
    list_row = halo_at >> 7
    list_lane = halo_at & (LANES - 1)
    atom_in = nbr
    block_id = jnp.zeros_like(nbr)
    for row, picks in enumerate(lists):
        table = jnp.broadcast_to(picks, (slots, atoms))
        picked = jnp.take_along_axis(table, list_lane, axis=1)
        here = list_row == row
        atom_in = jnp.where(here, picked, atom_in)
        block_id = jnp.where(here, block_of[row], block_id)
    entry = block_id * atoms + atom_in
    bucket = entry >> 8
    low = ((entry & (ROWS - 1)) + 1).astype(f32)
    atom_id = (lax.broadcasted_iota(i32, (slots, atoms), 1) + 1).astype(f32)
    live_float = live.astype(f32)

    radius = jnp.sqrt(geom[0] * geom[0] + geom[1] * geom[1] + geom[2] * geom[2])
    units = [comp / radius for comp in geom]
    cut = 0.5 * (jnp.cos(math.pi * radius / cut_radius) + 1.0) * live_float
    cut_high = cut.astype(bf16).astype(f32)
    cut_low = cut - cut_high
    decayed = jnp.exp(-(5.0 / cut_radius) * radius)
    start_value = math.exp(-cut_radius)
    ramp = lax.broadcasted_iota(i32, (NR, 1), 0).astype(f32) / float(NR - 1)
    centers = start_value * (1.0 - ramp) + ramp
    width_coef = (2.0 / NR * (1.0 - start_value)) ** (-2)
    extras = [live_float, low, atom_id, cut_high, cut_low] + units
    zeros = jnp.zeros((16 - len(extras), atoms), f32)
    for slot in range(slots):
        gap = decayed[slot : slot + 1, :] - centers
        basis = cut[slot : slot + 1, :] * jnp.exp(-width_coef * gap * gap)
        feat[slot, 0:NR, :] = basis.astype(bf16)
        rows = [extra[slot : slot + 1, :] for extra in extras] + [zeros]
        feat[slot, NR : NR + 16, :] = jnp.concatenate(rows, axis=0).astype(bf16)

    members = [jnp.where(live & (bucket == b), 1.0, 0.0) for b in range(buckets)]
    lane_from = lax.broadcasted_iota(i32, (atoms, 2 * atoms), 0)
    lane_to = lax.broadcasted_iota(i32, (atoms, 2 * atoms), 1)
    before = jnp.where((lane_from < lane_to) | (lane_to >= atoms), 1.0, 0.0).astype(bf16)
    slot_to = lax.broadcasted_iota(i32, (slots, slots), 0)
    slot_from = lax.broadcasted_iota(i32, (slots, slots), 1)
    same = (slot_to // BLOCK_SLOTS) == (slot_from // BLOCK_SLOTS)
    earlier = jnp.where(same & (slot_from < slot_to), 1.0, 0.0).astype(bf16)
    block_row = lax.broadcasted_iota(i32, (blocks, slots), 0)
    block_slot = lax.broadcasted_iota(i32, (blocks, slots), 1)
    gather_block = jnp.where(block_slot // BLOCK_SLOTS == block_row, 1.0, 0.0).astype(bf16)
    lane = lax.broadcasted_iota(i32, (blocks, LANES), 1)
    rank = jnp.zeros((slots, atoms), f32)
    counts = jnp.zeros((blocks, LANES), f32)
    for b in range(buckets):
        sums = dot_nn(members[b].astype(bf16), before)
        row_total = sums[:, atoms:].astype(bf16)
        offset = sums[:, :atoms] + dot_nn(earlier, row_total)
        rank = jnp.where(members[b] > 0.0, offset, rank)
        counts = jnp.where(lane == b, dot_nn(gather_block, row_total), counts)
    place[...] = jnp.where(live, bucket * 1024 + rank.astype(i32), -1)
    count_vec[...] = counts.astype(i32)


def pack_edges(blocks, atoms, buckets, feat, place, count_sc, packed):
    wide = BLOCK_SLOTS * atoms

    def total_body(block, totals):
        return tuple(
            total + (((count_sc[block, b] + 7) >> 3) << 3) for b, total in enumerate(totals)
        )

    totals = lax.fori_loop(0, blocks, total_body, (jnp.int32(0),) * buckets)
    held = [(total + (UNIT - 1)) >> 8 for total in totals]
    bases = [jnp.int32(UNIT)]
    for total in totals:
        bases.append(bases[-1] + (((total + (2 * UNIT - 1)) >> 8) << 8))

    def picks(places, b, first, tile):
        wanted = lax.broadcasted_iota(i32, (tile, wide), 0) + (b * 1024 + first)
        return jnp.where(places == wanted, 1.0, 0.0).astype(bf16)

    def places_of(block):
        rows = [place[pl.ds(block * BLOCK_SLOTS + t, 1), :] for t in range(BLOCK_SLOTS)]
        return jnp.concatenate(rows, axis=1)

    def feats_of(block):
        parts = [feat[block * BLOCK_SLOTS + t] for t in range(BLOCK_SLOTS)]
        return jnp.concatenate(parts, axis=1)

    def padded(block, b):
        return ((count_sc[block, b] + 7) >> 3) << 3

    def block_body(size, block, at):
        places = places_of(block)
        feats = feats_of(block)
        for b in range(buckets):
            made = dot_nt(picks(places, b, 0, size), feats)
            packed[pl.ds(pl.multiple_of(at[b], 8), size), :] = made
        return tuple(at[b] + padded(block, b) for b in range(buckets))

    def rest_body(size, block, at):
        for b in range(buckets):
            rows = padded(block, b)

            @pl.when(rows > size)
            def _(b=b, rows=rows):
                def tile_body(tile, carry):
                    first = jnp.minimum(tile * size, rows - size)
                    pick = picks(places_of(block), b, first, size)
                    start = pl.multiple_of(at[b] + first, 8)
                    packed[pl.ds(start, size), :] = dot_nt(pick, feats_of(block))
                    return carry

                lax.fori_loop(1, (rows + (size - 1)) // size, tile_body, 0)

        return tuple(at[b] + padded(block, b) for b in range(buckets))

    begin = 0
    ends = tuple(bases[:buckets])
    for share, size in TILES:
        until = int(blocks * share)
        ends = lax.fori_loop(begin, until, partial(block_body, size), ends, unroll=2)
        begin = until
    begin = 0
    ends = tuple(bases[:buckets])
    for share, size in TILES:
        until = int(blocks * share)
        ends = lax.fori_loop(begin, until, partial(rest_body, size), ends)
        begin = until
    zeros = jnp.zeros((UNIT, LANES), f32)
    for end in ends:
        packed[pl.ds(pl.multiple_of(end, 8), UNIT), :] = zeros
    packed[0:UNIT, :] = zeros
    return held, bases


def edge_kernel(domains, buckets, block_of, *refs):
    refs = list(refs)
    count_ref, list_ref, nbr_ref, mask_ref, geom_ref, x_ref, vec_ref, cotx_ref, cotv_ref = refs[:9]
    halo_refs = refs[9 : 9 + domains - 1]
    at = 9 + domains - 1
    w_ref, v_ref = refs[at : at + 2]
    at += 2
    outx_ref, outv_ref, gown_ref = refs[at : at + 3]
    at += 3
    back_refs = refs[at : at + domains - 1]
    at += domains - 1
    gm_ref, gv_ref = refs[at : at + 2]
    at += 2
    (
        feat,
        place,
        count_vec,
        count_sc,
        packed,
        sem,
        wide_w,
        wb,
        wd,
        norm_table,
        tab,
        acc,
        atom_tab,
        proj,
        go,
        agg,
        gwd,
        heads,
    ) = refs[at : at + 18]
    rest = refs[at + 18 :]
    sides = [tuple(rest[side::2]) for side in range(2)]
    micro = pl.program_id(0)
    slots, atoms = nbr_ref.shape[1:]
    feat_width = x_ref.shape[2]
    cells, parts_w, quarter = w_ref.shape[:3]
    parts = [slice(axis * atoms, (axis + 1) * atoms) for axis in range(3)]

    def vector(index):
        both = [v_ref[2 * index + half : 2 * index + half + 1, :].astype(f32) for half in range(2)]
        return jnp.concatenate(both, axis=1)

    @pl.when(micro == 0)
    def _():
        feat[...] = jnp.zeros_like(feat)
        for ref in sides[1][6:]:
            ref[...] = jnp.zeros_like(ref)
        gwd[...] = jnp.zeros_like(gwd)
        for cell in range(cells):
            for part in range(parts_w):
                start = (cell * parts_w + part) * quarter
                wide_w[start : start + quarter, :] = w_ref[cell, part].astype(f32)

        def weight_block(first, stride, column, rows):
            halves = [
                wide_w[pl.ds(first + 2 * column + half, rows, stride=stride), :]
                for half in range(2)
            ]
            return jnp.concatenate(halves, axis=1)

        for slot, first, stride, count in (
            (W_Q, Q_AT, 2, 1),
            (W_K, K_AT, 2, 1),
            (W_V, V_AT, 6, 3),
            (W_VEC, VEC_AT, 6, 3),
            (W_O, O_AT, 6, 3),
        ):
            for column in range(count):
                wb[slot + column] = weight_block(first, stride, column, ROWS).astype(bf16)
        bias_row = lax.broadcasted_iota(i32, (LANES - NR, 1), 0) == 0
        for column in range(4):
            if column == 0:
                block = weight_block(DK_AT, 2, 0, NR)
            else:
                block = weight_block(DV_AT, 6, column - 1, NR)
            bias = jnp.where(bias_row, vector(10 + column), 0.0)
            cols = slice(column * ROWS, (column + 1) * ROWS)
            wd[:, cols] = (jnp.concatenate([block, bias], axis=0) * 0.5).astype(bf16)
        head_from = lax.broadcasted_iota(i32, (ROWS, ROWS), 0) // (feat_width // HEADS)
        head_to = lax.broadcasted_iota(i32, (ROWS, ROWS), 1) // (feat_width // HEADS)
        heads[...] = jnp.where(head_from == head_to, 0.5, 0.0).astype(bf16)

    geom = [geom_ref[0, axis] for axis in range(3)]
    per_face = len(block_of) // list_ref.shape[0]
    lists = [
        list_ref[face, pl.ds(micro * per_face + row, 1), :]
        for face in range(list_ref.shape[0])
        for row in range(per_face)
    ]
    edge_features(
        nbr_ref[0], mask_ref[0], geom, lists, block_of, buckets, feat, place, count_vec
    )
    copy = pltpu.make_async_copy(count_vec, count_sc, sem)
    copy.start()

    gain = vector(0)
    shift = vector(1)
    own_hat, unused = normalise(x_ref[0])
    vec_low = vec_ref[0].astype(bf16)
    for domain in range(2 * buckets):
        rows = slice(domain * atoms, (domain + 1) * atoms)
        here = slice((domain % 2) * atoms, (domain % 2 + 1) * atoms)
        if domain == 0:
            norm_table[rows, :] = (own_hat * gain + shift).astype(bf16)
        elif domain < domains:
            hat = halo_refs[domain - 1][0, 0].astype(f32)
            norm_table[rows, :] = (hat * gain + shift).astype(bf16)
        else:
            norm_table[rows, :] = jnp.zeros((atoms, feat_width), bf16)
        for axis in range(3):
            cols = slice((4 + axis) * ROWS, (5 + axis) * ROWS)
            if domain < domains:
                block = vec_low[axis] if domain == 0 else halo_refs[domain - 1][0, 1 + axis]
            else:
                block = jnp.zeros((atoms, feat_width), bf16)
            tab[domain // 2, here, cols] = block
    for b in range(buckets):
        rows = slice(b * ROWS, (b + 1) * ROWS)
        for column in range(4):
            cols = slice(column * ROWS, (column + 1) * ROWS)
            made = dot_nn(norm_table[rows, :], wb[W_K + column]) + vector(3 + column)
            tab[b, :, cols] = made.astype(bf16)

    live = (lax.broadcasted_iota(i32, (atoms, 1), 0) < count_ref[micro, 0]).astype(f32)
    query = dot_nn(norm_table[0:atoms, :], wb[W_Q]) + vector(2)
    atom_tab[:, 0:ROWS] = query.astype(bf16)
    vec_rows = vec_low.reshape(3 * atoms, feat_width)
    for part in range(3):
        proj[part] = dot_nn(vec_rows, wb[W_VEC + part])
    cot_x = cotx_ref[0] * live
    vec_dot = jnp.zeros((atoms, feat_width), f32)
    go_one = jnp.zeros((atoms, feat_width), f32)
    for axis in range(3):
        cot_v = cotv_ref[0, axis] * live
        vec_dot += proj[0, parts[axis], :] * proj[1, parts[axis], :]
        go_one += proj[2, parts[axis], :] * cot_v
        atom_tab[:, (2 + axis) * ROWS : (3 + axis) * ROWS] = cot_v.astype(bf16)
    go[0] = go_one.astype(bf16)
    go[1] = (vec_dot * cot_x).astype(bf16)
    go[2] = cot_x.astype(bf16)
    g_agg = dot_nt(go[0], wb[W_O])
    for part in range(1, 3):
        g_agg += dot_nt(go[part], wb[W_O + part])
    atom_tab[:, ROWS : 2 * ROWS] = g_agg.astype(bf16)
    agg[...] = jnp.zeros_like(agg)
    for b in range(buckets):
        acc[b] = jnp.zeros((ROWS, 7 * ROWS), f32)

    copy.wait()
    held, bases = pack_edges(
        slots // BLOCK_SLOTS, atoms, buckets, feat, place, count_sc, packed
    )
    firsts = [jnp.int32(0)]
    for number in held:
        firsts.append(firsts[-1] + number)
    total_units = firsts[-1]

    def bucket_of(unit):
        b = jnp.int32(0)
        for at in range(1, buckets):
            b = b + jnp.where(unit >= firsts[at], 1, 0)
        return b

    def rows_of(unit):
        start = jnp.int32(0)
        for at in range(buckets):
            inside = (unit >= firsts[at]) & (unit < firsts[at + 1])
            start = jnp.where(inside, bases[at] + (unit - firsts[at]) * UNIT, start)
        return pl.ds(pl.multiple_of(start, UNIT), UNIT)

    def block_cols(block):
        return slice(block * ROWS, (block + 1) * ROWS)

    def hits(side, rows):
        hit, atom_one = side[:2]
        full = packed[rows, :]
        lane_row = lax.broadcasted_iota(i32, (UNIT, ROWS), 1).astype(f32) + 1.0
        lane_atom = lax.broadcasted_iota(i32, (UNIT, LANES), 1).astype(f32) + 1.0
        hit[...] = jnp.where(full[:, NR + 1 : NR + 2] == lane_row, 1.0, 0.0).astype(bf16)
        atom_one[...] = jnp.where(full[:, NR + 2 : NR + 3] == lane_atom, 1.0, 0.0).astype(bf16)

    def spread(side, rows):
        cutb, dirs = side[3:5]
        full = packed[rows, :]
        for axis in range(3):
            column = full[:, NR + 5 + axis : NR + 6 + axis]
            dirs[axis] = jnp.broadcast_to(column, (UNIT, LANES))
        column = full[:, NR + 3 : NR + 4] + full[:, NR + 4 : NR + 5]
        cutb[...] = jnp.broadcast_to(column, (UNIT, LANES))

    def gather_steps(side, unit):
        hit, atom_one, work = side[:3]
        b = jnp.minimum(bucket_of(unit), buckets - 1)
        rows = rows_of(unit)

        def gather_table(block):
            work[:, block_cols(GATH + block)] = dot_nn(hit[...], tab[b, :, block_cols(block)])

        def gather_atom(block):
            made = dot_nn(atom_one[...], atom_tab[:, block_cols(block)])
            work[:, block_cols(PER_ATOM + block)] = made

        def filters(block):
            low = packed[rows, :].astype(bf16)
            work[:, block_cols(FILT + block)] = dot_nn(low, wd[:, block_cols(block)])

        return (
            [partial(gather_table, block) for block in range(7)]
            + [partial(gather_atom, block) for block in range(5)]
            + [partial(filters, block) for block in range(4)]
        )

    def mix(first, second):
        done = 0
        for at, step in enumerate(first):
            step()
            until = (at + 1) * len(second) // len(first)
            for other in second[done:until]:
                other()
            done = until

    chunks = [
        (slice(start, start + CHUNK), half)
        for start in range(0, UNIT, CHUNK)
        for half in range(2)
    ]

    def put(ref, block, here, half, value):
        ref[2 * block + half, here, :] = value.astype(bf16)

    def reader(work):
        def part(block, here, half):
            start = block * ROWS + half * LANES
            return work[here, start : start + LANES]

        def gate(here, block, half):
            value = part(FILT + block, here, half)
            turn = jnp.tanh(value)
            lift = 1.0 + turn
            silu = value * lift
            return silu, lift + silu * (1.0 - turn)

        return part, gate

    def heads_stage(side, here, half):
        work, pair = side[2], side[5]
        part, gate = reader(work)

        def keep(block, value):
            start = (KEPT + block) * ROWS + half * LANES
            work[here, start : start + LANES] = value

        there = slice(UNIT + here.start, UNIT + here.stop)
        silu, slope = gate(here, 0, half)
        query_e = part(PER_ATOM, here, half)
        key_e = part(GATH, here, half)
        gated = query_e * silu
        keep(0, gated)
        keep(1, query_e * key_e * slope)
        keep(2, key_e * silu)
        pair[half, here, :] = (gated * key_e).astype(bf16)
        silu, slope = gate(here, 1, half)
        cot_e = part(PER_ATOM + 1, here, half)
        value_e = part(GATH + 1, here, half)
        gated = value_e * silu
        keep(3, cot_e * silu)
        keep(4, cot_e * value_e * slope)
        keep(5, gated)
        pair[half, there, :] = (cot_e * gated).astype(bf16)

    def head_sums(side):
        work, pair = side[2], side[5]
        for at in range(2):
            rows = slice(at * UNIT, (at + 1) * UNIT)
            both = jnp.concatenate([pair[0, rows, :], pair[1, rows, :]], axis=1)
            work[:, block_cols(SUMS + at)] = dot_nn(both, heads[...])

    def vector_stage(side, here, half):
        dirs, dedge, dfilt, msg = side[4], *side[6:]
        part, gate = reader(side[2])
        cots = [part(PER_ATOM + 2 + axis, here, half) for axis in range(3)]
        vecs = [part(GATH + 4 + axis, here, half) for axis in range(3)]
        turns = [dirs[axis, here, :] for axis in range(3)]
        silu, slope = gate(here, 2, half)
        value_e = part(GATH + 2, here, half)
        gated = value_e * silu
        down = cots[0] * vecs[0] + cots[1] * vecs[1] + cots[2] * vecs[2]
        for axis in range(3):
            put(msg, 1 + axis, here, half, vecs[axis] * gated)
            put(dedge, 4 + axis, here, half, cots[axis] * gated)
        put(dedge, 2, here, half, down * silu)
        put(dfilt, 2, here, half, down * value_e * slope)
        silu, slope = gate(here, 3, half)
        value_e = part(GATH + 3, here, half)
        down = cots[0] * turns[0] + cots[1] * turns[1] + cots[2] * turns[2]
        put(dedge, 3, here, half, down * silu)
        put(dfilt, 3, here, half, down * value_e * slope)
        put(msg, 5, here, half, value_e * silu)

    def score_stage(side, here, half):
        cutb, dedge, dfilt, msg = side[3], *side[6:]
        part, unused = reader(side[2])
        cut = cutb[here, :]
        score = part(SUMS, here, half)
        turn = jnp.tanh(score)
        lift = 1.0 + turn
        silu = score * lift
        attention = silu * cut
        dscore = part(SUMS + 1, here, half) * cut * (lift + silu * (1.0 - turn))
        put(dedge, 0, here, half, dscore * part(KEPT, here, half))
        put(dfilt, 0, here, half, dscore * part(KEPT + 1, here, half))
        put(msg, 4, here, half, dscore * part(KEPT + 2, here, half))
        put(dedge, 1, here, half, attention * part(KEPT + 3, here, half))
        put(dfilt, 1, here, half, attention * part(KEPT + 4, here, half))
        put(msg, 0, here, half, attention * part(KEPT + 5, here, half))

    def both_halves(ref, block):
        return jnp.concatenate([ref[2 * block], ref[2 * block + 1]], axis=1)

    def scatter_steps(side, unit):
        dedge, dfilt, msg = side[6:]
        b = jnp.minimum(bucket_of(unit), buckets - 1)
        turned = packed[rows_of(unit), :].T

        def across(index):
            return turned[NR + index : NR + index + 1, :]

        sub_row = lax.broadcasted_iota(i32, (ROWS, UNIT), 0).astype(f32) + 1.0
        sub_atom = lax.broadcasted_iota(i32, (atoms, UNIT), 0).astype(f32) + 1.0
        hit_t = jnp.where(across(1) == sub_row, 1.0, 0.0).astype(bf16)
        atom_hit = across(2) == sub_atom
        atom_t = jnp.where(atom_hit, 1.0, 0.0).astype(bf16)
        feats_t = turned[0:FEATS, :].astype(bf16)
        turn = both_halves(msg, 5)

        def add_vector(axis):
            along = jnp.where(atom_hit, across(5 + axis), 0.0).astype(bf16)
            agg[:, block_cols(1 + axis)] += dot_nn(
                jnp.concatenate([atom_t, along], axis=1),
                jnp.concatenate([both_halves(msg, 1 + axis), turn], axis=0),
            )

        def add_table(block):
            acc[b, :, block_cols(block)] += dot_nn(hit_t, both_halves(dedge, block))

        def add_filter(block):
            gwd[:, block_cols(block)] += dot_nn(feats_t, both_halves(dfilt, block))

        def add_atom(block):
            agg[:, block_cols(block)] += dot_nn(atom_t, both_halves(msg, block))

        return (
            [partial(add_vector, axis) for axis in range(3)]
            + [partial(add_table, block) for block in (2, 3, 4, 5, 6, 0, 1)]
            + [partial(add_filter, block) for block in (2, 3, 0, 1)]
            + [partial(add_atom, block) for block in (0, 4)]
        )

    def on_chunks(stage, side):
        return [partial(stage, side, here, half) for here, half in chunks]

    hits(sides[0], rows_of(jnp.int32(0)))
    mix(gather_steps(sides[0], jnp.int32(0)), [])

    def pair_body(step, carry):
        for at in range(2):
            unit = 2 * step + at
            mine, other = sides[at], sides[1 - at]

            @pl.when(count_sc[0, 0] >= 0)
            def _(unit=unit, mine=mine, other=other):
                spread(mine, rows_of(unit))
                hits(other, rows_of(unit + 1))
                mix(scatter_steps(other, unit - 1), on_chunks(heads_stage, mine))

            @pl.when(count_sc[0, 0] >= 0)
            def _(unit=unit, mine=mine, other=other):
                head_sums(mine)
                mix(
                    gather_steps(other, unit + 1),
                    [step for two in zip(on_chunks(vector_stage, mine), on_chunks(score_stage, mine)) for step in two],
                )

        return carry

    steps = (total_units + 1) // 2
    lax.fori_loop(0, steps, pair_body, 0)
    mix(scatter_steps(sides[1], 2 * steps - 1), [])

    agg_low = agg[:, 0:ROWS].astype(bf16)
    outs = [dot_nn(agg_low, wb[W_O + part]) + vector(7 + part) for part in range(3)]
    outx_ref[0] = x_ref[0] + (vec_dot * outs[1] + outs[2]) * live
    g_dot = cot_x * outs[1]
    for axis in range(3):
        rows = parts[axis]
        vec_agg = agg[:, block_cols(1 + axis)]
        outv_ref[0, axis] = vec_ref[0, axis] + (proj[2, rows, :] * outs[0] + vec_agg) * live
        proj[2, rows, :] = cotv_ref[0, axis] * live * outs[0]
        first_part = proj[0, rows, :]
        proj[0, rows, :] = g_dot * proj[1, rows, :]
        proj[1, rows, :] = g_dot * first_part

    later = micro > 0

    def put_grad(first, stride, column, rows, value):
        for half in range(2):
            at = pl.ds(first + 2 * column + half, rows, stride=stride)
            before = jnp.where(later, wide_w[at, :], 0.0)
            wide_w[at, :] = value[:, half * LANES : (half + 1) * LANES] + before

    def put_vector(index, value):
        for half in range(2):
            row = slice(2 * index + half, 2 * index + half + 1)
            before = jnp.where(later, gv_ref[row, :], 0.0)
            gv_ref[row, :] = value[:, half * LANES : (half + 1) * LANES] + before

    def column_sum(value):
        return jnp.sum(value.astype(f32), axis=0, keepdims=True)

    put_vector(0, jnp.zeros((1, ROWS), f32))
    put_vector(1, jnp.zeros((1, ROWS), f32))
    g_vec = jnp.zeros((3 * atoms, feat_width), f32)
    for part_at in range(3):
        put_grad(O_AT, 6, part_at, ROWS, dot_tn(agg_low, go[part_at]))
        put_vector(7 + part_at, column_sum(go[part_at]))
        gp = proj[part_at].astype(bf16)
        put_grad(VEC_AT, 6, part_at, ROWS, dot_tn(vec_rows, gp))
        g_vec += dot_nt(gp, wb[W_VEC + part_at])

    g_query = agg[:, block_cols(4)].astype(bf16)
    put_grad(Q_AT, 2, 0, ROWS, dot_tn(norm_table[0:atoms, :], g_query))
    put_vector(2, column_sum(g_query))
    g_norm = dot_nt(g_query, wb[W_Q])

    sums = [jnp.zeros((ROWS, ROWS), f32) for column in range(4)]
    biases = [jnp.zeros((1, ROWS), f32) for column in range(4)]
    for b in range(buckets):
        rows = slice(b * ROWS, (b + 1) * ROWS)
        g_table = jnp.zeros((ROWS, ROWS), f32)
        for column in range(4):
            low = acc[b, :, block_cols(column)].astype(bf16)
            sums[column] += dot_tn(norm_table[rows, :], low)
            biases[column] += column_sum(low)
            g_table += dot_nt(low, wb[W_K + column])
        for half in range(2):
            domain = 2 * b + half
            if domain >= domains:
                continue
            here = slice(half * atoms, (half + 1) * atoms)
            if domain == 0:
                gown_ref[0, 0] = g_table[here, :] + g_norm
            else:
                back_refs[domain - 1][0, 0] = g_table[here, :].astype(bf16)
            for axis in range(3):
                block = acc[b, here, block_cols(4 + axis)]
                if domain == 0:
                    gown_ref[0, 1 + axis] = block + g_vec[parts[axis], :]
                else:
                    back_refs[domain - 1][0, 1 + axis] = block.astype(bf16)
    for column in range(4):
        if column == 0:
            put_grad(K_AT, 2, 0, ROWS, sums[column])
        else:
            put_grad(V_AT, 6, column - 1, ROWS, sums[column])
        put_vector(3 + column, biases[column])

    @pl.when(micro == pl.num_programs(0) - 1)
    def _():
        for column in range(4):
            block = gwd[0:NR, block_cols(column)] * 0.5
            first, stride, at = (DK_AT, 2, 0) if column == 0 else (DV_AT, 6, column - 1)
            for half in range(2):
                cols = slice(half * LANES, (half + 1) * LANES)
                wide_w[pl.ds(first + 2 * at + half, NR, stride=stride), :] = block[:, cols]
                row = 2 * (10 + column) + half
                bias = gwd[NR : NR + 1, column * ROWS + half * LANES :][:, :LANES]
                gv_ref[row : row + 1, :] = bias * 0.5
        for cell in range(cells):
            for part_at in range(parts_w):
                start = (cell * parts_w + part_at) * quarter
                gm_ref[part_at, cell] = wide_w[start : start + quarter, :].astype(bf16)


def core_mate(depth_at):
    return depth_at + 1 - 2 * (depth_at % 2)


def chip_mate(depth_at):
    return (depth_at + 2) % 4


def greet(cells, depth):
    barrier = pltpu.get_barrier_semaphore()
    cell_at, depth_at = lax.axis_index("cells"), lax.axis_index("depth")
    for by in range(1, cells):
        pl.semaphore_signal(barrier, inc=1, device_id={"cells": (cell_at + by) % cells})
    for by in range(1, depth):
        pl.semaphore_signal(barrier, inc=1, device_id={"depth": (depth_at + by) % depth})
    pl.semaphore_wait(barrier, cells + depth - 2)


def remote(source, target, send, receive, device):
    return pltpu.make_async_remote_copy(
        src_ref=source, dst_ref=target, send_sem=send, recv_sem=receive, device_id=device
    )


def fetch_kernel(cells, depth, micros, sources, faces, *refs):
    own_ref, lists_ref, w_ref, v_ref = refs[:4]
    halo_refs = refs[4 : 4 + len(sources)]
    got_lists, got_w, got_v = refs[4 + len(sources) : 7 + len(sources)]
    (
        halo_send,
        halo_recv,
        list_send,
        list_recv,
        v_send,
        v_recv,
        w_send,
        w_recv,
    ) = refs[7 + len(sources) :]
    cell_at, depth_at = lax.axis_index("cells"), lax.axis_index("depth")
    sizes = {"cells": cells, "depth": depth}
    places = {"cells": cell_at, "depth": depth_at}
    got_w[cell_at] = w_ref[...]
    got_v[cell_at] = v_ref[...]
    greet(cells, depth)

    def ahead(axis, by):
        return {axis: (places[axis] + by) % sizes[axis]}

    started = []

    def start(*args):
        copy = remote(*args)
        copy.start()
        started.append(copy)
        return copy

    half = cells // 2
    base, place = cell_at // half * half, cell_at % half

    def beside(by):
        return base + (place + by) % half

    def from_beside(by):
        return base + (place + half - by) % half

    opposite = (cell_at + half) % cells

    def send_weight(source_cell, order, target):
        piece = got_w.at[source_cell, depth_at]
        return start(piece, piece, w_send.at[0, order], w_recv.at[0, order], {"cells": target})

    origins = {by: from_beside(by) for by in range(1, half)}
    origins[half] = opposite
    for by in range(1, half):
        origins[half + by] = (from_beside(by) + half) % cells
    first = {half: send_weight(cell_at, half, opposite)}
    for by in range(1, half):
        first[by] = send_weight(cell_at, by, beside(by))
    lists = [
        start(
            lists_ref.at[face],
            got_lists.at[face],
            list_send.at[face],
            list_recv.at[face],
            ahead(axis, by),
        )
        for face, (axis, by) in enumerate(faces)
    ]
    vectors = [
        start(v_ref, got_v.at[cell_at], v_send.at[by], v_recv.at[by], ahead("cells", by))
        for by in range(1, cells)
    ]
    order = [half, *range(1, half), *range(half + 1, cells)]
    first[half].wait_recv()
    for by in range(1, half):
        first[half + by] = send_weight(opposite, half + by, beside(by))
    halos = []
    for micro in range(micros):
        for index, (axis, by) in enumerate(sources):
            halos.append(
                start(
                    own_ref.at[micro],
                    halo_refs[index].at[micro],
                    halo_send.at[micro, index],
                    halo_recv.at[micro, index],
                    ahead(axis, by),
                )
            )
        if micro > 0:
            continue
        mate, other = core_mate(depth_at), chip_mate(depth_at)
        across = []
        last = []
        for by in order:
            if by != half:
                first[by].wait_recv()
            piece = got_w.at[origins[by], depth_at]
            across.append(
                start(piece, piece, w_send.at[1, by], w_recv.at[1, by], {"depth": other})
            )
            last.append(
                start(piece, piece, w_send.at[2, by], w_recv.at[2, by], {"depth": mate})
            )
    for at, by in enumerate(order):
        across[at].wait_recv()
        piece = got_w.at[origins[by], other]
        last.append(start(piece, piece, w_send.at[3, by], w_recv.at[3, by], {"depth": mate}))
    for copy in lists + vectors + last + halos:
        copy.wait_recv()
    for copy in started:
        copy.wait_send()


def close_kernel(cells, depth, micros, sources, *refs):
    count = len(sources)
    x_ref, cotx_ref, cotv_ref, gain_ref, gvec_in, part_ref, gown_ref = refs[:7]
    back_refs = refs[7 : 7 + count]
    gx_ref, gvec_ref, summ_ref, sumv_ref = refs[7 + count : 11 + count]
    (
        came,
        one_in,
        two_out,
        two_in,
        three_out,
        three_in,
        four_out,
        four_in,
        held,
        quad,
        octo,
        halo_send,
        halo_recv,
        m_send,
        m_recv,
        c_send,
        c_recv,
        d_send,
        d_recv,
        e_send,
        e_recv,
        f_send,
        f_recv,
    ) = refs[11 + count :]
    cell_at, depth_at = lax.axis_index("cells"), lax.axis_index("depth")
    sizes = {"cells": cells, "depth": depth}
    places = {"cells": cell_at, "depth": depth_at}
    greet(cells, depth)

    def ahead(axis, by):
        return {axis: (places[axis] + by) % sizes[axis]}

    started = []

    def start(*args):
        copy = remote(*args)
        copy.start()
        started.append(copy)
        return copy

    def go_home(micro, piece):
        parts = pl.ds(0, 1) if piece == 0 else pl.ds(1, 3)
        return [
            start(
                back_refs[index].at[micro, parts],
                came.at[micro, index, parts],
                halo_send.at[micro, index, piece],
                halo_recv.at[micro, index, piece],
                ahead(axis, -by),
            )
            for index, (axis, by) in enumerate(sources)
        ]

    mate, other = core_mate(depth_at), chip_mate(depth_at)
    mate_other = chip_mate(mate)
    one_far = start(
        part_ref.at[mate_other], one_in.at[1], m_send.at[0], m_recv.at[0], {"depth": mate}
    )
    one_near = start(part_ref.at[mate], one_in.at[0], m_send.at[1], m_recv.at[1], {"depth": mate})
    scalars = [go_home(micro, 0) for micro in range(micros)]
    vectors = [go_home(micro, 1) for micro in range(micros)]
    one_far.wait_recv()
    two_out[...] = (part_ref[other].astype(f32) + one_in[1].astype(f32)).astype(bf16)
    two = start(two_out, two_in, m_send.at[2], m_recv.at[2], {"depth": other})
    one_near.wait_recv()
    two.wait_recv()
    for cell in range(cells):
        total = (
            part_ref[depth_at, cell].astype(f32)
            + one_in[0, cell].astype(f32)
            + two_in[cell].astype(f32)
        )
        three_out[cell] = total.astype(bf16)
    half = cells // 2
    base, place = cell_at // half * half, cell_at % half
    opposite = (cell_at + half) % cells
    three = []
    for by in range(1, half):
        there = base + (place + by) % half
        for side in range(2):
            order = side * half + by
            three.append(
                start(
                    three_out.at[(there + side * half) % cells],
                    three_in.at[order],
                    c_send.at[order],
                    c_recv.at[order],
                    {"cells": there},
                )
            )

    def back_sum(micro, part):
        total = gown_ref[micro, part]
        for index in range(count):
            total = total + came[micro, index, part].astype(f32)
        return total

    gain = jnp.concatenate([gain_ref[side : side + 1, :].astype(f32) for side in range(2)], axis=1)
    norm_grads = [jnp.zeros((1, gain.shape[1]), f32) for part in range(2)]
    for micro in range(micros):
        for copy in scalars[micro]:
            copy.wait_recv()
        total = back_sum(micro, 0)
        hat, spread = normalise(x_ref[micro])
        norm_grads[0] += jnp.sum(total * hat, axis=0, keepdims=True)
        norm_grads[1] += jnp.sum(total, axis=0, keepdims=True)
        g_hat = total * gain
        g_x = spread * (g_hat - lane_mean(g_hat) - hat * lane_mean(g_hat * hat))
        gx_ref[micro] = cotx_ref[micro] + g_x
    held[...] = gvec_in[...]
    for part in range(2):
        for side in range(2):
            row = 2 * part + side
            held[row : row + 1, :] = norm_grads[part][:, side * LANES : (side + 1) * LANES]
    quad[depth_at] = held[...]
    four = [
        start(held, quad.at[depth_at], d_send.at[by], d_recv.at[by], ahead("depth", by))
        for by in range(1, depth)
    ]

    for copy in three:
        copy.wait_recv()
    sums = [three_out[cell_at].astype(f32), three_out[opposite].astype(f32)]
    for side in range(2):
        for by in range(1, half):
            sums[side] = sums[side] + three_in[side * half + by].astype(f32)
    four_out[...] = sums[1].astype(bf16)
    crossing = start(four_out, four_in, c_send.at[0], c_recv.at[0], {"cells": opposite})
    for copy in four:
        copy.wait_recv()
    total = quad[0]
    for at in range(1, depth):
        total = total + quad[at]
    octo[cell_at] = total
    eight = [
        start(
            octo.at[cell_at],
            octo.at[cell_at],
            f_send.at[by],
            f_recv.at[by],
            ahead("cells", by),
        )
        for by in range(1, cells)
    ]
    crossing.wait_recv()
    summ_ref[depth_at] = sums[0] + four_in[...].astype(f32)
    share = [
        start(
            summ_ref.at[depth_at],
            summ_ref.at[depth_at],
            e_send.at[by],
            e_recv.at[by],
            ahead("depth", by),
        )
        for by in range(1, depth)
    ]
    for micro in range(micros):
        for copy in vectors[micro]:
            copy.wait_recv()
        for axis in range(3):
            gvec_ref[micro, axis] = cotv_ref[micro, axis] + back_sum(micro, 1 + axis)
    for copy in eight:
        copy.wait_recv()
    total = octo[0]
    for cell in range(1, cells):
        total = total + octo[cell]
    sumv_ref[...] = total
    for copy in share:
        copy.wait_recv()
    for copy in started:
        copy.wait_send()


def adam_update(weight, grad, first, second):
    first_new = beta_one * first + (1.0 - beta_one) * grad
    second_new = beta_two * second + (1.0 - beta_two) * grad * grad
    first_hat = first_new / (1.0 - beta_one**STEP)
    second_hat = second_new / (1.0 - beta_two**STEP)
    weight_new = weight - learn_rate * (
        first_hat / (jnp.sqrt(second_hat) + adam_eps) + decay_rate * weight
    )
    return (weight_new, first_new, second_new)


def shards(
    x_in,
    vec_in,
    cot_x,
    cot_vec,
    mats,
    vecs,
    mats_first,
    mats_second,
    vecs_first,
    vecs_second,
    atom_count,
    neighbours,
    edge_mask,
    edge_vec,
    send_list,
):
    micros, atoms, width = x_in.shape
    slots = neighbours.shape[1]
    halo = send_list.shape[-1]
    per_face = halo // LANES
    cells, depth = lax.axis_size("cells"), lax.axis_size("depth")
    faces = [("cells", 1), ("cells", -1), ("cells", FOLD), ("cells", -FOLD), ("depth", 1), ("depth", -1)]
    sizes = {"cells": cells, "depth": depth}
    sources = []
    face_source = []
    for axis, by in faces:
        key = (axis, by % sizes[axis])
        if key not in sources:
            sources.append(key)
        face_source.append(sources.index(key))
    domains = 1 + len(sources)
    buckets = (domains * atoms + ROWS - 1) // ROWS
    block_of = [1 + face_source[row // per_face] for row in range(6 * per_face)]

    whole = pl.BlockSpec(memory_space=pltpu.VMEM)
    scalars = pl.BlockSpec(memory_space=pltpu.SMEM)

    any_space = pl.BlockSpec(memory_space=pl.ANY)
    count = len(sources)
    quarter = mats.shape[0] // LANES // depth
    list_shape = jax.ShapeDtypeStruct((6, micros * per_face, LANES), i32)

    own, w_low, my_lists = pl.pallas_call(
        norm_kernel,
        out_shape=(
            jax.ShapeDtypeStruct((micros, 4, atoms, width), bf16),
            jax.ShapeDtypeStruct((depth, quarter, LANES), bf16),
            list_shape,
        ),
        in_specs=[whole] * 4,
        out_specs=[whole] * 3,
        name="norm",
    )(x_in, vec_in, mats.reshape(-1, LANES), send_list)

    dma = pltpu.SemaphoreType.DMA
    fetched = pl.pallas_call(
        partial(fetch_kernel, cells, depth, micros, sources, faces),
        out_shape=tuple(
            [jax.ShapeDtypeStruct((micros, 4, atoms, width), bf16)] * count
            + [
                list_shape,
                jax.ShapeDtypeStruct((cells, depth, quarter, LANES), bf16),
                jax.ShapeDtypeStruct((cells, 1, vecs.shape[0]), f32),
            ]
        ),
        in_specs=[any_space] + [whole] * 3,
        out_specs=[any_space] * count + [whole] * 3,
        scratch_shapes=[
            dma((micros, count)),
            dma((micros, count)),
            dma((6,)),
            dma((6,)),
            dma((cells,)),
            dma((cells,)),
            dma((4, cells)),
            dma((4, cells)),
        ],
        compiler_params=pltpu.CompilerParams(
            collective_id=0, has_side_effects=True, vmem_limit_bytes=VMEM_LIMIT
        ),
        name="fetch",
    )(own, my_lists, w_low, vecs.reshape(1, -1))
    halos = fetched[:count]
    got_lists, w_all, v_all = fetched[count:]
    v_all = v_all.astype(bf16).reshape(-1, LANES)
    w_rows, v_rows = cells * depth * quarter, v_all.shape[0]

    limit = slots * atoms + buckets * (slots // BLOCK_SLOTS) * 8 + buckets * 2 * UNIT
    capacity = (limit + UNIT - 1) // UNIT * UNIT + 4 * UNIT

    def by_micro(array):
        zeros = (0,) * (len(array.shape) - 1)
        return pl.BlockSpec((1,) + tuple(array.shape[1:]), lambda i: (i,) + zeros)

    per_micro = [neighbours, edge_mask, edge_vec, x_in, vec_in, cot_x, cot_vec, *halos]
    out_blocks = [
        jax.ShapeDtypeStruct((micros, atoms, width), f32),
        jax.ShapeDtypeStruct((micros, 3, atoms, width), f32),
        jax.ShapeDtypeStruct((micros, 4, atoms, width), f32),
    ] + [jax.ShapeDtypeStruct((micros, 4, atoms, width), bf16)] * count
    results = pl.pallas_call(
        partial(edge_kernel, domains, buckets, block_of),
        out_shape=tuple(
            out_blocks
            + [
                jax.ShapeDtypeStruct((depth, cells, quarter, LANES), bf16),
                jax.ShapeDtypeStruct((v_rows, LANES), f32),
            ]
        ),
        grid=(micros,),
        in_specs=[scalars, whole] + [by_micro(array) for array in per_micro] + [whole] * 2,
        out_specs=[by_micro(block) for block in out_blocks] + [whole] * 2,
        scratch_shapes=[
            pltpu.VMEM((slots, LANES, LANES), bf16),
            pltpu.VMEM((slots, atoms), i32),
            pltpu.VMEM((slots // BLOCK_SLOTS, LANES), i32),
            pltpu.SMEM((slots // BLOCK_SLOTS, LANES), i32),
            pltpu.VMEM((capacity, LANES), f32),
            pltpu.SemaphoreType.DMA(()),
            pltpu.VMEM((w_rows, LANES), f32),
            pltpu.VMEM((11, ROWS, ROWS), bf16),
            pltpu.VMEM((LANES, 4 * ROWS), bf16),
            pltpu.VMEM((buckets * ROWS, ROWS), bf16),
            pltpu.VMEM((buckets, ROWS, 7 * ROWS), bf16),
            pltpu.VMEM((buckets, ROWS, 7 * ROWS), f32),
            pltpu.VMEM((atoms, 5 * ROWS), bf16),
            pltpu.VMEM((3, 3 * atoms, ROWS), f32),
            pltpu.VMEM((3, atoms, ROWS), bf16),
            pltpu.VMEM((atoms, 5 * ROWS), f32),
            pltpu.VMEM((FEATS, 4 * ROWS), f32),
            pltpu.VMEM((ROWS, ROWS), bf16),
        ]
        + [
            scratch
            for scratch in (
                pltpu.VMEM((UNIT, ROWS), bf16),
                pltpu.VMEM((UNIT, LANES), bf16),
                pltpu.VMEM((UNIT, WORK * ROWS), f32),
                pltpu.VMEM((UNIT, LANES), f32),
                pltpu.VMEM((3, UNIT, LANES), f32),
                pltpu.VMEM((2, 2 * UNIT, LANES), bf16),
                pltpu.VMEM((14, UNIT, LANES), bf16),
                pltpu.VMEM((8, UNIT, LANES), bf16),
                pltpu.VMEM((12, UNIT, LANES), bf16),
            )
            for side in range(2)
        ],
        compiler_params=pltpu.CompilerParams(vmem_limit_bytes=VMEM_LIMIT),
        name="edges",
    )(atom_count, got_lists, *per_micro, w_all, v_all)
    out_x, out_vec, g_own = results[:3]
    backs = results[3 : 3 + count]
    part_m, part_v = results[3 + count :]
    grad_x, grad_vec, sum_mats, sum_vecs = pl.pallas_call(
        partial(close_kernel, cells, depth, micros, sources),
        out_shape=(
            jax.ShapeDtypeStruct(x_in.shape, f32),
            jax.ShapeDtypeStruct(vec_in.shape, f32),
            jax.ShapeDtypeStruct((depth, quarter, LANES), f32),
            jax.ShapeDtypeStruct((v_rows, LANES), f32),
        ),
        in_specs=[whole] * 7 + [any_space] * count,
        out_specs=[whole] * 4,
        scratch_shapes=[
            pltpu.VMEM((micros, count, 4, atoms, width), bf16),
            pltpu.VMEM((2, cells, quarter, LANES), bf16),
            pltpu.VMEM((cells, quarter, LANES), bf16),
            pltpu.VMEM((cells, quarter, LANES), bf16),
            pltpu.VMEM((cells, quarter, LANES), bf16),
            pltpu.VMEM((cells, quarter, LANES), bf16),
            pltpu.VMEM((quarter, LANES), bf16),
            pltpu.VMEM((quarter, LANES), bf16),
            pltpu.VMEM((v_rows, LANES), f32),
            pltpu.VMEM((depth, v_rows, LANES), f32),
            pltpu.VMEM((cells, v_rows, LANES), f32),
            dma((micros, count, 2)),
            dma((micros, count, 2)),
            dma((3,)),
            dma((3,)),
            dma((cells,)),
            dma((cells,)),
            dma((depth,)),
            dma((depth,)),
            dma((depth,)),
            dma((depth,)),
            dma((cells,)),
            dma((cells,)),
        ],
        compiler_params=pltpu.CompilerParams(
            collective_id=1, has_side_effects=True, vmem_limit_bytes=VMEM_LIMIT
        ),
        name="close",
    )(
        x_in,
        cot_x,
        cot_vec,
        v_all,
        part_v,
        part_m,
        g_own,
        *backs,
    )
    sum_mats = sum_mats.reshape(-1)
    sum_vecs = lax.dynamic_slice_in_dim(
        sum_vecs.reshape(-1), lax.axis_index("cells") * vecs.shape[0], vecs.shape[0]
    )
    new_mats, mats_one, mats_two = adam_update(mats, sum_mats, mats_first, mats_second)
    new_vecs, vecs_one, vecs_two = adam_update(vecs, sum_vecs, vecs_first, vecs_second)
    return (
        out_x,
        out_vec,
        grad_x,
        grad_vec,
        sum_mats,
        sum_vecs,
        new_mats,
        new_vecs,
        mats_one,
        mats_two,
        vecs_one,
        vecs_two,
    )


def solution(mesh):
    by_atom = ("cells", "depth")
    shard = P("cells")
    in_specs = (
        P(None, by_atom, None),
        P(None, None, by_atom, None),
        P(None, by_atom, None),
        P(None, None, by_atom, None),
        shard,
        shard,
        shard,
        shard,
        shard,
        shard,
        P(None, by_atom),
        P(None, None, by_atom),
        P(None, None, by_atom),
        P(None, None, None, by_atom),
        P(None, by_atom, None),
    )
    out_specs = (
        P(None, by_atom, None),
        P(None, None, by_atom, None),
        P(None, by_atom, None),
        P(None, None, by_atom, None),
    ) + (shard,) * 8
    return jax.shard_map(shards, mesh=mesh, in_specs=in_specs, out_specs=out_specs, check_vma=False)
```

```python
from functools import partial
import math

import jax
import jax.numpy as jnp
from jax import lax
from jax.experimental import pallas as pl
from jax.experimental.pallas import tpu as pltpu
from jax.sharding import PartitionSpec as P

HEADS = 8
NR = 32
FOLD = 4
STEP = 3

LANES = 128
ROWS = 256
UNIT = 256
BLOCK_SLOTS = 4
TILES = ((0.3, 192), (0.625, 128), (1.0, 80))

norm_eps = 1e-05
cut_radius = 5.0
beta_one = 0.5
beta_two = 0.5
learn_rate = 0.05
decay_rate = 0.01
adam_eps = 1e-08

f32 = jnp.float32
bf16 = jnp.bfloat16
i32 = jnp.int32

VMEM_LIMIT = 60 * 1024 * 1024


def dot_nn(left, right):
    return lax.dot_general(left, right, (((1,), (0,)), ((), ())), preferred_element_type=f32)


def dot_nt(left, right):
    return lax.dot_general(left, right, (((1,), (1,)), ((), ())), preferred_element_type=f32)


def dot_tn(left, right):
    return lax.dot_general(left, right, (((0,), (0,)), ((), ())), preferred_element_type=f32)


def lane_mean(block):
    return jnp.sum(block, axis=-1, keepdims=True) * (1.0 / block.shape[-1])


def normalise(block):
    centered = block - lane_mean(block)
    spread = lax.rsqrt(lane_mean(centered * centered) + norm_eps)
    return centered * spread, spread


def norm_kernel(x_ref, vec_ref, mats_ref, list_ref, own_ref, low_ref, lists_ref):
    micros, faces, halo = list_ref.shape
    per_face = halo // LANES
    for face in range(faces):
        for row in range(micros * per_face):
            lanes = slice(row % per_face * LANES, (row % per_face + 1) * LANES)
            lists_ref[face, row : row + 1, :] = list_ref[row // per_face, face : face + 1, lanes]
    quarter = low_ref.shape[1]
    for part in range(low_ref.shape[0]):
        low_ref[part] = mats_ref[part * quarter : (part + 1) * quarter, :].astype(bf16)
    for micro in range(x_ref.shape[0]):
        own_ref[micro, 0] = normalise(x_ref[micro])[0].astype(bf16)
        own_ref[micro, 1:] = vec_ref[micro].astype(bf16)


Q_AT, K_AT, V_AT, VEC_AT, O_AT, DK_AT, DV_AT = 0, 512, 1024, 2560, 4096, 5632, 5696
W_Q, W_K, W_V, W_VEC, W_O = 0, 1, 2, 5, 8
FEATS = 48
CHUNK = 16
GATH, PER_ATOM, FILT, SUMS, KEPT, WORK = 0, 7, 12, 16, 18, 24


def edge_features(nbr, mask, geom, lists, block_of, buckets, feat, place, count_vec):
    slots, atoms = nbr.shape
    blocks = slots // BLOCK_SLOTS
    live = mask > 0
    halo_at = nbr - atoms
    list_row = halo_at >> 7
    list_lane = halo_at & (LANES - 1)
    atom_in = nbr
    block_id = jnp.zeros_like(nbr)
    for row, picks in enumerate(lists):
        table = jnp.broadcast_to(picks, (slots, atoms))
        picked = jnp.take_along_axis(table, list_lane, axis=1)
        here = list_row == row
        atom_in = jnp.where(here, picked, atom_in)
        block_id = jnp.where(here, block_of[row], block_id)
    entry = block_id * atoms + atom_in
    bucket = entry >> 8
    low = ((entry & (ROWS - 1)) + 1).astype(f32)
    atom_id = (lax.broadcasted_iota(i32, (slots, atoms), 1) + 1).astype(f32)
    live_float = live.astype(f32)

    radius = jnp.sqrt(geom[0] * geom[0] + geom[1] * geom[1] + geom[2] * geom[2])
    units = [comp / radius for comp in geom]
    cut = 0.5 * (jnp.cos(math.pi * radius / cut_radius) + 1.0) * live_float
    cut_high = cut.astype(bf16).astype(f32)
    cut_low = cut - cut_high
    decayed = jnp.exp(-(5.0 / cut_radius) * radius)
    start_value = math.exp(-cut_radius)
    ramp = lax.broadcasted_iota(i32, (NR, 1), 0).astype(f32) / float(NR - 1)
    centers = start_value * (1.0 - ramp) + ramp
    width_coef = (2.0 / NR * (1.0 - start_value)) ** (-2)
    extras = [live_float, low, atom_id, cut_high, cut_low] + units
    zeros = jnp.zeros((16 - len(extras), atoms), f32)
    for slot in range(slots):
        gap = decayed[slot : slot + 1, :] - centers
        basis = cut[slot : slot + 1, :] * jnp.exp(-width_coef * gap * gap)
        feat[slot, 0:NR, :] = basis.astype(bf16)
        rows = [extra[slot : slot + 1, :] for extra in extras] + [zeros]
        feat[slot, NR : NR + 16, :] = jnp.concatenate(rows, axis=0).astype(bf16)

    members = [jnp.where(live & (bucket == b), 1.0, 0.0) for b in range(buckets)]
    lane_from = lax.broadcasted_iota(i32, (atoms, 2 * atoms), 0)
    lane_to = lax.broadcasted_iota(i32, (atoms, 2 * atoms), 1)
    before = jnp.where((lane_from < lane_to) | (lane_to >= atoms), 1.0, 0.0).astype(bf16)
    slot_to = lax.broadcasted_iota(i32, (slots, slots), 0)
    slot_from = lax.broadcasted_iota(i32, (slots, slots), 1)
    same = (slot_to // BLOCK_SLOTS) == (slot_from // BLOCK_SLOTS)
    earlier = jnp.where(same & (slot_from < slot_to), 1.0, 0.0).astype(bf16)
    block_row = lax.broadcasted_iota(i32, (blocks, slots), 0)
    block_slot = lax.broadcasted_iota(i32, (blocks, slots), 1)
    gather_block = jnp.where(block_slot // BLOCK_SLOTS == block_row, 1.0, 0.0).astype(bf16)
    lane = lax.broadcasted_iota(i32, (blocks, LANES), 1)
    rank = jnp.zeros((slots, atoms), f32)
    counts = jnp.zeros((blocks, LANES), f32)
    for b in range(buckets):
        sums = dot_nn(members[b].astype(bf16), before)
        row_total = sums[:, atoms:].astype(bf16)
        offset = sums[:, :atoms] + dot_nn(earlier, row_total)
        rank = jnp.where(members[b] > 0.0, offset, rank)
        counts = jnp.where(lane == b, dot_nn(gather_block, row_total), counts)
    place[...] = jnp.where(live, bucket * 1024 + rank.astype(i32), -1)
    count_vec[...] = counts.astype(i32)


def pack_edges(blocks, atoms, buckets, feat, place, count_sc, packed):
    wide = BLOCK_SLOTS * atoms

    def total_body(block, totals):
        return tuple(
            total + (((count_sc[block, b] + 7) >> 3) << 3) for b, total in enumerate(totals)
        )

    totals = lax.fori_loop(0, blocks, total_body, (jnp.int32(0),) * buckets)
    held = [(total + (UNIT - 1)) >> 8 for total in totals]
    bases = [jnp.int32(UNIT)]
    for total in totals:
        bases.append(bases[-1] + (((total + (2 * UNIT - 1)) >> 8) << 8))

    def picks(places, b, first, tile):
        wanted = lax.broadcasted_iota(i32, (tile, wide), 0) + (b * 1024 + first)
        return jnp.where(places == wanted, 1.0, 0.0).astype(bf16)

    def places_of(block):
        rows = [place[pl.ds(block * BLOCK_SLOTS + t, 1), :] for t in range(BLOCK_SLOTS)]
        return jnp.concatenate(rows, axis=1)

    def feats_of(block):
        parts = [feat[block * BLOCK_SLOTS + t] for t in range(BLOCK_SLOTS)]
        return jnp.concatenate(parts, axis=1)

    def padded(block, b):
        return ((count_sc[block, b] + 7) >> 3) << 3

    def block_body(size, block, at):
        places = places_of(block)
        feats = feats_of(block)
        for b in range(buckets):
            made = dot_nt(picks(places, b, 0, size), feats)
            packed[pl.ds(pl.multiple_of(at[b], 8), size), :] = made
        return tuple(at[b] + padded(block, b) for b in range(buckets))

    def rest_body(size, block, at):
        for b in range(buckets):
            rows = padded(block, b)

            @pl.when(rows > size)
            def _(b=b, rows=rows):
                def tile_body(tile, carry):
                    first = jnp.minimum(tile * size, rows - size)
                    pick = picks(places_of(block), b, first, size)
                    start = pl.multiple_of(at[b] + first, 8)
                    packed[pl.ds(start, size), :] = dot_nt(pick, feats_of(block))
                    return carry

                lax.fori_loop(1, (rows + (size - 1)) // size, tile_body, 0)

        return tuple(at[b] + padded(block, b) for b in range(buckets))

    begin = 0
    ends = tuple(bases[:buckets])
    for share, size in TILES:
        until = int(blocks * share)
        ends = lax.fori_loop(begin, until, partial(block_body, size), ends, unroll=2)
        begin = until
    begin = 0
    ends = tuple(bases[:buckets])
    for share, size in TILES:
        until = int(blocks * share)
        ends = lax.fori_loop(begin, until, partial(rest_body, size), ends)
        begin = until
    zeros = jnp.zeros((UNIT, LANES), f32)
    for end in ends:
        packed[pl.ds(pl.multiple_of(end, 8), UNIT), :] = zeros
    packed[0:UNIT, :] = zeros
    return held, bases


def edge_kernel(domains, buckets, block_of, *refs):
    refs = list(refs)
    count_ref, list_ref, nbr_ref, mask_ref, geom_ref, x_ref, vec_ref, cotx_ref, cotv_ref = refs[:9]
    halo_refs = refs[9 : 9 + domains - 1]
    at = 9 + domains - 1
    w_ref, v_ref = refs[at : at + 2]
    at += 2
    outx_ref, outv_ref, gown_ref = refs[at : at + 3]
    at += 3
    back_refs = refs[at : at + domains - 1]
    at += domains - 1
    gm_ref, gv_ref = refs[at : at + 2]
    at += 2
    (
        feat,
        place,
        count_vec,
        count_sc,
        packed,
        sem,
        wide_w,
        wb,
        wd,
        norm_table,
        tab,
        acc,
        atom_tab,
        proj,
        go,
        agg,
        gwd,
        heads,
    ) = refs[at : at + 18]
    rest = refs[at + 18 :]
    sides = [tuple(rest[side::2]) for side in range(2)]
    micro = pl.program_id(0)
    slots, atoms = nbr_ref.shape[1:]
    feat_width = x_ref.shape[2]
    cells, parts_w, quarter = w_ref.shape[:3]
    parts = [slice(axis * atoms, (axis + 1) * atoms) for axis in range(3)]

    def vector(index):
        both = [v_ref[2 * index + half : 2 * index + half + 1, :].astype(f32) for half in range(2)]
        return jnp.concatenate(both, axis=1)

    @pl.when(micro == 0)
    def _():
        feat[...] = jnp.zeros_like(feat)
        for ref in sides[1][6:]:
            ref[...] = jnp.zeros_like(ref)
        gwd[...] = jnp.zeros_like(gwd)
        for cell in range(cells):
            for part in range(parts_w):
                start = (cell * parts_w + part) * quarter
                wide_w[start : start + quarter, :] = w_ref[cell, part].astype(f32)

        def weight_block(first, stride, column, rows):
            halves = [
                wide_w[pl.ds(first + 2 * column + half, rows, stride=stride), :]
                for half in range(2)
            ]
            return jnp.concatenate(halves, axis=1)

        for slot, first, stride, count in (
            (W_Q, Q_AT, 2, 1),
            (W_K, K_AT, 2, 1),
            (W_V, V_AT, 6, 3),
            (W_VEC, VEC_AT, 6, 3),
            (W_O, O_AT, 6, 3),
        ):
            for column in range(count):
                wb[slot + column] = weight_block(first, stride, column, ROWS).astype(bf16)
        bias_row = lax.broadcasted_iota(i32, (LANES - NR, 1), 0) == 0
        for column in range(4):
            if column == 0:
                block = weight_block(DK_AT, 2, 0, NR)
            else:
                block = weight_block(DV_AT, 6, column - 1, NR)
            bias = jnp.where(bias_row, vector(10 + column), 0.0)
            cols = slice(column * ROWS, (column + 1) * ROWS)
            wd[:, cols] = (jnp.concatenate([block, bias], axis=0) * 0.5).astype(bf16)
        head_from = lax.broadcasted_iota(i32, (ROWS, ROWS), 0) // (feat_width // HEADS)
        head_to = lax.broadcasted_iota(i32, (ROWS, ROWS), 1) // (feat_width // HEADS)
        heads[...] = jnp.where(head_from == head_to, 0.5, 0.0).astype(bf16)

    geom = [geom_ref[0, axis] for axis in range(3)]
    per_face = len(block_of) // list_ref.shape[0]
    lists = [
        list_ref[face, pl.ds(micro * per_face + row, 1), :]
        for face in range(list_ref.shape[0])
        for row in range(per_face)
    ]
    edge_features(
        nbr_ref[0], mask_ref[0], geom, lists, block_of, buckets, feat, place, count_vec
    )
    copy = pltpu.make_async_copy(count_vec, count_sc, sem)
    copy.start()

    gain = vector(0)
    shift = vector(1)
    own_hat, unused = normalise(x_ref[0])
    vec_low = vec_ref[0].astype(bf16)
    for domain in range(2 * buckets):
        rows = slice(domain * atoms, (domain + 1) * atoms)
        here = slice((domain % 2) * atoms, (domain % 2 + 1) * atoms)
        if domain == 0:
            norm_table[rows, :] = (own_hat * gain + shift).astype(bf16)
        elif domain < domains:
            hat = halo_refs[domain - 1][0, 0].astype(f32)
            norm_table[rows, :] = (hat * gain + shift).astype(bf16)
        else:
            norm_table[rows, :] = jnp.zeros((atoms, feat_width), bf16)
        for axis in range(3):
            cols = slice((4 + axis) * ROWS, (5 + axis) * ROWS)
            if domain < domains:
                block = vec_low[axis] if domain == 0 else halo_refs[domain - 1][0, 1 + axis]
            else:
                block = jnp.zeros((atoms, feat_width), bf16)
            tab[domain // 2, here, cols] = block
    for b in range(buckets):
        rows = slice(b * ROWS, (b + 1) * ROWS)
        for column in range(4):
            cols = slice(column * ROWS, (column + 1) * ROWS)
            made = dot_nn(norm_table[rows, :], wb[W_K + column]) + vector(3 + column)
            tab[b, :, cols] = made.astype(bf16)

    live = (lax.broadcasted_iota(i32, (atoms, 1), 0) < count_ref[micro, 0]).astype(f32)
    query = dot_nn(norm_table[0:atoms, :], wb[W_Q]) + vector(2)
    atom_tab[:, 0:ROWS] = query.astype(bf16)
    vec_rows = vec_low.reshape(3 * atoms, feat_width)
    for part in range(3):
        proj[part] = dot_nn(vec_rows, wb[W_VEC + part])
    cot_x = cotx_ref[0] * live
    vec_dot = jnp.zeros((atoms, feat_width), f32)
    go_one = jnp.zeros((atoms, feat_width), f32)
    for axis in range(3):
        cot_v = cotv_ref[0, axis] * live
        vec_dot += proj[0, parts[axis], :] * proj[1, parts[axis], :]
        go_one += proj[2, parts[axis], :] * cot_v
        atom_tab[:, (2 + axis) * ROWS : (3 + axis) * ROWS] = cot_v.astype(bf16)
    go[0] = go_one.astype(bf16)
    go[1] = (vec_dot * cot_x).astype(bf16)
    go[2] = cot_x.astype(bf16)
    g_agg = dot_nt(go[0], wb[W_O])
    for part in range(1, 3):
        g_agg += dot_nt(go[part], wb[W_O + part])
    atom_tab[:, ROWS : 2 * ROWS] = g_agg.astype(bf16)
    agg[...] = jnp.zeros_like(agg)
    for b in range(buckets):
        acc[b] = jnp.zeros((ROWS, 7 * ROWS), f32)

    copy.wait()
    held, bases = pack_edges(
        slots // BLOCK_SLOTS, atoms, buckets, feat, place, count_sc, packed
    )
    firsts = [jnp.int32(0)]
    for number in held:
        firsts.append(firsts[-1] + number)
    total_units = firsts[-1]

    def bucket_of(unit):
        b = jnp.int32(0)
        for at in range(1, buckets):
            b = b + jnp.where(unit >= firsts[at], 1, 0)
        return b

    def rows_of(unit):
        start = jnp.int32(0)
        for at in range(buckets):
            inside = (unit >= firsts[at]) & (unit < firsts[at + 1])
            start = jnp.where(inside, bases[at] + (unit - firsts[at]) * UNIT, start)
        return pl.ds(pl.multiple_of(start, UNIT), UNIT)

    def block_cols(block):
        return slice(block * ROWS, (block + 1) * ROWS)

    def hits(side, rows):
        hit, atom_one = side[:2]
        full = packed[rows, :]
        lane_row = lax.broadcasted_iota(i32, (UNIT, ROWS), 1).astype(f32) + 1.0
        lane_atom = lax.broadcasted_iota(i32, (UNIT, LANES), 1).astype(f32) + 1.0
        hit[...] = jnp.where(full[:, NR + 1 : NR + 2] == lane_row, 1.0, 0.0).astype(bf16)
        atom_one[...] = jnp.where(full[:, NR + 2 : NR + 3] == lane_atom, 1.0, 0.0).astype(bf16)

    def spread(side, rows):
        cutb, dirs = side[3:5]
        full = packed[rows, :]
        for axis in range(3):
            column = full[:, NR + 5 + axis : NR + 6 + axis]
            dirs[axis] = jnp.broadcast_to(column, (UNIT, LANES))
        column = full[:, NR + 3 : NR + 4] + full[:, NR + 4 : NR + 5]
        cutb[...] = jnp.broadcast_to(column, (UNIT, LANES))

    def gather_steps(side, unit):
        hit, atom_one, work = side[:3]
        b = jnp.minimum(bucket_of(unit), buckets - 1)
        rows = rows_of(unit)

        def gather_table(block):
            work[:, block_cols(GATH + block)] = dot_nn(hit[...], tab[b, :, block_cols(block)])

        def gather_atom(block):
            made = dot_nn(atom_one[...], atom_tab[:, block_cols(block)])
            work[:, block_cols(PER_ATOM + block)] = made

        def filters(block):
            low = packed[rows, :].astype(bf16)
            work[:, block_cols(FILT + block)] = dot_nn(low, wd[:, block_cols(block)])

        return (
            [partial(gather_table, block) for block in range(7)]
            + [partial(gather_atom, block) for block in range(5)]
            + [partial(filters, block) for block in range(4)]
        )

    def mix(first, second):
        done = 0
        for at, step in enumerate(first):
            step()
            until = (at + 1) * len(second) // len(first)
            for other in second[done:until]:
                other()
            done = until

    chunks = [
        (slice(start, start + CHUNK), half)
        for start in range(0, UNIT, CHUNK)
        for half in range(2)
    ]

    def put(ref, block, here, half, value):
        ref[2 * block + half, here, :] = value.astype(bf16)

    def reader(work):
        def part(block, here, half):
            start = block * ROWS + half * LANES
            return work[here, start : start + LANES]

        def gate(here, block, half):
            value = part(FILT + block, here, half)
            turn = jnp.tanh(value)
            lift = 1.0 + turn
            silu = value * lift
            return silu, lift + silu * (1.0 - turn)

        return part, gate

    def heads_stage(side, here, half):
        work, pair = side[2], side[5]
        part, gate = reader(work)

        def keep(block, value):
            start = (KEPT + block) * ROWS + half * LANES
            work[here, start : start + LANES] = value

        there = slice(UNIT + here.start, UNIT + here.stop)
        silu, slope = gate(here, 0, half)
        query_e = part(PER_ATOM, here, half)
        key_e = part(GATH, here, half)
        gated = query_e * silu
        keep(0, gated)
        keep(1, query_e * key_e * slope)
        keep(2, key_e * silu)
        pair[half, here, :] = (gated * key_e).astype(bf16)
        silu, slope = gate(here, 1, half)
        cot_e = part(PER_ATOM + 1, here, half)
        value_e = part(GATH + 1, here, half)
        gated = value_e * silu
        keep(3, cot_e * silu)
        keep(4, cot_e * value_e * slope)
        keep(5, gated)
        pair[half, there, :] = (cot_e * gated).astype(bf16)

    def head_sums(side):
        work, pair = side[2], side[5]
        for at in range(2):
            rows = slice(at * UNIT, (at + 1) * UNIT)
            both = jnp.concatenate([pair[0, rows, :], pair[1, rows, :]], axis=1)
            work[:, block_cols(SUMS + at)] = dot_nn(both, heads[...])

    def vector_stage(side, here, half):
        dirs, dedge, dfilt, msg = side[4], *side[6:]
        part, gate = reader(side[2])
        cots = [part(PER_ATOM + 2 + axis, here, half) for axis in range(3)]
        vecs = [part(GATH + 4 + axis, here, half) for axis in range(3)]
        turns = [dirs[axis, here, :] for axis in range(3)]
        silu, slope = gate(here, 2, half)
        value_e = part(GATH + 2, here, half)
        gated = value_e * silu
        down = cots[0] * vecs[0] + cots[1] * vecs[1] + cots[2] * vecs[2]
        for axis in range(3):
            put(msg, 1 + axis, here, half, vecs[axis] * gated)
            put(dedge, 4 + axis, here, half, cots[axis] * gated)
        put(dedge, 2, here, half, down * silu)
        put(dfilt, 2, here, half, down * value_e * slope)
        silu, slope = gate(here, 3, half)
        value_e = part(GATH + 3, here, half)
        down = cots[0] * turns[0] + cots[1] * turns[1] + cots[2] * turns[2]
        put(dedge, 3, here, half, down * silu)
        put(dfilt, 3, here, half, down * value_e * slope)
        put(msg, 5, here, half, value_e * silu)

    def score_stage(side, here, half):
        cutb, dedge, dfilt, msg = side[3], *side[6:]
        part, unused = reader(side[2])
        cut = cutb[here, :]
        score = part(SUMS, here, half)
        turn = jnp.tanh(score)
        lift = 1.0 + turn
        silu = score * lift
        attention = silu * cut
        dscore = part(SUMS + 1, here, half) * cut * (lift + silu * (1.0 - turn))
        put(dedge, 0, here, half, dscore * part(KEPT, here, half))
        put(dfilt, 0, here, half, dscore * part(KEPT + 1, here, half))
        put(msg, 4, here, half, dscore * part(KEPT + 2, here, half))
        put(dedge, 1, here, half, attention * part(KEPT + 3, here, half))
        put(dfilt, 1, here, half, attention * part(KEPT + 4, here, half))
        put(msg, 0, here, half, attention * part(KEPT + 5, here, half))

    def both_halves(ref, block):
        return jnp.concatenate([ref[2 * block], ref[2 * block + 1]], axis=1)

    def scatter_steps(side, unit):
        dedge, dfilt, msg = side[6:]
        b = jnp.minimum(bucket_of(unit), buckets - 1)
        turned = packed[rows_of(unit), :].T

        def across(index):
            return turned[NR + index : NR + index + 1, :]

        sub_row = lax.broadcasted_iota(i32, (ROWS, UNIT), 0).astype(f32) + 1.0
        sub_atom = lax.broadcasted_iota(i32, (atoms, UNIT), 0).astype(f32) + 1.0
        hit_t = jnp.where(across(1) == sub_row, 1.0, 0.0).astype(bf16)
        atom_hit = across(2) == sub_atom
        atom_t = jnp.where(atom_hit, 1.0, 0.0).astype(bf16)
        feats_t = turned[0:FEATS, :].astype(bf16)
        turn = both_halves(msg, 5)

        def add_vector(axis):
            along = jnp.where(atom_hit, across(5 + axis), 0.0).astype(bf16)
            agg[:, block_cols(1 + axis)] += dot_nn(
                jnp.concatenate([atom_t, along], axis=1),
                jnp.concatenate([both_halves(msg, 1 + axis), turn], axis=0),
            )

        def add_table(block):
            acc[b, :, block_cols(block)] += dot_nn(hit_t, both_halves(dedge, block))

        def add_filter(block):
            gwd[:, block_cols(block)] += dot_nn(feats_t, both_halves(dfilt, block))

        def add_atom(block):
            agg[:, block_cols(block)] += dot_nn(atom_t, both_halves(msg, block))

        return (
            [partial(add_vector, axis) for axis in range(3)]
            + [partial(add_table, block) for block in (2, 3, 4, 5, 6, 0, 1)]
            + [partial(add_filter, block) for block in (2, 3, 0, 1)]
            + [partial(add_atom, block) for block in (0, 4)]
        )

    def on_chunks(stage, side):
        return [partial(stage, side, here, half) for here, half in chunks]

    hits(sides[0], rows_of(jnp.int32(0)))
    mix(gather_steps(sides[0], jnp.int32(0)), [])

    def pair_body(step, carry):
        for at in range(2):
            unit = 2 * step + at
            mine, other = sides[at], sides[1 - at]

            @pl.when(count_sc[0, 0] >= 0)
            def _(unit=unit, mine=mine, other=other):
                spread(mine, rows_of(unit))
                hits(other, rows_of(unit + 1))
                mix(scatter_steps(other, unit - 1), on_chunks(heads_stage, mine))

            @pl.when(count_sc[0, 0] >= 0 if at == 0 else unit < total_units)
            def _(unit=unit, mine=mine, other=other):
                head_sums(mine)
                mix(
                    gather_steps(other, unit + 1),
                    [step for two in zip(on_chunks(vector_stage, mine), on_chunks(score_stage, mine)) for step in two],
                )

        return carry

    steps = (total_units + 1) // 2
    lax.fori_loop(0, steps, pair_body, 0)
    mix(scatter_steps(sides[1], 2 * steps - 1), [])

    agg_low = agg[:, 0:ROWS].astype(bf16)
    outs = [dot_nn(agg_low, wb[W_O + part]) + vector(7 + part) for part in range(3)]
    outx_ref[0] = x_ref[0] + (vec_dot * outs[1] + outs[2]) * live
    g_dot = cot_x * outs[1]
    for axis in range(3):
        rows = parts[axis]
        vec_agg = agg[:, block_cols(1 + axis)]
        outv_ref[0, axis] = vec_ref[0, axis] + (proj[2, rows, :] * outs[0] + vec_agg) * live
        proj[2, rows, :] = cotv_ref[0, axis] * live * outs[0]
        first_part = proj[0, rows, :]
        proj[0, rows, :] = g_dot * proj[1, rows, :]
        proj[1, rows, :] = g_dot * first_part

    later = micro > 0

    def put_grad(first, stride, column, rows, value):
        for half in range(2):
            at = pl.ds(first + 2 * column + half, rows, stride=stride)
            before = jnp.where(later, wide_w[at, :], 0.0)
            wide_w[at, :] = value[:, half * LANES : (half + 1) * LANES] + before

    def put_vector(index, value):
        for half in range(2):
            row = slice(2 * index + half, 2 * index + half + 1)
            before = jnp.where(later, gv_ref[row, :], 0.0)
            gv_ref[row, :] = value[:, half * LANES : (half + 1) * LANES] + before

    def column_sum(value):
        return jnp.sum(value.astype(f32), axis=0, keepdims=True)

    put_vector(0, jnp.zeros((1, ROWS), f32))
    put_vector(1, jnp.zeros((1, ROWS), f32))
    g_vec = jnp.zeros((3 * atoms, feat_width), f32)
    for part_at in range(3):
        put_grad(O_AT, 6, part_at, ROWS, dot_tn(agg_low, go[part_at]))
        put_vector(7 + part_at, column_sum(go[part_at]))
        gp = proj[part_at].astype(bf16)
        put_grad(VEC_AT, 6, part_at, ROWS, dot_tn(vec_rows, gp))
        g_vec += dot_nt(gp, wb[W_VEC + part_at])

    g_query = agg[:, block_cols(4)].astype(bf16)
    put_grad(Q_AT, 2, 0, ROWS, dot_tn(norm_table[0:atoms, :], g_query))
    put_vector(2, column_sum(g_query))
    g_norm = dot_nt(g_query, wb[W_Q])

    sums = [jnp.zeros((ROWS, ROWS), f32) for column in range(4)]
    biases = [jnp.zeros((1, ROWS), f32) for column in range(4)]
    for b in range(buckets):
        rows = slice(b * ROWS, (b + 1) * ROWS)
        g_table = jnp.zeros((ROWS, ROWS), f32)
        for column in range(4):
            low = acc[b, :, block_cols(column)].astype(bf16)
            sums[column] += dot_tn(norm_table[rows, :], low)
            biases[column] += column_sum(low)
            g_table += dot_nt(low, wb[W_K + column])
        for half in range(2):
            domain = 2 * b + half
            if domain >= domains:
                continue
            here = slice(half * atoms, (half + 1) * atoms)
            if domain == 0:
                gown_ref[0, 0] = g_table[here, :] + g_norm
            else:
                back_refs[domain - 1][0, 0] = g_table[here, :].astype(bf16)
            for axis in range(3):
                block = acc[b, here, block_cols(4 + axis)]
                if domain == 0:
                    gown_ref[0, 1 + axis] = block + g_vec[parts[axis], :]
                else:
                    back_refs[domain - 1][0, 1 + axis] = block.astype(bf16)
    for column in range(4):
        if column == 0:
            put_grad(K_AT, 2, 0, ROWS, sums[column])
        else:
            put_grad(V_AT, 6, column - 1, ROWS, sums[column])
        put_vector(3 + column, biases[column])

    @pl.when(micro == pl.num_programs(0) - 1)
    def _():
        for column in range(4):
            block = gwd[0:NR, block_cols(column)] * 0.5
            first, stride, at = (DK_AT, 2, 0) if column == 0 else (DV_AT, 6, column - 1)
            for half in range(2):
                cols = slice(half * LANES, (half + 1) * LANES)
                wide_w[pl.ds(first + 2 * at + half, NR, stride=stride), :] = block[:, cols]
                row = 2 * (10 + column) + half
                bias = gwd[NR : NR + 1, column * ROWS + half * LANES :][:, :LANES]
                gv_ref[row : row + 1, :] = bias * 0.5
        for cell in range(cells):
            for part_at in range(parts_w):
                start = (cell * parts_w + part_at) * quarter
                gm_ref[part_at, cell] = wide_w[start : start + quarter, :].astype(bf16)


def core_mate(depth_at):
    return depth_at + 1 - 2 * (depth_at % 2)


def chip_mate(depth_at):
    return (depth_at + 2) % 4


def greet(cells, depth):
    barrier = pltpu.get_barrier_semaphore()
    cell_at, depth_at = lax.axis_index("cells"), lax.axis_index("depth")
    for by in range(1, cells):
        pl.semaphore_signal(barrier, inc=1, device_id={"cells": (cell_at + by) % cells})
    for by in range(1, depth):
        pl.semaphore_signal(barrier, inc=1, device_id={"depth": (depth_at + by) % depth})
    pl.semaphore_wait(barrier, cells + depth - 2)


def remote(source, target, send, receive, device):
    return pltpu.make_async_remote_copy(
        src_ref=source, dst_ref=target, send_sem=send, recv_sem=receive, device_id=device
    )


def fetch_kernel(cells, depth, micros, sources, faces, *refs):
    own_ref, lists_ref, w_ref, v_ref = refs[:4]
    halo_refs = refs[4 : 4 + len(sources)]
    got_lists, got_w, got_v = refs[4 + len(sources) : 7 + len(sources)]
    (
        halo_send,
        halo_recv,
        list_send,
        list_recv,
        v_send,
        v_recv,
        w_send,
        w_recv,
    ) = refs[7 + len(sources) :]
    cell_at, depth_at = lax.axis_index("cells"), lax.axis_index("depth")
    sizes = {"cells": cells, "depth": depth}
    places = {"cells": cell_at, "depth": depth_at}
    got_w[cell_at] = w_ref[...]
    got_v[cell_at] = v_ref[...]
    greet(cells, depth)

    def ahead(axis, by):
        return {axis: (places[axis] + by) % sizes[axis]}

    started = []

    def start(*args):
        copy = remote(*args)
        copy.start()
        started.append(copy)
        return copy

    half = cells // 2
    base, place = cell_at // half * half, cell_at % half

    def beside(by):
        return base + (place + by) % half

    def from_beside(by):
        return base + (place + half - by) % half

    opposite = (cell_at + half) % cells

    def send_weight(source_cell, order, target):
        piece = got_w.at[source_cell, depth_at]
        return start(piece, piece, w_send.at[0, order], w_recv.at[0, order], {"cells": target})

    origins = {by: from_beside(by) for by in range(1, half)}
    origins[half] = opposite
    for by in range(1, half):
        origins[half + by] = (from_beside(by) + half) % cells
    first = {half: send_weight(cell_at, half, opposite)}
    for by in range(1, half):
        first[by] = send_weight(cell_at, by, beside(by))
    lists = [
        start(
            lists_ref.at[face],
            got_lists.at[face],
            list_send.at[face],
            list_recv.at[face],
            ahead(axis, by),
        )
        for face, (axis, by) in enumerate(faces)
    ]
    vectors = [
        start(v_ref, got_v.at[cell_at], v_send.at[by], v_recv.at[by], ahead("cells", by))
        for by in range(1, cells)
    ]
    halos = []

    def send_halos(micro):
        for index, (axis, by) in enumerate(sources):
            halos.append(
                start(
                    own_ref.at[micro],
                    halo_refs[index].at[micro],
                    halo_send.at[micro, index],
                    halo_recv.at[micro, index],
                    ahead(axis, by),
                )
            )

    send_halos(0)
    order = [half, *range(1, half), *range(half + 1, cells)]
    first[half].wait_recv()
    for by in range(1, half):
        first[half + by] = send_weight(opposite, half + by, beside(by))
    mate, other = core_mate(depth_at), chip_mate(depth_at)
    across = []
    last = []
    for by in order:
        if by != half:
            first[by].wait_recv()
        piece = got_w.at[origins[by], depth_at]
        across.append(
            start(piece, piece, w_send.at[1, by], w_recv.at[1, by], {"depth": other})
        )
        last.append(start(piece, piece, w_send.at[2, by], w_recv.at[2, by], {"depth": mate}))
        if by == order[min(half - 1, cells - 2)]:
            for micro in range(1, micros):
                send_halos(micro)
    for at, by in enumerate(order):
        across[at].wait_recv()
        piece = got_w.at[origins[by], other]
        last.append(start(piece, piece, w_send.at[3, by], w_recv.at[3, by], {"depth": mate}))
    for copy in lists + vectors + last + halos:
        copy.wait_recv()
    for copy in started:
        copy.wait_send()


def close_kernel(cells, depth, micros, sources, *refs):
    count = len(sources)
    x_far, cotx_far, cotv_far, gain_ref, gvec_in, part_ref, gown_far = refs[:7]
    back_refs = refs[7 : 7 + count]
    gx_ref, gvec_ref, summ_ref, sumv_ref = refs[7 + count : 11 + count]
    (
        came,
        one_in,
        two_out,
        two_in,
        three_out,
        three_in,
        four_out,
        four_in,
        held,
        quad,
        octo,
        x_ref,
        cotx_ref,
        cotv_ref,
        gown_ref,
        load_sem,
        halo_send,
        halo_recv,
        m_send,
        m_recv,
        c_send,
        c_recv,
        d_send,
        d_recv,
        e_send,
        e_recv,
        f_send,
        f_recv,
    ) = refs[11 + count :]
    cell_at, depth_at = lax.axis_index("cells"), lax.axis_index("depth")
    sizes = {"cells": cells, "depth": depth}
    places = {"cells": cell_at, "depth": depth_at}
    greet(cells, depth)

    def ahead(axis, by):
        return {axis: (places[axis] + by) % sizes[axis]}

    started = []

    def start(*args):
        copy = remote(*args)
        copy.start()
        started.append(copy)
        return copy

    def go_home(micro, piece):
        parts = pl.ds(0, 1) if piece == 0 else pl.ds(1, 3)
        return [
            start(
                back_refs[index].at[micro, parts],
                came.at[micro, index, parts],
                halo_send.at[micro, index, piece],
                halo_recv.at[micro, index, piece],
                ahead(axis, -by),
            )
            for index, (axis, by) in enumerate(sources)
        ]

    mate, other = core_mate(depth_at), chip_mate(depth_at)
    mate_other = chip_mate(mate)
    one_far = start(
        part_ref.at[mate_other], one_in.at[1], m_send.at[0], m_recv.at[0], {"depth": mate}
    )
    one_near = start(part_ref.at[mate], one_in.at[0], m_send.at[1], m_recv.at[1], {"depth": mate})
    scalars = [go_home(micro, 0) for micro in range(micros)]
    vectors = [go_home(micro, 1) for micro in range(micros)]
    loads = [
        pltpu.make_async_copy(far, near, load_sem.at[at])
        for at, (far, near) in enumerate(
            ((gown_far, gown_ref), (x_far, x_ref), (cotx_far, cotx_ref), (cotv_far, cotv_ref))
        )
    ]
    for load in loads:
        load.start()
    one_far.wait_recv()
    two_out[...] = (part_ref[other].astype(f32) + one_in[1].astype(f32)).astype(bf16)
    two = start(two_out, two_in, m_send.at[2], m_recv.at[2], {"depth": other})
    one_near.wait_recv()
    two.wait_recv()
    for cell in range(cells):
        total = (
            part_ref[depth_at, cell].astype(f32)
            + one_in[0, cell].astype(f32)
            + two_in[cell].astype(f32)
        )
        three_out[cell] = total.astype(bf16)
    half = cells // 2
    base, place = cell_at // half * half, cell_at % half
    opposite = (cell_at + half) % cells
    three = []
    for by in range(1, half):
        there = base + (place + by) % half
        for side in range(2):
            order = side * half + by
            three.append(
                start(
                    three_out.at[(there + side * half) % cells],
                    three_in.at[order],
                    c_send.at[order],
                    c_recv.at[order],
                    {"cells": there},
                )
            )

    def back_sum(micro, part):
        total = gown_ref[micro, part]
        for index in range(count):
            total = total + came[micro, index, part].astype(f32)
        return total

    gain = jnp.concatenate([gain_ref[side : side + 1, :].astype(f32) for side in range(2)], axis=1)
    norm_grads = [jnp.zeros((1, gain.shape[1]), f32) for part in range(2)]
    for load in loads:
        load.wait()
    for micro in range(micros):
        for copy in scalars[micro]:
            copy.wait_recv()
        total = back_sum(micro, 0)
        hat, spread = normalise(x_ref[micro])
        norm_grads[0] += jnp.sum(total * hat, axis=0, keepdims=True)
        norm_grads[1] += jnp.sum(total, axis=0, keepdims=True)
        g_hat = total * gain
        g_x = spread * (g_hat - lane_mean(g_hat) - hat * lane_mean(g_hat * hat))
        gx_ref[micro] = cotx_ref[micro] + g_x
    held[...] = gvec_in[...]
    for part in range(2):
        for side in range(2):
            row = 2 * part + side
            held[row : row + 1, :] = norm_grads[part][:, side * LANES : (side + 1) * LANES]
    quad[depth_at] = held[...]
    four = [
        start(held, quad.at[depth_at], d_send.at[by], d_recv.at[by], ahead("depth", by))
        for by in range(1, depth)
    ]

    for copy in three:
        copy.wait_recv()
    sums = [three_out[cell_at].astype(f32), three_out[opposite].astype(f32)]
    for side in range(2):
        for by in range(1, half):
            sums[side] = sums[side] + three_in[side * half + by].astype(f32)
    four_out[...] = sums[1].astype(bf16)
    crossing = start(four_out, four_in, c_send.at[0], c_recv.at[0], {"cells": opposite})
    for copy in four:
        copy.wait_recv()
    total = quad[0]
    for at in range(1, depth):
        total = total + quad[at]
    octo[cell_at] = total
    eight = [
        start(
            octo.at[cell_at],
            octo.at[cell_at],
            f_send.at[by],
            f_recv.at[by],
            ahead("cells", by),
        )
        for by in range(1, cells)
    ]
    crossing.wait_recv()
    summ_ref[depth_at] = sums[0] + four_in[...].astype(f32)
    share = [
        start(
            summ_ref.at[depth_at],
            summ_ref.at[depth_at],
            e_send.at[by],
            e_recv.at[by],
            ahead("depth", by),
        )
        for by in range(1, depth)
    ]
    for micro in range(micros):
        for copy in vectors[micro]:
            copy.wait_recv()
        for axis in range(3):
            gvec_ref[micro, axis] = cotv_ref[micro, axis] + back_sum(micro, 1 + axis)
    for copy in eight:
        copy.wait_recv()
    total = octo[0]
    for cell in range(1, cells):
        total = total + octo[cell]
    sumv_ref[...] = total
    for copy in share:
        copy.wait_recv()
    for copy in started:
        copy.wait_send()


def adam_update(weight, grad, first, second):
    first_new = beta_one * first + (1.0 - beta_one) * grad
    second_new = beta_two * second + (1.0 - beta_two) * grad * grad
    first_hat = first_new / (1.0 - beta_one**STEP)
    second_hat = second_new / (1.0 - beta_two**STEP)
    weight_new = weight - learn_rate * (
        first_hat / (jnp.sqrt(second_hat) + adam_eps) + decay_rate * weight
    )
    return (weight_new, first_new, second_new)


def update_kernel(*refs):
    ins, outs = refs[:6], refs[6:]
    outs[0][...] = ins[0][...]
    outs[1][...] = ins[1][...]
    grad = ins[2][...]
    outs[2][...] = grad
    updated = adam_update(ins[3][...], grad, ins[4][...], ins[5][...])
    for out, value in zip(outs[3:], updated):
        out[...] = value


def shards(
    x_in,
    vec_in,
    cot_x,
    cot_vec,
    mats,
    vecs,
    mats_first,
    mats_second,
    vecs_first,
    vecs_second,
    atom_count,
    neighbours,
    edge_mask,
    edge_vec,
    send_list,
):
    micros, atoms, width = x_in.shape
    slots = neighbours.shape[1]
    halo = send_list.shape[-1]
    per_face = halo // LANES
    cells, depth = lax.axis_size("cells"), lax.axis_size("depth")
    faces = [("cells", 1), ("cells", -1), ("cells", FOLD), ("cells", -FOLD), ("depth", 1), ("depth", -1)]
    sizes = {"cells": cells, "depth": depth}
    sources = []
    face_source = []
    for axis, by in faces:
        key = (axis, by % sizes[axis])
        if key not in sources:
            sources.append(key)
        face_source.append(sources.index(key))
    domains = 1 + len(sources)
    buckets = (domains * atoms + ROWS - 1) // ROWS
    block_of = [1 + face_source[row // per_face] for row in range(6 * per_face)]

    whole = pl.BlockSpec(memory_space=pltpu.VMEM)
    scalars = pl.BlockSpec(memory_space=pltpu.SMEM)

    any_space = pl.BlockSpec(memory_space=pl.ANY)
    count = len(sources)
    quarter = mats.shape[0] // LANES // depth
    list_shape = jax.ShapeDtypeStruct((6, micros * per_face, LANES), i32)

    own, w_low, my_lists = pl.pallas_call(
        norm_kernel,
        out_shape=(
            jax.ShapeDtypeStruct((micros, 4, atoms, width), bf16),
            jax.ShapeDtypeStruct((depth, quarter, LANES), bf16),
            list_shape,
        ),
        in_specs=[whole] * 4,
        out_specs=[whole] * 3,
        name="norm",
    )(x_in, vec_in, mats.reshape(-1, LANES), send_list)

    dma = pltpu.SemaphoreType.DMA
    fetched = pl.pallas_call(
        partial(fetch_kernel, cells, depth, micros, sources, faces),
        out_shape=tuple(
            [jax.ShapeDtypeStruct((micros, 4, atoms, width), bf16)] * count
            + [
                list_shape,
                jax.ShapeDtypeStruct((cells, depth, quarter, LANES), bf16),
                jax.ShapeDtypeStruct((cells, 1, vecs.shape[0]), f32),
            ]
        ),
        in_specs=[any_space] + [whole] * 3,
        out_specs=[any_space] * count + [whole] * 3,
        scratch_shapes=[
            dma((micros, count)),
            dma((micros, count)),
            dma((6,)),
            dma((6,)),
            dma((cells,)),
            dma((cells,)),
            dma((4, cells)),
            dma((4, cells)),
        ],
        compiler_params=pltpu.CompilerParams(
            collective_id=0, has_side_effects=True, vmem_limit_bytes=VMEM_LIMIT
        ),
        name="fetch",
    )(own, my_lists, w_low, vecs.reshape(1, -1))
    halos = fetched[:count]
    got_lists, w_all, v_all = fetched[count:]
    v_all = v_all.astype(bf16).reshape(-1, LANES)
    w_rows, v_rows = cells * depth * quarter, v_all.shape[0]

    limit = slots * atoms + buckets * (slots // BLOCK_SLOTS) * 8 + buckets * 2 * UNIT
    capacity = (limit + UNIT - 1) // UNIT * UNIT + 4 * UNIT

    def by_micro(array):
        zeros = (0,) * (len(array.shape) - 1)
        return pl.BlockSpec((1,) + tuple(array.shape[1:]), lambda i: (i,) + zeros)

    per_micro = [neighbours, edge_mask, edge_vec, x_in, vec_in, cot_x, cot_vec, *halos]
    out_blocks = [
        jax.ShapeDtypeStruct((micros, atoms, width), f32),
        jax.ShapeDtypeStruct((micros, 3, atoms, width), f32),
        jax.ShapeDtypeStruct((micros, 4, atoms, width), f32),
    ] + [jax.ShapeDtypeStruct((micros, 4, atoms, width), bf16)] * count
    results = pl.pallas_call(
        partial(edge_kernel, domains, buckets, block_of),
        out_shape=tuple(
            out_blocks
            + [
                jax.ShapeDtypeStruct((depth, cells, quarter, LANES), bf16),
                jax.ShapeDtypeStruct((v_rows, LANES), f32),
            ]
        ),
        grid=(micros,),
        in_specs=[scalars, whole] + [by_micro(array) for array in per_micro] + [whole] * 2,
        out_specs=[by_micro(block) for block in out_blocks] + [whole] * 2,
        scratch_shapes=[
            pltpu.VMEM((slots, LANES, LANES), bf16),
            pltpu.VMEM((slots, atoms), i32),
            pltpu.VMEM((slots // BLOCK_SLOTS, LANES), i32),
            pltpu.SMEM((slots // BLOCK_SLOTS, LANES), i32),
            pltpu.VMEM((capacity, LANES), f32),
            pltpu.SemaphoreType.DMA(()),
            pltpu.VMEM((w_rows, LANES), f32),
            pltpu.VMEM((11, ROWS, ROWS), bf16),
            pltpu.VMEM((LANES, 4 * ROWS), bf16),
            pltpu.VMEM((buckets * ROWS, ROWS), bf16),
            pltpu.VMEM((buckets, ROWS, 7 * ROWS), bf16),
            pltpu.VMEM((buckets, ROWS, 7 * ROWS), f32),
            pltpu.VMEM((atoms, 5 * ROWS), bf16),
            pltpu.VMEM((3, 3 * atoms, ROWS), f32),
            pltpu.VMEM((3, atoms, ROWS), bf16),
            pltpu.VMEM((atoms, 5 * ROWS), f32),
            pltpu.VMEM((FEATS, 4 * ROWS), f32),
            pltpu.VMEM((ROWS, ROWS), bf16),
        ]
        + [
            scratch
            for scratch in (
                pltpu.VMEM((UNIT, ROWS), bf16),
                pltpu.VMEM((UNIT, LANES), bf16),
                pltpu.VMEM((UNIT, WORK * ROWS), f32),
                pltpu.VMEM((UNIT, LANES), f32),
                pltpu.VMEM((3, UNIT, LANES), f32),
                pltpu.VMEM((2, 2 * UNIT, LANES), bf16),
                pltpu.VMEM((14, UNIT, LANES), bf16),
                pltpu.VMEM((8, UNIT, LANES), bf16),
                pltpu.VMEM((12, UNIT, LANES), bf16),
            )
            for side in range(2)
        ],
        compiler_params=pltpu.CompilerParams(vmem_limit_bytes=VMEM_LIMIT),
        name="edges",
    )(atom_count, got_lists, *per_micro, w_all, v_all)
    out_x, out_vec, g_own = results[:3]
    backs = results[3 : 3 + count]
    part_m, part_v = results[3 + count :]
    grad_x, grad_vec, sum_mats, sum_vecs = pl.pallas_call(
        partial(close_kernel, cells, depth, micros, sources),
        out_shape=(
            jax.ShapeDtypeStruct(x_in.shape, f32),
            jax.ShapeDtypeStruct(vec_in.shape, f32),
            jax.ShapeDtypeStruct((depth, quarter, LANES), f32),
            jax.ShapeDtypeStruct((v_rows, LANES), f32),
        ),
        in_specs=[any_space] * 3 + [whole] * 3 + [any_space] * (1 + count),
        out_specs=[whole] * 4,
        scratch_shapes=[
            pltpu.VMEM((micros, count, 4, atoms, width), bf16),
            pltpu.VMEM((2, cells, quarter, LANES), bf16),
            pltpu.VMEM((cells, quarter, LANES), bf16),
            pltpu.VMEM((cells, quarter, LANES), bf16),
            pltpu.VMEM((cells, quarter, LANES), bf16),
            pltpu.VMEM((cells, quarter, LANES), bf16),
            pltpu.VMEM((quarter, LANES), bf16),
            pltpu.VMEM((quarter, LANES), bf16),
            pltpu.VMEM((v_rows, LANES), f32),
            pltpu.VMEM((depth, v_rows, LANES), f32),
            pltpu.VMEM((cells, v_rows, LANES), f32),
            pltpu.VMEM(x_in.shape, f32),
            pltpu.VMEM(cot_x.shape, f32),
            pltpu.VMEM(cot_vec.shape, f32),
            pltpu.VMEM(g_own.shape, f32),
            dma((4,)),
            dma((micros, count, 2)),
            dma((micros, count, 2)),
            dma((3,)),
            dma((3,)),
            dma((cells,)),
            dma((cells,)),
            dma((depth,)),
            dma((depth,)),
            dma((depth,)),
            dma((depth,)),
            dma((cells,)),
            dma((cells,)),
        ],
        compiler_params=pltpu.CompilerParams(
            collective_id=1, has_side_effects=True, vmem_limit_bytes=VMEM_LIMIT
        ),
        name="close",
    )(
        x_in,
        cot_x,
        cot_vec,
        v_all,
        part_v,
        part_m,
        g_own,
        *backs,
    )
    flat = [
        grad_x.reshape(-1, width),
        grad_vec.reshape(-1, width),
        *[array.reshape(-1, LANES) for array in (sum_mats, mats, mats_first, mats_second)],
    ]
    steps = 4 if all(array.shape[0] % 32 == 0 for array in flat) else 1

    def by_step(array):
        return pl.BlockSpec((array.shape[0] // steps, array.shape[1]), lambda i: (i, 0))

    outs = flat[:3] + [flat[3]] * 3
    grad_x, grad_vec, *matrices = pl.pallas_call(
        update_kernel,
        out_shape=tuple(jax.ShapeDtypeStruct(array.shape, f32) for array in outs),
        grid=(steps,),
        in_specs=[by_step(array) for array in flat],
        out_specs=[by_step(array) for array in outs],
        name="update",
    )(*flat)
    grad_x = grad_x.reshape(x_in.shape)
    grad_vec = grad_vec.reshape(vec_in.shape)
    sum_mats, new_mats, mats_one, mats_two = [matrix.reshape(-1) for matrix in matrices]
    sum_vecs = lax.dynamic_slice_in_dim(
        sum_vecs.reshape(-1), lax.axis_index("cells") * vecs.shape[0], vecs.shape[0]
    )
    new_vecs, vecs_one, vecs_two = adam_update(vecs, sum_vecs, vecs_first, vecs_second)
    return (
        out_x,
        out_vec,
        grad_x,
        grad_vec,
        sum_mats,
        sum_vecs,
        new_mats,
        new_vecs,
        mats_one,
        mats_two,
        vecs_one,
        vecs_two,
    )


def solution(mesh):
    by_atom = ("cells", "depth")
    shard = P("cells")
    in_specs = (
        P(None, by_atom, None),
        P(None, None, by_atom, None),
        P(None, by_atom, None),
        P(None, None, by_atom, None),
        shard,
        shard,
        shard,
        shard,
        shard,
        shard,
        P(None, by_atom),
        P(None, None, by_atom),
        P(None, None, by_atom),
        P(None, None, None, by_atom),
        P(None, by_atom, None),
    )
    out_specs = (
        P(None, by_atom, None),
        P(None, None, by_atom, None),
        P(None, by_atom, None),
        P(None, None, by_atom, None),
    ) + (shard,) * 8
    return jax.shard_map(shards, mesh=mesh, in_specs=in_specs, out_specs=out_specs, check_vma=False)
```

```python
from functools import partial
import math

import jax
import jax.numpy as jnp
from jax import lax
from jax.experimental import pallas as pl
from jax.experimental.pallas import tpu as pltpu
from jax.sharding import PartitionSpec as P

HEADS = 8
NR = 32
FOLD = 4
STEP = 3

LANES = 128
ROWS = 256
UNIT = 256
BLOCK_SLOTS = 4
TILES = ((0.3, 192), (0.625, 128), (1.0, 80))

norm_eps = 1e-05
cut_radius = 5.0
beta_one = 0.5
beta_two = 0.5
learn_rate = 0.05
decay_rate = 0.01
adam_eps = 1e-08

f32 = jnp.float32
bf16 = jnp.bfloat16
i32 = jnp.int32

VMEM_LIMIT = 60 * 1024 * 1024


def dot_nn(left, right):
    return lax.dot_general(left, right, (((1,), (0,)), ((), ())), preferred_element_type=f32)


def dot_nt(left, right):
    return lax.dot_general(left, right, (((1,), (1,)), ((), ())), preferred_element_type=f32)


def dot_tn(left, right):
    return lax.dot_general(left, right, (((0,), (0,)), ((), ())), preferred_element_type=f32)


def lane_mean(block):
    return jnp.sum(block, axis=-1, keepdims=True) * (1.0 / block.shape[-1])


def normalise(block):
    centered = block - lane_mean(block)
    spread = lax.rsqrt(lane_mean(centered * centered) + norm_eps)
    return centered * spread, spread


def norm_kernel(x_ref, vec_ref, mats_ref, list_ref, own_ref, low_ref, lists_ref):
    micros, faces, halo = list_ref.shape
    per_face = halo // LANES
    for face in range(faces):
        for row in range(micros * per_face):
            lanes = slice(row % per_face * LANES, (row % per_face + 1) * LANES)
            lists_ref[face, row : row + 1, :] = list_ref[row // per_face, face : face + 1, lanes]
    quarter = low_ref.shape[1]
    for part in range(low_ref.shape[0]):
        low_ref[part] = mats_ref[part * quarter : (part + 1) * quarter, :].astype(bf16)
    for micro in range(x_ref.shape[0]):
        own_ref[micro, 0] = normalise(x_ref[micro])[0].astype(bf16)
        own_ref[micro, 1:] = vec_ref[micro].astype(bf16)


Q_AT, K_AT, V_AT, VEC_AT, O_AT, DK_AT, DV_AT = 0, 512, 1024, 2560, 4096, 5632, 5696
W_Q, W_K, W_V, W_VEC, W_O = 0, 1, 2, 5, 8
FEATS = 48
CHUNK = 16
GATH, PER_ATOM, FILT, SUMS, KEPT, WORK = 0, 7, 12, 16, 18, 24


def edge_features(nbr, mask, geom, lists, block_of, buckets, feat, place, count_vec):
    slots, atoms = nbr.shape
    blocks = slots // BLOCK_SLOTS
    live = mask > 0
    halo_at = nbr - atoms
    list_row = halo_at >> 7
    list_lane = halo_at & (LANES - 1)
    atom_in = nbr
    block_id = jnp.zeros_like(nbr)
    for row, picks in enumerate(lists):
        table = jnp.broadcast_to(picks, (slots, atoms))
        picked = jnp.take_along_axis(table, list_lane, axis=1)
        here = list_row == row
        atom_in = jnp.where(here, picked, atom_in)
        block_id = jnp.where(here, block_of[row], block_id)
    entry = block_id * atoms + atom_in
    bucket = entry >> 8
    low = ((entry & (ROWS - 1)) + 1).astype(f32)
    atom_id = (lax.broadcasted_iota(i32, (slots, atoms), 1) + 1).astype(f32)
    live_float = live.astype(f32)

    radius = jnp.sqrt(geom[0] * geom[0] + geom[1] * geom[1] + geom[2] * geom[2])
    units = [comp / radius for comp in geom]
    cut = 0.5 * (jnp.cos(math.pi * radius / cut_radius) + 1.0) * live_float
    cut_high = cut.astype(bf16).astype(f32)
    cut_low = cut - cut_high
    decayed = jnp.exp(-(5.0 / cut_radius) * radius)
    start_value = math.exp(-cut_radius)
    ramp = lax.broadcasted_iota(i32, (NR, 1), 0).astype(f32) / float(NR - 1)
    centers = start_value * (1.0 - ramp) + ramp
    width_coef = (2.0 / NR * (1.0 - start_value)) ** (-2)
    extras = [live_float, low, atom_id, cut_high, cut_low] + units
    zeros = jnp.zeros((16 - len(extras), atoms), f32)
    for slot in range(slots):
        gap = decayed[slot : slot + 1, :] - centers
        basis = cut[slot : slot + 1, :] * jnp.exp(-width_coef * gap * gap)
        feat[slot, 0:NR, :] = basis.astype(bf16)
        rows = [extra[slot : slot + 1, :] for extra in extras] + [zeros]
        feat[slot, NR : NR + 16, :] = jnp.concatenate(rows, axis=0).astype(bf16)

    members = [jnp.where(live & (bucket == b), 1.0, 0.0) for b in range(buckets)]
    lane_from = lax.broadcasted_iota(i32, (atoms, 2 * atoms), 0)
    lane_to = lax.broadcasted_iota(i32, (atoms, 2 * atoms), 1)
    before = jnp.where((lane_from < lane_to) | (lane_to >= atoms), 1.0, 0.0).astype(bf16)
    slot_to = lax.broadcasted_iota(i32, (slots, slots), 0)
    slot_from = lax.broadcasted_iota(i32, (slots, slots), 1)
    same = (slot_to // BLOCK_SLOTS) == (slot_from // BLOCK_SLOTS)
    earlier = jnp.where(same & (slot_from < slot_to), 1.0, 0.0).astype(bf16)
    block_row = lax.broadcasted_iota(i32, (blocks, slots), 0)
    block_slot = lax.broadcasted_iota(i32, (blocks, slots), 1)
    gather_block = jnp.where(block_slot // BLOCK_SLOTS == block_row, 1.0, 0.0).astype(bf16)
    lane = lax.broadcasted_iota(i32, (blocks, LANES), 1)
    rank = jnp.zeros((slots, atoms), f32)
    counts = jnp.zeros((blocks, LANES), f32)
    for b in range(buckets):
        sums = dot_nn(members[b].astype(bf16), before)
        row_total = sums[:, atoms:].astype(bf16)
        offset = sums[:, :atoms] + dot_nn(earlier, row_total)
        rank = jnp.where(members[b] > 0.0, offset, rank)
        counts = jnp.where(lane == b, dot_nn(gather_block, row_total), counts)
    place[...] = jnp.where(live, bucket * 1024 + rank.astype(i32), -1)
    count_vec[...] = counts.astype(i32)


def pack_edges(blocks, atoms, buckets, feat, place, count_sc, packed):
    wide = BLOCK_SLOTS * atoms

    def total_body(block, totals):
        return tuple(
            total + (((count_sc[block, b] + 7) >> 3) << 3) for b, total in enumerate(totals)
        )

    totals = lax.fori_loop(0, blocks, total_body, (jnp.int32(0),) * buckets)
    held = [(total + (UNIT - 1)) >> 8 for total in totals]
    bases = [jnp.int32(UNIT)]
    for total in totals:
        bases.append(bases[-1] + (((total + (2 * UNIT - 1)) >> 8) << 8))

    def picks(places, b, first, tile):
        wanted = lax.broadcasted_iota(i32, (tile, wide), 0) + (b * 1024 + first)
        return jnp.where(places == wanted, 1.0, 0.0).astype(bf16)

    def places_of(block):
        rows = [place[pl.ds(block * BLOCK_SLOTS + t, 1), :] for t in range(BLOCK_SLOTS)]
        return jnp.concatenate(rows, axis=1)

    def feats_of(block):
        parts = [feat[block * BLOCK_SLOTS + t] for t in range(BLOCK_SLOTS)]
        return jnp.concatenate(parts, axis=1)

    def padded(block, b):
        return ((count_sc[block, b] + 7) >> 3) << 3

    def block_body(size, block, at):
        places = places_of(block)
        feats = feats_of(block)
        for b in range(buckets):
            made = dot_nt(picks(places, b, 0, size), feats)
            packed[pl.ds(pl.multiple_of(at[b], 8), size), :] = made
        return tuple(at[b] + padded(block, b) for b in range(buckets))

    def rest_body(size, block, at):
        for b in range(buckets):
            rows = padded(block, b)

            @pl.when(rows > size)
            def _(b=b, rows=rows):
                def tile_body(tile, carry):
                    first = jnp.minimum(tile * size, rows - size)
                    pick = picks(places_of(block), b, first, size)
                    start = pl.multiple_of(at[b] + first, 8)
                    packed[pl.ds(start, size), :] = dot_nt(pick, feats_of(block))
                    return carry

                lax.fori_loop(1, (rows + (size - 1)) // size, tile_body, 0)

        return tuple(at[b] + padded(block, b) for b in range(buckets))

    begin = 0
    ends = tuple(bases[:buckets])
    for share, size in TILES:
        until = int(blocks * share)
        ends = lax.fori_loop(begin, until, partial(block_body, size), ends, unroll=True)
        begin = until
    begin = 0
    ends = tuple(bases[:buckets])
    for share, size in TILES:
        until = int(blocks * share)
        ends = lax.fori_loop(begin, until, partial(rest_body, size), ends)
        begin = until
    zeros = jnp.zeros((UNIT, LANES), f32)
    for end in ends:
        packed[pl.ds(pl.multiple_of(end, 8), UNIT), :] = zeros
    packed[0:UNIT, :] = zeros
    return held, bases


def edge_kernel(domains, buckets, block_of, *refs):
    refs = list(refs)
    count_ref, list_ref, nbr_ref, mask_ref, geom_ref, x_ref, vec_ref, cotx_ref, cotv_ref = refs[:9]
    halo_refs = refs[9 : 9 + domains - 1]
    at = 9 + domains - 1
    w_ref, v_ref = refs[at : at + 2]
    at += 2
    outx_ref, outv_ref, gown_ref = refs[at : at + 3]
    at += 3
    back_refs = refs[at : at + domains - 1]
    at += domains - 1
    gm_ref, gv_ref = refs[at : at + 2]
    at += 2
    (
        feat,
        place,
        count_vec,
        count_sc,
        packed,
        sem,
        wide_w,
        wb,
        wd,
        norm_table,
        tab,
        acc,
        atom_tab,
        proj,
        go,
        agg,
        gwd,
        heads,
    ) = refs[at : at + 18]
    rest = refs[at + 18 :]
    sides = [tuple(rest[side::2]) for side in range(2)]
    micro = pl.program_id(0)
    slots, atoms = nbr_ref.shape[1:]
    feat_width = x_ref.shape[2]
    cells, parts_w, quarter = w_ref.shape[:3]
    parts = [slice(axis * atoms, (axis + 1) * atoms) for axis in range(3)]

    def vector(index):
        both = [v_ref[2 * index + half : 2 * index + half + 1, :].astype(f32) for half in range(2)]
        return jnp.concatenate(both, axis=1)

    @pl.when(micro == 0)
    def _():
        feat[...] = jnp.zeros_like(feat)
        for ref in sides[1][6:]:
            ref[...] = jnp.zeros_like(ref)
        gwd[...] = jnp.zeros_like(gwd)
        for cell in range(cells):
            for part in range(parts_w):
                start = (cell * parts_w + part) * quarter
                wide_w[start : start + quarter, :] = w_ref[cell, part].astype(f32)

        def weight_block(first, stride, column, rows):
            halves = [
                wide_w[pl.ds(first + 2 * column + half, rows, stride=stride), :]
                for half in range(2)
            ]
            return jnp.concatenate(halves, axis=1)

        for slot, first, stride, count in (
            (W_Q, Q_AT, 2, 1),
            (W_K, K_AT, 2, 1),
            (W_V, V_AT, 6, 3),
            (W_VEC, VEC_AT, 6, 3),
            (W_O, O_AT, 6, 3),
        ):
            for column in range(count):
                wb[slot + column] = weight_block(first, stride, column, ROWS).astype(bf16)
        bias_row = lax.broadcasted_iota(i32, (LANES - NR, 1), 0) == 0
        for column in range(4):
            if column == 0:
                block = weight_block(DK_AT, 2, 0, NR)
            else:
                block = weight_block(DV_AT, 6, column - 1, NR)
            bias = jnp.where(bias_row, vector(10 + column), 0.0)
            cols = slice(column * ROWS, (column + 1) * ROWS)
            wd[:, cols] = (jnp.concatenate([block, bias], axis=0) * 0.5).astype(bf16)
        head_from = lax.broadcasted_iota(i32, (ROWS, ROWS), 0) // (feat_width // HEADS)
        head_to = lax.broadcasted_iota(i32, (ROWS, ROWS), 1) // (feat_width // HEADS)
        heads[...] = jnp.where(head_from == head_to, 0.5, 0.0).astype(bf16)

    geom = [geom_ref[0, axis] for axis in range(3)]
    per_face = len(block_of) // list_ref.shape[0]
    lists = [
        list_ref[face, pl.ds(micro * per_face + row, 1), :]
        for face in range(list_ref.shape[0])
        for row in range(per_face)
    ]
    edge_features(
        nbr_ref[0], mask_ref[0], geom, lists, block_of, buckets, feat, place, count_vec
    )
    copy = pltpu.make_async_copy(count_vec, count_sc, sem)
    copy.start()

    gain = vector(0)
    shift = vector(1)
    own_hat, unused = normalise(x_ref[0])
    vec_low = vec_ref[0].astype(bf16)
    for domain in range(2 * buckets):
        rows = slice(domain * atoms, (domain + 1) * atoms)
        here = slice((domain % 2) * atoms, (domain % 2 + 1) * atoms)
        if domain == 0:
            norm_table[rows, :] = (own_hat * gain + shift).astype(bf16)
        elif domain < domains:
            hat = halo_refs[domain - 1][0, 0].astype(f32)
            norm_table[rows, :] = (hat * gain + shift).astype(bf16)
        else:
            norm_table[rows, :] = jnp.zeros((atoms, feat_width), bf16)
        for axis in range(3):
            cols = slice((4 + axis) * ROWS, (5 + axis) * ROWS)
            if domain < domains:
                block = vec_low[axis] if domain == 0 else halo_refs[domain - 1][0, 1 + axis]
            else:
                block = jnp.zeros((atoms, feat_width), bf16)
            tab[domain // 2, here, cols] = block
    for b in range(buckets):
        rows = slice(b * ROWS, (b + 1) * ROWS)
        for column in range(4):
            cols = slice(column * ROWS, (column + 1) * ROWS)
            made = dot_nn(norm_table[rows, :], wb[W_K + column]) + vector(3 + column)
            tab[b, :, cols] = made.astype(bf16)

    live = (lax.broadcasted_iota(i32, (atoms, 1), 0) < count_ref[micro, 0]).astype(f32)
    query = dot_nn(norm_table[0:atoms, :], wb[W_Q]) + vector(2)
    atom_tab[:, 0:ROWS] = query.astype(bf16)
    vec_rows = vec_low.reshape(3 * atoms, feat_width)
    for part in range(3):
        proj[part] = dot_nn(vec_rows, wb[W_VEC + part])
    cot_x = cotx_ref[0] * live
    vec_dot = jnp.zeros((atoms, feat_width), f32)
    go_one = jnp.zeros((atoms, feat_width), f32)
    for axis in range(3):
        cot_v = cotv_ref[0, axis] * live
        vec_dot += proj[0, parts[axis], :] * proj[1, parts[axis], :]
        go_one += proj[2, parts[axis], :] * cot_v
        atom_tab[:, (2 + axis) * ROWS : (3 + axis) * ROWS] = cot_v.astype(bf16)
    go[0] = go_one.astype(bf16)
    go[1] = (vec_dot * cot_x).astype(bf16)
    go[2] = cot_x.astype(bf16)
    g_agg = dot_nt(go[0], wb[W_O])
    for part in range(1, 3):
        g_agg += dot_nt(go[part], wb[W_O + part])
    atom_tab[:, ROWS : 2 * ROWS] = g_agg.astype(bf16)
    agg[...] = jnp.zeros_like(agg)
    for b in range(buckets):
        acc[b] = jnp.zeros((ROWS, 7 * ROWS), f32)

    copy.wait()
    held, bases = pack_edges(
        slots // BLOCK_SLOTS, atoms, buckets, feat, place, count_sc, packed
    )
    firsts = [jnp.int32(0)]
    for number in held:
        firsts.append(firsts[-1] + number)
    total_units = firsts[-1]

    def bucket_of(unit):
        b = jnp.int32(0)
        for at in range(1, buckets):
            b = b + jnp.where(unit >= firsts[at], 1, 0)
        return b

    def rows_of(unit):
        start = jnp.int32(0)
        for at in range(buckets):
            inside = (unit >= firsts[at]) & (unit < firsts[at + 1])
            start = jnp.where(inside, bases[at] + (unit - firsts[at]) * UNIT, start)
        return pl.ds(pl.multiple_of(start, UNIT), UNIT)

    def block_cols(block):
        return slice(block * ROWS, (block + 1) * ROWS)

    def hits(side, rows):
        hit, atom_one = side[:2]
        full = packed[rows, :]
        lane_row = lax.broadcasted_iota(i32, (UNIT, ROWS), 1).astype(f32) + 1.0
        lane_atom = lax.broadcasted_iota(i32, (UNIT, LANES), 1).astype(f32) + 1.0
        hit[...] = jnp.where(full[:, NR + 1 : NR + 2] == lane_row, 1.0, 0.0).astype(bf16)
        atom_one[...] = jnp.where(full[:, NR + 2 : NR + 3] == lane_atom, 1.0, 0.0).astype(bf16)

    def spread(side, rows):
        cutb, dirs = side[3:5]
        full = packed[rows, :]
        for axis in range(3):
            column = full[:, NR + 5 + axis : NR + 6 + axis]
            dirs[axis] = jnp.broadcast_to(column, (UNIT, LANES))
        column = full[:, NR + 3 : NR + 4] + full[:, NR + 4 : NR + 5]
        cutb[...] = jnp.broadcast_to(column, (UNIT, LANES))

    def gather_steps(side, unit):
        hit, atom_one, work = side[:3]
        b = jnp.minimum(bucket_of(unit), buckets - 1)
        rows = rows_of(unit)

        def gather_table(block):
            work[:, block_cols(GATH + block)] = dot_nn(hit[...], tab[b, :, block_cols(block)])

        def gather_atom(block):
            made = dot_nn(atom_one[...], atom_tab[:, block_cols(block)])
            work[:, block_cols(PER_ATOM + block)] = made

        def filters(block):
            low = packed[rows, :].astype(bf16)
            work[:, block_cols(FILT + block)] = dot_nn(low, wd[:, block_cols(block)])

        return (
            [partial(gather_table, block) for block in range(7)]
            + [partial(gather_atom, block) for block in range(5)]
            + [partial(filters, block) for block in range(4)]
        )

    def mix(first, second):
        done = 0
        for at, step in enumerate(first):
            step()
            until = (at + 1) * len(second) // len(first)
            for other in second[done:until]:
                other()
            done = until

    chunks = [
        (slice(start, start + CHUNK), half)
        for start in range(0, UNIT, CHUNK)
        for half in range(2)
    ]

    def put(ref, block, here, half, value):
        ref[2 * block + half, here, :] = value.astype(bf16)

    def reader(work):
        def part(block, here, half):
            start = block * ROWS + half * LANES
            return work[here, start : start + LANES]

        def gate(here, block, half):
            value = part(FILT + block, here, half)
            turn = jnp.tanh(value)
            lift = 1.0 + turn
            silu = value * lift
            return silu, lift + silu * (1.0 - turn)

        return part, gate

    def heads_stage(side, here, half):
        work, pair = side[2], side[5]
        part, gate = reader(work)

        def keep(block, value):
            start = (KEPT + block) * ROWS + half * LANES
            work[here, start : start + LANES] = value

        there = slice(UNIT + here.start, UNIT + here.stop)
        silu, slope = gate(here, 0, half)
        query_e = part(PER_ATOM, here, half)
        key_e = part(GATH, here, half)
        gated = query_e * silu
        keep(0, gated)
        keep(1, query_e * key_e * slope)
        keep(2, key_e * silu)
        pair[half, here, :] = (gated * key_e).astype(bf16)
        silu, slope = gate(here, 1, half)
        cot_e = part(PER_ATOM + 1, here, half)
        value_e = part(GATH + 1, here, half)
        gated = value_e * silu
        keep(3, cot_e * silu)
        keep(4, cot_e * value_e * slope)
        keep(5, gated)
        pair[half, there, :] = (cot_e * gated).astype(bf16)

    def head_sums(side):
        work, pair = side[2], side[5]
        for at in range(2):
            rows = slice(at * UNIT, (at + 1) * UNIT)
            both = jnp.concatenate([pair[0, rows, :], pair[1, rows, :]], axis=1)
            work[:, block_cols(SUMS + at)] = dot_nn(both, heads[...])

    def vector_stage(side, here, half):
        dirs, dedge, dfilt, msg = side[4], *side[6:]
        part, gate = reader(side[2])
        cots = [part(PER_ATOM + 2 + axis, here, half) for axis in range(3)]
        vecs = [part(GATH + 4 + axis, here, half) for axis in range(3)]
        turns = [dirs[axis, here, :] for axis in range(3)]
        silu, slope = gate(here, 2, half)
        value_e = part(GATH + 2, here, half)
        gated = value_e * silu
        down = cots[0] * vecs[0] + cots[1] * vecs[1] + cots[2] * vecs[2]
        for axis in range(3):
            put(msg, 1 + axis, here, half, vecs[axis] * gated)
            put(dedge, 4 + axis, here, half, cots[axis] * gated)
        put(dedge, 2, here, half, down * silu)
        put(dfilt, 2, here, half, down * value_e * slope)
        silu, slope = gate(here, 3, half)
        value_e = part(GATH + 3, here, half)
        down = cots[0] * turns[0] + cots[1] * turns[1] + cots[2] * turns[2]
        put(dedge, 3, here, half, down * silu)
        put(dfilt, 3, here, half, down * value_e * slope)
        put(msg, 5, here, half, value_e * silu)

    def score_stage(side, here, half):
        cutb, dedge, dfilt, msg = side[3], *side[6:]
        part, unused = reader(side[2])
        cut = cutb[here, :]
        score = part(SUMS, here, half)
        turn = jnp.tanh(score)
        lift = 1.0 + turn
        silu = score * lift
        attention = silu * cut
        dscore = part(SUMS + 1, here, half) * cut * (lift + silu * (1.0 - turn))
        put(dedge, 0, here, half, dscore * part(KEPT, here, half))
        put(dfilt, 0, here, half, dscore * part(KEPT + 1, here, half))
        put(msg, 4, here, half, dscore * part(KEPT + 2, here, half))
        put(dedge, 1, here, half, attention * part(KEPT + 3, here, half))
        put(dfilt, 1, here, half, attention * part(KEPT + 4, here, half))
        put(msg, 0, here, half, attention * part(KEPT + 5, here, half))

    def both_halves(ref, block):
        return jnp.concatenate([ref[2 * block], ref[2 * block + 1]], axis=1)

    def scatter_steps(side, unit):
        dedge, dfilt, msg = side[6:]
        b = jnp.minimum(bucket_of(unit), buckets - 1)
        turned = packed[rows_of(unit), :].T

        def across(index):
            return turned[NR + index : NR + index + 1, :]

        sub_row = lax.broadcasted_iota(i32, (ROWS, UNIT), 0).astype(f32) + 1.0
        sub_atom = lax.broadcasted_iota(i32, (atoms, UNIT), 0).astype(f32) + 1.0
        hit_t = jnp.where(across(1) == sub_row, 1.0, 0.0).astype(bf16)
        atom_hit = across(2) == sub_atom
        atom_t = jnp.where(atom_hit, 1.0, 0.0).astype(bf16)
        feats_t = turned[0:FEATS, :].astype(bf16)
        turn = both_halves(msg, 5)

        def add_vector(axis):
            along = jnp.where(atom_hit, across(5 + axis), 0.0).astype(bf16)
            agg[:, block_cols(1 + axis)] += dot_nn(
                jnp.concatenate([atom_t, along], axis=1),
                jnp.concatenate([both_halves(msg, 1 + axis), turn], axis=0),
            )

        def add_table(block):
            acc[b, :, block_cols(block)] += dot_nn(hit_t, both_halves(dedge, block))

        def add_filter(block):
            gwd[:, block_cols(block)] += dot_nn(feats_t, both_halves(dfilt, block))

        def add_atom(block):
            agg[:, block_cols(block)] += dot_nn(atom_t, both_halves(msg, block))

        return (
            [partial(add_vector, axis) for axis in range(3)]
            + [partial(add_table, block) for block in (2, 3, 4, 5, 6, 0, 1)]
            + [partial(add_filter, block) for block in (2, 3, 0, 1)]
            + [partial(add_atom, block) for block in (0, 4)]
        )

    def on_chunks(stage, side):
        return [partial(stage, side, here, half) for here, half in chunks]

    hits(sides[0], rows_of(jnp.int32(0)))
    mix(gather_steps(sides[0], jnp.int32(0)), [])

    def pair_body(step, carry):
        for at in range(2):
            unit = 2 * step + at
            mine, other = sides[at], sides[1 - at]

            @pl.when(count_sc[0, 0] >= 0)
            def _(unit=unit, mine=mine, other=other):
                spread(mine, rows_of(unit))
                hits(other, rows_of(unit + 1))
                mix(scatter_steps(other, unit - 1), on_chunks(heads_stage, mine))

            @pl.when(count_sc[0, 0] >= 0 if at == 0 else unit < total_units)
            def _(unit=unit, mine=mine, other=other):
                head_sums(mine)
                mix(
                    gather_steps(other, unit + 1),
                    [step for two in zip(on_chunks(vector_stage, mine), on_chunks(score_stage, mine)) for step in two],
                )

        return carry

    steps = (total_units + 1) // 2
    lax.fori_loop(0, steps, pair_body, 0)
    mix(scatter_steps(sides[1], 2 * steps - 1), [])

    agg_low = agg[:, 0:ROWS].astype(bf16)
    outs = [dot_nn(agg_low, wb[W_O + part]) + vector(7 + part) for part in range(3)]
    outx_ref[0] = x_ref[0] + (vec_dot * outs[1] + outs[2]) * live
    g_dot = cot_x * outs[1]
    for axis in range(3):
        rows = parts[axis]
        vec_agg = agg[:, block_cols(1 + axis)]
        outv_ref[0, axis] = vec_ref[0, axis] + (proj[2, rows, :] * outs[0] + vec_agg) * live
        proj[2, rows, :] = cotv_ref[0, axis] * live * outs[0]
        first_part = proj[0, rows, :]
        proj[0, rows, :] = g_dot * proj[1, rows, :]
        proj[1, rows, :] = g_dot * first_part

    later = micro > 0

    def put_grad(first, stride, column, rows, value):
        for half in range(2):
            at = pl.ds(first + 2 * column + half, rows, stride=stride)
            before = jnp.where(later, wide_w[at, :], 0.0)
            wide_w[at, :] = value[:, half * LANES : (half + 1) * LANES] + before

    def put_vector(index, value):
        for half in range(2):
            row = slice(2 * index + half, 2 * index + half + 1)
            before = jnp.where(later, gv_ref[row, :], 0.0)
            gv_ref[row, :] = value[:, half * LANES : (half + 1) * LANES] + before

    def column_sum(value):
        return jnp.sum(value.astype(f32), axis=0, keepdims=True)

    put_vector(0, jnp.zeros((1, ROWS), f32))
    put_vector(1, jnp.zeros((1, ROWS), f32))
    g_vec = jnp.zeros((3 * atoms, feat_width), f32)
    for part_at in range(3):
        put_grad(O_AT, 6, part_at, ROWS, dot_tn(agg_low, go[part_at]))
        put_vector(7 + part_at, column_sum(go[part_at]))
        gp = proj[part_at].astype(bf16)
        put_grad(VEC_AT, 6, part_at, ROWS, dot_tn(vec_rows, gp))
        g_vec += dot_nt(gp, wb[W_VEC + part_at])

    g_query = agg[:, block_cols(4)].astype(bf16)
    put_grad(Q_AT, 2, 0, ROWS, dot_tn(norm_table[0:atoms, :], g_query))
    put_vector(2, column_sum(g_query))
    g_norm = dot_nt(g_query, wb[W_Q])

    sums = [jnp.zeros((ROWS, ROWS), f32) for column in range(4)]
    biases = [jnp.zeros((1, ROWS), f32) for column in range(4)]
    for b in range(buckets):
        rows = slice(b * ROWS, (b + 1) * ROWS)
        g_table = jnp.zeros((ROWS, ROWS), f32)
        for column in range(4):
            low = acc[b, :, block_cols(column)].astype(bf16)
            sums[column] += dot_tn(norm_table[rows, :], low)
            biases[column] += column_sum(low)
            g_table += dot_nt(low, wb[W_K + column])
        for half in range(2):
            domain = 2 * b + half
            if domain >= domains:
                continue
            here = slice(half * atoms, (half + 1) * atoms)
            if domain == 0:
                gown_ref[0, 0] = g_table[here, :] + g_norm
            else:
                back_refs[domain - 1][0, 0] = g_table[here, :].astype(bf16)
            for axis in range(3):
                block = acc[b, here, block_cols(4 + axis)]
                if domain == 0:
                    gown_ref[0, 1 + axis] = block + g_vec[parts[axis], :]
                else:
                    back_refs[domain - 1][0, 1 + axis] = block.astype(bf16)
    for column in range(4):
        if column == 0:
            put_grad(K_AT, 2, 0, ROWS, sums[column])
        else:
            put_grad(V_AT, 6, column - 1, ROWS, sums[column])
        put_vector(3 + column, biases[column])

    @pl.when(micro == pl.num_programs(0) - 1)
    def _():
        for column in range(4):
            block = gwd[0:NR, block_cols(column)] * 0.5
            first, stride, at = (DK_AT, 2, 0) if column == 0 else (DV_AT, 6, column - 1)
            for half in range(2):
                cols = slice(half * LANES, (half + 1) * LANES)
                wide_w[pl.ds(first + 2 * at + half, NR, stride=stride), :] = block[:, cols]
                row = 2 * (10 + column) + half
                bias = gwd[NR : NR + 1, column * ROWS + half * LANES :][:, :LANES]
                gv_ref[row : row + 1, :] = bias * 0.5
        for cell in range(cells):
            for part_at in range(parts_w):
                start = (cell * parts_w + part_at) * quarter
                gm_ref[part_at, cell] = wide_w[start : start + quarter, :].astype(bf16)


def core_mate(depth_at):
    return depth_at + 1 - 2 * (depth_at % 2)


def chip_mate(depth_at):
    return (depth_at + 2) % 4


def greet(cells, depth):
    barrier = pltpu.get_barrier_semaphore()
    cell_at, depth_at = lax.axis_index("cells"), lax.axis_index("depth")
    for by in range(1, cells):
        pl.semaphore_signal(barrier, inc=1, device_id={"cells": (cell_at + by) % cells})
    for by in range(1, depth):
        pl.semaphore_signal(barrier, inc=1, device_id={"depth": (depth_at + by) % depth})
    pl.semaphore_wait(barrier, cells + depth - 2)


def remote(source, target, send, receive, device):
    return pltpu.make_async_remote_copy(
        src_ref=source, dst_ref=target, send_sem=send, recv_sem=receive, device_id=device
    )


def fetch_kernel(cells, depth, micros, sources, faces, *refs):
    own_ref, lists_ref, w_ref, v_ref = refs[:4]
    halo_refs = refs[4 : 4 + len(sources)]
    got_lists, got_w, got_v = refs[4 + len(sources) : 7 + len(sources)]
    (
        halo_send,
        halo_recv,
        list_send,
        list_recv,
        v_send,
        v_recv,
        w_send,
        w_recv,
    ) = refs[7 + len(sources) :]
    cell_at, depth_at = lax.axis_index("cells"), lax.axis_index("depth")
    sizes = {"cells": cells, "depth": depth}
    places = {"cells": cell_at, "depth": depth_at}
    got_w[cell_at] = w_ref[...]
    got_v[cell_at] = v_ref[...]
    greet(cells, depth)

    def ahead(axis, by):
        return {axis: (places[axis] + by) % sizes[axis]}

    started = []

    def start(*args):
        copy = remote(*args)
        copy.start()
        started.append(copy)
        return copy

    half = cells // 2
    base, place = cell_at // half * half, cell_at % half

    def beside(by):
        return base + (place + by) % half

    def from_beside(by):
        return base + (place + half - by) % half

    opposite = (cell_at + half) % cells

    def send_weight(source_cell, order, target):
        piece = got_w.at[source_cell, depth_at]
        return start(piece, piece, w_send.at[0, order], w_recv.at[0, order], {"cells": target})

    origins = {by: from_beside(by) for by in range(1, half)}
    origins[half] = opposite
    for by in range(1, half):
        origins[half + by] = (from_beside(by) + half) % cells
    first = {half: send_weight(cell_at, half, opposite)}
    for by in range(1, half):
        first[by] = send_weight(cell_at, by, beside(by))
    lists = [
        start(
            lists_ref.at[face],
            got_lists.at[face],
            list_send.at[face],
            list_recv.at[face],
            ahead(axis, by),
        )
        for face, (axis, by) in enumerate(faces)
    ]
    vectors = [
        start(v_ref, got_v.at[cell_at], v_send.at[by], v_recv.at[by], ahead("cells", by))
        for by in range(1, cells)
    ]
    halos = []

    def send_halos(micro):
        for index, (axis, by) in enumerate(sources):
            halos.append(
                start(
                    own_ref.at[micro],
                    halo_refs[index].at[micro],
                    halo_send.at[micro, index],
                    halo_recv.at[micro, index],
                    ahead(axis, by),
                )
            )

    send_halos(0)
    order = [half, *range(1, half), *range(half + 1, cells)]
    first[half].wait_recv()
    for by in range(1, half):
        first[half + by] = send_weight(opposite, half + by, beside(by))
    mate, other = core_mate(depth_at), chip_mate(depth_at)
    across = []
    last = []
    for by in order:
        if by != half:
            first[by].wait_recv()
        piece = got_w.at[origins[by], depth_at]
        across.append(
            start(piece, piece, w_send.at[1, by], w_recv.at[1, by], {"depth": other})
        )
        last.append(start(piece, piece, w_send.at[2, by], w_recv.at[2, by], {"depth": mate}))
        if by == order[min(half - 1, cells - 2)]:
            for micro in range(1, micros):
                send_halos(micro)
    for at, by in enumerate(order):
        across[at].wait_recv()
        piece = got_w.at[origins[by], other]
        last.append(start(piece, piece, w_send.at[3, by], w_recv.at[3, by], {"depth": mate}))
    for copy in lists + vectors + last + halos:
        copy.wait_recv()
    for copy in started:
        copy.wait_send()


def close_kernel(cells, depth, micros, sources, *refs):
    count = len(sources)
    x_far, cotx_far, cotv_far, gain_ref, gvec_in, part_ref, gown_far = refs[:7]
    back_refs = refs[7 : 7 + count]
    gx_ref, gvec_ref, summ_ref, sumv_ref = refs[7 + count : 11 + count]
    (
        came,
        one_in,
        two_out,
        two_in,
        three_out,
        three_in,
        four_out,
        four_in,
        held,
        quad,
        octo,
        x_ref,
        cotx_ref,
        cotv_ref,
        gown_ref,
        load_sem,
        halo_send,
        halo_recv,
        m_send,
        m_recv,
        c_send,
        c_recv,
        d_send,
        d_recv,
        e_send,
        e_recv,
        f_send,
        f_recv,
    ) = refs[11 + count :]
    cell_at, depth_at = lax.axis_index("cells"), lax.axis_index("depth")
    sizes = {"cells": cells, "depth": depth}
    places = {"cells": cell_at, "depth": depth_at}
    greet(cells, depth)

    def ahead(axis, by):
        return {axis: (places[axis] + by) % sizes[axis]}

    started = []

    def start(*args):
        copy = remote(*args)
        copy.start()
        started.append(copy)
        return copy

    def go_home(micro, piece):
        parts = pl.ds(0, 1) if piece == 0 else pl.ds(1, 3)
        return [
            start(
                back_refs[index].at[micro, parts],
                came.at[micro, index, parts],
                halo_send.at[micro, index, piece],
                halo_recv.at[micro, index, piece],
                ahead(axis, -by),
            )
            for index, (axis, by) in enumerate(sources)
        ]

    mate, other = core_mate(depth_at), chip_mate(depth_at)
    mate_other = chip_mate(mate)
    one_far = start(
        part_ref.at[mate_other], one_in.at[1], m_send.at[0], m_recv.at[0], {"depth": mate}
    )
    one_near = start(part_ref.at[mate], one_in.at[0], m_send.at[1], m_recv.at[1], {"depth": mate})
    scalars = [go_home(micro, 0) for micro in range(micros)]
    vectors = [go_home(micro, 1) for micro in range(micros)]
    loads = [
        pltpu.make_async_copy(far, near, load_sem.at[at])
        for at, (far, near) in enumerate(
            ((gown_far, gown_ref), (x_far, x_ref), (cotx_far, cotx_ref), (cotv_far, cotv_ref))
        )
    ]
    for load in loads:
        load.start()
    one_far.wait_recv()
    two_out[...] = (part_ref[other].astype(f32) + one_in[1].astype(f32)).astype(bf16)
    two = start(two_out, two_in, m_send.at[2], m_recv.at[2], {"depth": other})
    one_near.wait_recv()
    two.wait_recv()
    for cell in range(cells):
        total = (
            part_ref[depth_at, cell].astype(f32)
            + one_in[0, cell].astype(f32)
            + two_in[cell].astype(f32)
        )
        three_out[cell] = total.astype(bf16)
    half = cells // 2
    base, place = cell_at // half * half, cell_at % half
    opposite = (cell_at + half) % cells
    three = []
    for by in range(1, half):
        there = base + (place + by) % half
        for side in range(2):
            order = side * half + by
            three.append(
                start(
                    three_out.at[(there + side * half) % cells],
                    three_in.at[order],
                    c_send.at[order],
                    c_recv.at[order],
                    {"cells": there},
                )
            )

    def back_sum(micro, part):
        total = gown_ref[micro, part]
        for index in range(count):
            total = total + came[micro, index, part].astype(f32)
        return total

    gain = jnp.concatenate([gain_ref[side : side + 1, :].astype(f32) for side in range(2)], axis=1)
    norm_grads = [jnp.zeros((1, gain.shape[1]), f32) for part in range(2)]
    for load in loads:
        load.wait()
    for micro in range(micros):
        for copy in scalars[micro]:
            copy.wait_recv()
        total = back_sum(micro, 0)
        hat, spread = normalise(x_ref[micro])
        norm_grads[0] += jnp.sum(total * hat, axis=0, keepdims=True)
        norm_grads[1] += jnp.sum(total, axis=0, keepdims=True)
        g_hat = total * gain
        g_x = spread * (g_hat - lane_mean(g_hat) - hat * lane_mean(g_hat * hat))
        gx_ref[micro] = cotx_ref[micro] + g_x
    held[...] = gvec_in[...]
    for part in range(2):
        for side in range(2):
            row = 2 * part + side
            held[row : row + 1, :] = norm_grads[part][:, side * LANES : (side + 1) * LANES]
    quad[depth_at] = held[...]
    four = [
        start(held, quad.at[depth_at], d_send.at[by], d_recv.at[by], ahead("depth", by))
        for by in range(1, depth)
    ]

    for copy in three:
        copy.wait_recv()
    sums = [three_out[cell_at].astype(f32), three_out[opposite].astype(f32)]
    for side in range(2):
        for by in range(1, half):
            sums[side] = sums[side] + three_in[side * half + by].astype(f32)
    four_out[...] = sums[1].astype(bf16)
    crossing = start(four_out, four_in, c_send.at[0], c_recv.at[0], {"cells": opposite})
    for copy in four:
        copy.wait_recv()
    total = quad[0]
    for at in range(1, depth):
        total = total + quad[at]
    octo[cell_at] = total
    eight = [
        start(
            octo.at[cell_at],
            octo.at[cell_at],
            f_send.at[by],
            f_recv.at[by],
            ahead("cells", by),
        )
        for by in range(1, cells)
    ]
    crossing.wait_recv()
    summ_ref[depth_at] = sums[0] + four_in[...].astype(f32)
    share = [
        start(
            summ_ref.at[depth_at],
            summ_ref.at[depth_at],
            e_send.at[by],
            e_recv.at[by],
            ahead("depth", by),
        )
        for by in range(1, depth)
    ]
    for micro in range(micros):
        for copy in vectors[micro]:
            copy.wait_recv()
        for axis in range(3):
            gvec_ref[micro, axis] = cotv_ref[micro, axis] + back_sum(micro, 1 + axis)
    for copy in eight:
        copy.wait_recv()
    total = octo[0]
    for cell in range(1, cells):
        total = total + octo[cell]
    sumv_ref[...] = total
    for copy in share:
        copy.wait_recv()
    for copy in started:
        copy.wait_send()


def adam_update(weight, grad, first, second):
    first_new = beta_one * first + (1.0 - beta_one) * grad
    second_new = beta_two * second + (1.0 - beta_two) * grad * grad
    first_hat = first_new / (1.0 - beta_one**STEP)
    second_hat = second_new / (1.0 - beta_two**STEP)
    weight_new = weight - learn_rate * (
        first_hat / (jnp.sqrt(second_hat) + adam_eps) + decay_rate * weight
    )
    return (weight_new, first_new, second_new)


def update_kernel(*refs):
    ins, outs = refs[:6], refs[6:]
    outs[0][...] = ins[0][...]
    outs[1][...] = ins[1][...]
    grad = ins[2][...]
    outs[2][...] = grad
    updated = adam_update(ins[3][...], grad, ins[4][...], ins[5][...])
    for out, value in zip(outs[3:], updated):
        out[...] = value


def shards(
    x_in,
    vec_in,
    cot_x,
    cot_vec,
    mats,
    vecs,
    mats_first,
    mats_second,
    vecs_first,
    vecs_second,
    atom_count,
    neighbours,
    edge_mask,
    edge_vec,
    send_list,
):
    micros, atoms, width = x_in.shape
    slots = neighbours.shape[1]
    halo = send_list.shape[-1]
    per_face = halo // LANES
    cells, depth = lax.axis_size("cells"), lax.axis_size("depth")
    faces = [("cells", 1), ("cells", -1), ("cells", FOLD), ("cells", -FOLD), ("depth", 1), ("depth", -1)]
    sizes = {"cells": cells, "depth": depth}
    sources = []
    face_source = []
    for axis, by in faces:
        key = (axis, by % sizes[axis])
        if key not in sources:
            sources.append(key)
        face_source.append(sources.index(key))
    domains = 1 + len(sources)
    buckets = (domains * atoms + ROWS - 1) // ROWS
    block_of = [1 + face_source[row // per_face] for row in range(6 * per_face)]

    whole = pl.BlockSpec(memory_space=pltpu.VMEM)
    scalars = pl.BlockSpec(memory_space=pltpu.SMEM)

    any_space = pl.BlockSpec(memory_space=pl.ANY)
    count = len(sources)
    quarter = mats.shape[0] // LANES // depth
    list_shape = jax.ShapeDtypeStruct((6, micros * per_face, LANES), i32)

    own, w_low, my_lists = pl.pallas_call(
        norm_kernel,
        out_shape=(
            jax.ShapeDtypeStruct((micros, 4, atoms, width), bf16),
            jax.ShapeDtypeStruct((depth, quarter, LANES), bf16),
            list_shape,
        ),
        in_specs=[whole] * 4,
        out_specs=[whole] * 3,
        name="norm",
    )(x_in, vec_in, mats.reshape(-1, LANES), send_list)

    dma = pltpu.SemaphoreType.DMA
    fetched = pl.pallas_call(
        partial(fetch_kernel, cells, depth, micros, sources, faces),
        out_shape=tuple(
            [jax.ShapeDtypeStruct((micros, 4, atoms, width), bf16)] * count
            + [
                list_shape,
                jax.ShapeDtypeStruct((cells, depth, quarter, LANES), bf16),
                jax.ShapeDtypeStruct((cells, 1, vecs.shape[0]), f32),
            ]
        ),
        in_specs=[any_space] + [whole] * 3,
        out_specs=[any_space] * count + [whole] * 3,
        scratch_shapes=[
            dma((micros, count)),
            dma((micros, count)),
            dma((6,)),
            dma((6,)),
            dma((cells,)),
            dma((cells,)),
            dma((4, cells)),
            dma((4, cells)),
        ],
        compiler_params=pltpu.CompilerParams(
            collective_id=0, has_side_effects=True, vmem_limit_bytes=VMEM_LIMIT
        ),
        name="fetch",
    )(own, my_lists, w_low, vecs.reshape(1, -1))
    halos = fetched[:count]
    got_lists, w_all, v_all = fetched[count:]
    v_all = v_all.astype(bf16).reshape(-1, LANES)
    w_rows, v_rows = cells * depth * quarter, v_all.shape[0]

    limit = slots * atoms + buckets * (slots // BLOCK_SLOTS) * 8 + buckets * 2 * UNIT
    capacity = (limit + UNIT - 1) // UNIT * UNIT + 4 * UNIT

    def by_micro(array):
        zeros = (0,) * (len(array.shape) - 1)
        return pl.BlockSpec((1,) + tuple(array.shape[1:]), lambda i: (i,) + zeros)

    per_micro = [neighbours, edge_mask, edge_vec, x_in, vec_in, cot_x, cot_vec, *halos]
    out_blocks = [
        jax.ShapeDtypeStruct((micros, atoms, width), f32),
        jax.ShapeDtypeStruct((micros, 3, atoms, width), f32),
        jax.ShapeDtypeStruct((micros, 4, atoms, width), f32),
    ] + [jax.ShapeDtypeStruct((micros, 4, atoms, width), bf16)] * count
    results = pl.pallas_call(
        partial(edge_kernel, domains, buckets, block_of),
        out_shape=tuple(
            out_blocks
            + [
                jax.ShapeDtypeStruct((depth, cells, quarter, LANES), bf16),
                jax.ShapeDtypeStruct((v_rows, LANES), f32),
            ]
        ),
        grid=(micros,),
        in_specs=[scalars, whole] + [by_micro(array) for array in per_micro] + [whole] * 2,
        out_specs=[by_micro(block) for block in out_blocks] + [whole] * 2,
        scratch_shapes=[
            pltpu.VMEM((slots, LANES, LANES), bf16),
            pltpu.VMEM((slots, atoms), i32),
            pltpu.VMEM((slots // BLOCK_SLOTS, LANES), i32),
            pltpu.SMEM((slots // BLOCK_SLOTS, LANES), i32),
            pltpu.VMEM((capacity, LANES), f32),
            pltpu.SemaphoreType.DMA(()),
            pltpu.VMEM((w_rows, LANES), f32),
            pltpu.VMEM((11, ROWS, ROWS), bf16),
            pltpu.VMEM((LANES, 4 * ROWS), bf16),
            pltpu.VMEM((buckets * ROWS, ROWS), bf16),
            pltpu.VMEM((buckets, ROWS, 7 * ROWS), bf16),
            pltpu.VMEM((buckets, ROWS, 7 * ROWS), f32),
            pltpu.VMEM((atoms, 5 * ROWS), bf16),
            pltpu.VMEM((3, 3 * atoms, ROWS), f32),
            pltpu.VMEM((3, atoms, ROWS), bf16),
            pltpu.VMEM((atoms, 5 * ROWS), f32),
            pltpu.VMEM((FEATS, 4 * ROWS), f32),
            pltpu.VMEM((ROWS, ROWS), bf16),
        ]
        + [
            scratch
            for scratch in (
                pltpu.VMEM((UNIT, ROWS), bf16),
                pltpu.VMEM((UNIT, LANES), bf16),
                pltpu.VMEM((UNIT, WORK * ROWS), f32),
                pltpu.VMEM((UNIT, LANES), f32),
                pltpu.VMEM((3, UNIT, LANES), f32),
                pltpu.VMEM((2, 2 * UNIT, LANES), bf16),
                pltpu.VMEM((14, UNIT, LANES), bf16),
                pltpu.VMEM((8, UNIT, LANES), bf16),
                pltpu.VMEM((12, UNIT, LANES), bf16),
            )
            for side in range(2)
        ],
        compiler_params=pltpu.CompilerParams(vmem_limit_bytes=VMEM_LIMIT),
        name="edges",
    )(atom_count, got_lists, *per_micro, w_all, v_all)
    out_x, out_vec, g_own = results[:3]
    backs = results[3 : 3 + count]
    part_m, part_v = results[3 + count :]
    grad_x, grad_vec, sum_mats, sum_vecs = pl.pallas_call(
        partial(close_kernel, cells, depth, micros, sources),
        out_shape=(
            jax.ShapeDtypeStruct(x_in.shape, f32),
            jax.ShapeDtypeStruct(vec_in.shape, f32),
            jax.ShapeDtypeStruct((depth, quarter, LANES), f32),
            jax.ShapeDtypeStruct((v_rows, LANES), f32),
        ),
        in_specs=[any_space] * 3 + [whole] * 3 + [any_space] * (1 + count),
        out_specs=[whole] * 4,
        scratch_shapes=[
            pltpu.VMEM((micros, count, 4, atoms, width), bf16),
            pltpu.VMEM((2, cells, quarter, LANES), bf16),
            pltpu.VMEM((cells, quarter, LANES), bf16),
            pltpu.VMEM((cells, quarter, LANES), bf16),
            pltpu.VMEM((cells, quarter, LANES), bf16),
            pltpu.VMEM((cells, quarter, LANES), bf16),
            pltpu.VMEM((quarter, LANES), bf16),
            pltpu.VMEM((quarter, LANES), bf16),
            pltpu.VMEM((v_rows, LANES), f32),
            pltpu.VMEM((depth, v_rows, LANES), f32),
            pltpu.VMEM((cells, v_rows, LANES), f32),
            pltpu.VMEM(x_in.shape, f32),
            pltpu.VMEM(cot_x.shape, f32),
            pltpu.VMEM(cot_vec.shape, f32),
            pltpu.VMEM(g_own.shape, f32),
            dma((4,)),
            dma((micros, count, 2)),
            dma((micros, count, 2)),
            dma((3,)),
            dma((3,)),
            dma((cells,)),
            dma((cells,)),
            dma((depth,)),
            dma((depth,)),
            dma((depth,)),
            dma((depth,)),
            dma((cells,)),
            dma((cells,)),
        ],
        compiler_params=pltpu.CompilerParams(
            collective_id=1, has_side_effects=True, vmem_limit_bytes=VMEM_LIMIT
        ),
        name="close",
    )(
        x_in,
        cot_x,
        cot_vec,
        v_all,
        part_v,
        part_m,
        g_own,
        *backs,
    )
    flat = [
        grad_x.reshape(-1, width),
        grad_vec.reshape(-1, width),
        *[array.reshape(-1, LANES) for array in (sum_mats, mats, mats_first, mats_second)],
    ]
    steps = 4 if all(array.shape[0] % 32 == 0 for array in flat) else 1

    def by_step(array):
        return pl.BlockSpec((array.shape[0] // steps, array.shape[1]), lambda i: (i, 0))

    outs = flat[:3] + [flat[3]] * 3
    grad_x, grad_vec, *matrices = pl.pallas_call(
        update_kernel,
        out_shape=tuple(jax.ShapeDtypeStruct(array.shape, f32) for array in outs),
        grid=(steps,),
        in_specs=[by_step(array) for array in flat],
        out_specs=[by_step(array) for array in outs],
        name="update",
    )(*flat)
    grad_x = grad_x.reshape(x_in.shape)
    grad_vec = grad_vec.reshape(vec_in.shape)
    sum_mats, new_mats, mats_one, mats_two = [matrix.reshape(-1) for matrix in matrices]
    sum_vecs = lax.dynamic_slice_in_dim(
        sum_vecs.reshape(-1), lax.axis_index("cells") * vecs.shape[0], vecs.shape[0]
    )
    new_vecs, vecs_one, vecs_two = adam_update(vecs, sum_vecs, vecs_first, vecs_second)
    return (
        out_x,
        out_vec,
        grad_x,
        grad_vec,
        sum_mats,
        sum_vecs,
        new_mats,
        new_vecs,
        mats_one,
        mats_two,
        vecs_one,
        vecs_two,
    )


def solution(mesh):
    by_atom = ("cells", "depth")
    shard = P("cells")
    in_specs = (
        P(None, by_atom, None),
        P(None, None, by_atom, None),
        P(None, by_atom, None),
        P(None, None, by_atom, None),
        shard,
        shard,
        shard,
        shard,
        shard,
        shard,
        P(None, by_atom),
        P(None, None, by_atom),
        P(None, None, by_atom),
        P(None, None, None, by_atom),
        P(None, by_atom, None),
    )
    out_specs = (
        P(None, by_atom, None),
        P(None, None, by_atom, None),
        P(None, by_atom, None),
        P(None, None, by_atom, None),
    ) + (shard,) * 8
    return jax.shard_map(shards, mesh=mesh, in_specs=in_specs, out_specs=out_specs, check_vma=False)
```
